32 devices in a mesh: dp: 8 (over y, x, core), expert: 4 (over z).
Axes of the slice: x: 2, y: 2, z: 4, core: 2. Of those that a mesh axis runs over, the one named last changes fastest.
Arguments:
- hidden_in: bfloat16 [2, 32, 256, 768], P(None, ('dp', 'expert')), may hold values from -6 to 6
- prev_logits: float32 [2, 32, 256, 12], P(None, ('dp', 'expert')), may hold values from -3 to 3
- routes: int32 [2, 32, 256, 2], P(None, ('dp', 'expert')), may hold values from 0 to 11, all different within a row; in each aligned block of 256 rows (0 to 255, 256 to 511, ..., all dimensions but the last counted through in order) at most 80 rows name the same one
- adapter_ids: int32 [2, 32], P(None, ('dp', 'expert')), may hold values from 0 to 7, as said below
- image_spans: int32 [2, 32, 2, 2], P(None, ('dp', 'expert')), may hold values from 0 to 256, as said below
- cotangent: bfloat16 [2, 32, 256, 768], P(None, ('dp', 'expert')), may hold values from -6 to 6
- gain_attn: float32 [768], replicated, may hold values from 0.1 to 1.9
- gain_moe: float32 [768], replicated, may hold values from 0.1 to 1.9
- router_weight: float32 [768, 12], replicated, may hold values from -0.109375 to 0.109375
- const_gate: float32 [768, 2], replicated, may hold values from -0.21875 to 0.21875
- const_value: float32 [2, 768], replicated, may hold values from -6 to 6
- w_qkv: bfloat16 [768, 2304], P('dp'), may hold values from -0.21875 to 0.21875
- w_out: bfloat16 [768, 768], P('dp'), may hold values from -0.875 to 0.875
- a_qkv: bfloat16 [768, 384], P('dp'), may hold values from -0.21875 to 0.21875
- b_qkv: bfloat16 [128, 2304], P('dp'), may hold values from -1.5 to 1.5
- a_out: bfloat16 [768, 128], P('dp'), may hold values from -0.875 to 0.875
- b_out: bfloat16 [128, 768], P('dp'), may hold values from -1.5 to 1.5
- w_gate_up: bfloat16 [8, 768, 4096], P('expert', 'dp'), may hold values from -0.21875 to 0.21875
- w_down: bfloat16 [8, 2048, 768], P('expert', 'dp'), may hold values from -0.125 to 0.125
- a_gate_up: bfloat16 [8, 768, 256], P('expert', 'dp'), may hold values from -0.21875 to 0.21875
- b_gate_up: bfloat16 [8, 128, 4096], P('expert', 'dp'), may hold values from -1.5 to 1.5
- a_down: bfloat16 [8, 2048, 128], P('expert', 'dp'), may hold values from -0.125 to 0.125
- b_down: bfloat16 [8, 128, 768], P('expert', 'dp'), may hold values from -1.5 to 1.5
Outputs:
- block_out: bfloat16 [2, 32, 256, 768], P(None, ('dp', 'expert'))
- grad_input: float32 [2, 32, 256, 768], P(None, ('dp', 'expert'))
- grad_a_qkv: float32 [768, 384], P('dp')
- grad_b_qkv: float32 [128, 2304], P('dp')
- grad_a_out: float32 [768, 128], P('dp')
- grad_b_out: float32 [128, 768], P('dp')
- grad_a_gate_up: float32 [8, 768, 256], P('expert', 'dp')
- grad_b_gate_up: float32 [8, 128, 4096], P('expert', 'dp')
- grad_a_down: float32 [8, 2048, 128], P('expert', 'dp')
- grad_b_down: float32 [8, 128, 768], P('expert', 'dp')
The draws below stay inside these ranges and needn't reach their ends.
Inputs may be any that keep to these rules, and one draw needn't show every extreme that they name: `routes`: each token names 2 different experts; in each sequence no expert is named by more than 80 tokens, a bound that some block reaches. `adapter_ids`: each of the 8 adapters is used by equally many sequences. `image_spans`: span j of a sequence lies within tokens j * 128 to (j + 1) * 128; start < end, and a span has at most 64 tokens.
All inputs are finite; a program needn't handle non-finite values.
Results may differ from the reference program's by a relative error of at most 0.018.
Values may be sent and summed in bfloat16 or wider, within the bound.
No kernel may reach another device: no remote copies, remote signals or barrier semaphores. Data moves between devices by JAX's collectives and lax.ppermute only.
A program may use at most 136 MiB of HBM per device.

```python
import math
import jax
import jax.numpy as jnp
import numpy as np
from jax import lax

D = 768
HEADS = 12
HEAD = 64
FF = 2048
FFN_EXPERTS = 8
EXPERTS = 12
TOPK = 2
RANK = 16
ADAPTERS = 8
RANKS_ALL = 128
SEQ = 256
MICRO = 2
SPANS = 2
IMG = 64
CAP = 80
NSEQ = 32


def draw_adapter_ids(key, part):
    order = jax.random.permutation(key, MICRO * NSEQ)
    return (order % ADAPTERS).reshape(MICRO, NSEQ).astype(jnp.int32)


def draw_image_spans(key, part):
    half_len = SEQ // SPANS
    key_len, key_off = jax.random.split(jax.random.fold_in(key, 17))
    lengths = jax.random.randint(key_len, (MICRO, NSEQ, SPANS), IMG // 4, IMG + 1)
    lengths = lengths.at[:, 0, :].set(IMG)
    room = half_len - lengths + 1
    offsets = jax.random.randint(key_off, (MICRO, NSEQ, SPANS), 0, 1 << 20) % room
    offsets = offsets.at[0, 0, 0].set(0)
    offsets = offsets.at[0, 0, SPANS - 1].set(half_len - IMG)
    starts = jnp.arange(SPANS, dtype=jnp.int32)[None, None, :] * half_len + offsets
    return jnp.stack([starts, starts + lengths], axis=-1).astype(jnp.int32)


def block_scale(stream_key, extent, pieces, smallest, largest):
    factor_of, own = 1.0, jax.random.fold_in(stream_key, 6)
    for dim, parts in pieces:
        steps = jnp.exp(jax.random.uniform(jax.random.fold_in(own, dim), (parts,), jnp.float32, smallest / len(pieces), largest / len(pieces)))
        factor_of = factor_of * jnp.repeat(steps, extent[dim] // parts).reshape([-1 if axis == dim else 1 for axis in range(len(extent))])
    return factor_of


def deal_out(key, own, number, rows, count, top, most, lean):
    ranking = jax.random.permutation(key, count)
    packed, common = portions_of(count, rows * top, most, lean, True), portions_of(count, rows * top, most, lean, False)
    places = jnp.arange(count)

    def named(sizes, offset_by):
        used = int((sizes > 0).sum())
        fixed = max(1, used // 4)
        moved = fixed + (places - fixed + offset_by * (used - fixed)) % max(1, count - fixed)
        return jnp.zeros((count,), jnp.int32).at[ranking[jnp.where(places < fixed, places, moved)]].set(jnp.asarray(sizes, jnp.int32))

    sizes = jnp.where(number % 4 == 0, named(packed, number // 4), named(common, number - number // 4 - 1))
    mixed = jax.random.permutation(jax.random.fold_in(own, 3), count)
    source_of, receiver = mixed[0:count // 2 * 2:2], mixed[1:count // 2 * 2:2]
    room = jnp.minimum(sizes[source_of] - 1, most - sizes[receiver]) // 2
    room = jnp.where((source_of == ranking[0]) | (receiver == ranking[0]) | (sizes[receiver] == 0), 0, jnp.maximum(room, 0))
    moved = jax.random.randint(jax.random.fold_in(own, 4), (count // 2,), 0, 1 << 20) % (room + 1)
    sizes = sizes.at[source_of].add(-moved).at[receiver].add(moved)
    labels = jnp.searchsorted(jnp.cumsum(sizes), jnp.arange(rows * top), side="right").astype(jnp.int32)
    grid = labels.reshape(top, rows).T
    grid = grid[jax.random.permutation(jax.random.fold_in(own, 1), rows)]
    offset_by = jax.random.randint(jax.random.fold_in(own, 2), (rows, 1), 0, top)
    return jnp.take_along_axis(grid, (jnp.arange(top)[None, :] + offset_by) % top, axis=1)


def portions_of(count, total, most, lean, full):
    weights = [(1 << 20) // math.isqrt(rank ** lean) + 1 for rank in range(1, count + 1)]
    largest = most if full else min(most, max(-(-total // count), total * weights[0] // sum(weights)))
    least = 1 if total - largest >= count - 1 else 0
    counts, spare = [largest] + [least] * (count - 1), total - largest - least * (count - 1)
    while spare > 0:
        free = [i for i in range(1, count) if counts[i] < largest] or [i for i in range(1, count) if counts[i] < most]
        whole, budget = sum([weights[i] for i in free]), spare
        for i in free:
            addition = min(most - counts[i], max(1, budget * weights[i] // whole), spare)
            counts[i] = counts[i] + addition
            spare = spare - addition
    return np.array(counts)


def normal_values(rng, dims, deviation, limit, cuts=(), kind=jnp.bfloat16):
    factor_of = block_scale(rng, dims, cuts, -0.22, 0.18) if cuts else 1.0
    values = jax.random.normal(rng, dims, jnp.float32) * deviation * factor_of
    return jnp.minimum(jnp.maximum(values, -limit), limit).astype(kind)


def setup_inputs(seed: int = 0) -> dict:
    arg_keys = jax.random.split(jax.random.key(seed), 24)
    hidden_in = normal_values(arg_keys[0], (MICRO, NSEQ, SEQ, D), 1.0, 6.0, ((1, 32),))
    prev_logits = normal_values(arg_keys[1], (MICRO, NSEQ, SEQ, EXPERTS), 0.5, 3.0, ((1, 32),), jnp.float32)
    routes_keys = jax.random.split(jax.random.fold_in(arg_keys[2], 1), MICRO * NSEQ * SEQ // SEQ)
    routes_turns = jax.random.permutation(jax.random.fold_in(arg_keys[2], 3), MICRO * NSEQ * SEQ // SEQ)
    routes = jax.vmap(lambda own, number: deal_out(jax.random.fold_in(arg_keys[2], 2), own, number, SEQ, EXPERTS, TOPK, CAP, 1))(routes_keys, routes_turns).reshape((MICRO, NSEQ, SEQ, TOPK))
    adapter_ids = draw_adapter_ids(jax.random.fold_in(arg_keys[23], 71), 0)
    image_spans = draw_image_spans(jax.random.fold_in(arg_keys[23], 71), 0)
    cotangent = normal_values(arg_keys[5], (MICRO, NSEQ, SEQ, D), 1.0, 6.0, ((1, 32),))
    gain_attn = jnp.clip(1.0 + 0.18 * jax.random.normal(arg_keys[6], (D,), jnp.float32), 0.1, 1.9)
    gain_moe = jnp.clip(1.0 + 0.18 * jax.random.normal(arg_keys[7], (D,), jnp.float32), 0.1, 1.9)
    router_weight = normal_values(arg_keys[8], (D, EXPERTS), (4 * D) ** -0.5, 0.109375, (), jnp.float32)
    const_gate = normal_values(arg_keys[9], (D, 2), D ** -0.5, 0.21875, (), jnp.float32)
    const_value = normal_values(arg_keys[10], (2, D), 1.0, 6.0, (), jnp.float32)
    w_qkv = normal_values(arg_keys[11], (D, 3 * D), D ** -0.5, 0.21875, ((0, 8),))
    w_out = normal_values(arg_keys[12], (D, D), (D // 16) ** -0.5, 0.875, ((0, 8),))
    a_qkv = normal_values(arg_keys[13], (D, 3 * RANKS_ALL), D ** -0.5, 0.21875, ((0, 8),))
    b_qkv = normal_values(arg_keys[14], (RANKS_ALL, 3 * D), RANK ** -0.5, 1.5, ((0, 8),))
    a_out = normal_values(arg_keys[15], (D, RANKS_ALL), (D // 16) ** -0.5, 0.875, ((0, 8),))
    b_out = normal_values(arg_keys[16], (RANKS_ALL, D), RANK ** -0.5, 1.5, ((0, 8),))
    w_gate_up = normal_values(arg_keys[17], (FFN_EXPERTS, D, 2 * FF), D ** -0.5, 0.21875, ((0, 4), (1, 8)))
    w_down = normal_values(arg_keys[18], (FFN_EXPERTS, FF, D), FF ** -0.5, 0.125, ((0, 4), (1, 8)))
    a_gate_up = normal_values(arg_keys[19], (FFN_EXPERTS, D, 2 * RANKS_ALL), D ** -0.5, 0.21875, ((0, 4), (1, 8)))
    b_gate_up = normal_values(arg_keys[20], (FFN_EXPERTS, RANKS_ALL, 2 * FF), RANK ** -0.5, 1.5, ((0, 4), (1, 8)))
    a_down = normal_values(arg_keys[21], (FFN_EXPERTS, FF, RANKS_ALL), FF ** -0.5, 0.125, ((0, 4), (1, 8)))
    b_down = normal_values(arg_keys[22], (FFN_EXPERTS, RANKS_ALL, D), RANK ** -0.5, 1.5, ((0, 4), (1, 8)))
    return {"hidden_in": hidden_in, "prev_logits": prev_logits, "routes": routes, "adapter_ids": adapter_ids, "image_spans": image_spans, "cotangent": cotangent, "gain_attn": gain_attn, "gain_moe": gain_moe, "router_weight": router_weight, "const_gate": const_gate, "const_value": const_value, "w_qkv": w_qkv, "w_out": w_out, "a_qkv": a_qkv, "b_qkv": b_qkv, "a_out": a_out, "b_out": b_out, "w_gate_up": w_gate_up, "w_down": w_down, "a_gate_up": a_gate_up, "b_gate_up": b_gate_up, "a_down": a_down, "b_down": b_down}


PRECISE = lax.Precision.HIGHEST

@jax.custom_vjp
def low(v):
    return lax.optimization_barrier(v.astype(jnp.bfloat16)).astype(jnp.float32)

@jax.custom_vjp
def low_back(v):
    return v

def low_keep(v):
    return (low(v), None)

def low_pass(kept, grad):
    return (grad,)

def back_keep(v):
    return (v, None)

def back_low(kept, grad):
    return (low(grad),)
low.defvjp(low_keep, low_pass)
low_back.defvjp(back_keep, back_low)

def matmul(left, right):
    return jnp.dot(left, right, precision=PRECISE)

def rms_norm(values, gain):
    return values * lax.rsqrt(lax.optimization_barrier(jnp.mean(values * values, axis=-1, keepdims=True)) + 1e-05) * gain

def rotate(values, direction):
    seq_rows = values.shape[0]
    heads_view = values.reshape(seq_rows, HEADS, HEAD)
    half_size = HEAD // 2
    freqs = jnp.exp(jnp.arange(half_size, dtype=jnp.float32) * (-2.0 * math.log(10000.0) / HEAD))
    angles = jnp.arange(seq_rows, dtype=jnp.float32)[:, None] * freqs[None, :]
    cosine = jnp.cos(angles)[:, None, :]
    sine = direction * jnp.sin(angles)[:, None, :]
    first = heads_view[:, :, :half_size]
    second = heads_view[:, :, half_size:]
    turned = jnp.concatenate([first * cosine - second * sine, second * cosine + first * sine], axis=-1)
    return turned.reshape(seq_rows, HEADS * HEAD)

def allowed_mask(bounds, seq_rows):
    places = jnp.arange(seq_rows, dtype=jnp.int32)
    inside = ((places[None, :] >= bounds[:, 0:1]) & (places[None, :] < bounds[:, 1:2])).astype(jnp.float32)
    shared = jnp.einsum('si,sj->ij', inside, inside, precision=PRECISE)
    return (places[:, None] >= places[None, :]) | (shared > 0.5)

def dispatch_table(route_rows):
    entries = route_rows.reshape(-1)
    one_hot = (entries[:, None] == jnp.arange(FFN_EXPERTS, dtype=jnp.int32)[None, :]).astype(jnp.int32)
    before = jnp.cumsum(one_hot, axis=0) - one_hot
    ranked = lax.optimization_barrier(jnp.sum(before * one_hot, axis=1))
    slot_hit = (ranked[None, :] == jnp.arange(CAP, dtype=jnp.int32)[:, None]).astype(jnp.int32)
    table = one_hot.T[:, None, :] * slot_hit[None, :, :]
    return table.reshape(FFN_EXPERTS * CAP, entries.shape[0]).astype(jnp.float32)

def mixture(normed, lowered, ffn_out, route_rows, prev_rows, router_weight, const_gate, const_value):
    logits = jnp.dot(lowered, router_weight, precision=PRECISE) + prev_rows
    route_hot = (route_rows[:, :, None] == jnp.arange(EXPERTS, dtype=jnp.int32)[None, None, :]).astype(jnp.float32)
    chosen = lax.optimization_barrier(jnp.sum(route_hot * logits[:, None, :], axis=2))
    gates = jax.nn.softmax(chosen, axis=1)
    keep_share = jax.nn.sigmoid(jnp.dot(lowered, const_gate, precision=PRECISE))
    is_copy = (route_rows == FFN_EXPERTS + 1).astype(jnp.float32)
    is_first = (route_rows == FFN_EXPERTS + 2).astype(jnp.float32)
    is_second = (route_rows == FFN_EXPERTS + 3).astype(jnp.float32)
    const_first = keep_share[:, 0:1] * normed + (1.0 - keep_share[:, 0:1]) * const_value[0][None, :]
    const_second = keep_share[:, 1:2] * normed + (1.0 - keep_share[:, 1:2]) * const_value[1][None, :]
    outputs = ffn_out + is_copy[:, :, None] * normed[:, None, :]
    outputs = outputs + is_first[:, :, None] * const_first[:, None, :] + is_second[:, :, None] * const_second[:, None, :]
    return lax.optimization_barrier(jnp.sum(gates[:, :, None] * outputs, axis=1))

def attend(query, key_rot, value_low, allowed):
    seq_rows = query.shape[0]
    query_h = query.reshape(seq_rows, HEADS, HEAD)
    key_h = key_rot.reshape(seq_rows, HEADS, HEAD)
    value_h = value_low.reshape(seq_rows, HEADS, HEAD)
    scores = jnp.einsum('qhd,khd->hqk', query_h, key_h, precision=PRECISE) * (1.0 / math.sqrt(HEAD))
    scores = low_back(jnp.where(allowed[None], scores, -1e+30))
    attn_probs = jax.nn.softmax(scores, axis=-1)
    attended = jnp.einsum('hqk,khd->qhd', low(attn_probs), value_h, precision=PRECISE)
    return attended.reshape(seq_rows, HEADS * HEAD)

def attention_block(hidden, bounds, mask_cols, gain_attn, w_qkv, w_out, a_qkv, b_qkv, a_out, b_out):
    seq_rows = hidden.shape[0]
    normed = low(rms_norm(hidden, gain_attn))
    proj_in = low_back(matmul(normed, a_qkv))
    ranks_in = low(proj_in * jnp.tile(mask_cols, 3)[None, :])
    adapted = jnp.einsum('sjr,rjd->sjd', ranks_in.reshape(seq_rows, 3, RANKS_ALL), b_qkv.reshape(RANKS_ALL, 3, D), precision=PRECISE)
    qkv_all = low_back(matmul(normed, w_qkv) + adapted.reshape(seq_rows, 3 * D))
    query = low(rotate(qkv_all[:, :D], 1.0))
    key_rot = low(rotate(qkv_all[:, D:2 * D], 1.0))
    value_low = low(qkv_all[:, 2 * D:])
    mixed = low(low_back(attend(query, key_rot, value_low, allowed_mask(bounds, seq_rows))))
    proj_out = low_back(matmul(mixed, a_out))
    ranks_out = low(proj_out * mask_cols[None, :])
    branch = low_back(matmul(mixed, w_out) + matmul(ranks_out, b_out))
    return hidden + branch

def expert_ffn(tokens, slot_mask, w_gate_up, w_down, a_gate_up, b_gate_up, a_down, b_down):
    slot_rows = tokens.shape[0]
    proj_in = low_back(matmul(tokens, a_gate_up))
    ranks_in = low(proj_in * jnp.concatenate([slot_mask, slot_mask], axis=1))
    adapted = jnp.einsum('njr,rjf->njf', ranks_in.reshape(slot_rows, 2, RANKS_ALL), b_gate_up.reshape(RANKS_ALL, 2, FF), precision=PRECISE)
    both_parts = low_back(matmul(tokens, w_gate_up) + adapted.reshape(slot_rows, 2 * FF))
    hidden = low(jax.nn.silu(both_parts[:, :FF]) * both_parts[:, FF:])
    proj_down = low_back(matmul(hidden, a_down))
    ranks_down = low(proj_down * slot_mask)
    return low(low_back(matmul(hidden, w_down) + matmul(ranks_down, b_down)))

def reference(hidden_in, prev_logits, routes, adapter_ids, image_spans, cotangent, gain_attn, gain_moe, router_weight, const_gate, const_value, w_qkv, w_out, a_qkv, b_qkv, a_out, b_out, w_gate_up, w_down, a_gate_up, b_gate_up, a_down, b_down):
    tables = jax.vmap(jax.vmap(dispatch_table))(routes)
    masks = ((jnp.arange(RANKS_ALL, dtype=jnp.int32) // RANK)[None, None, :] == adapter_ids[:, :, None]).astype(jnp.float32)
    w_qkv_f = w_qkv.astype(jnp.float32)
    w_out_f = w_out.astype(jnp.float32)
    w_gate_up_f = w_gate_up.astype(jnp.float32)
    w_down_f = w_down.astype(jnp.float32)
    trained = (a_qkv.astype(jnp.float32), b_qkv.astype(jnp.float32), a_out.astype(jnp.float32), b_out.astype(jnp.float32), a_gate_up.astype(jnp.float32), b_gate_up.astype(jnp.float32), a_down.astype(jnp.float32), b_down.astype(jnp.float32))

    def forward(inputs, params):
        pa_qkv, pb_qkv, pa_out, pb_out, pa_gu, pb_gu, pa_down, pb_down = params
        results_all = []
        for micro_step in range(MICRO):

            def one_sequence(items):
                hidden, bounds, mask_cols = items
                return attention_block(hidden, bounds, mask_cols, gain_attn, w_qkv_f, w_out_f, pa_qkv, pb_qkv, pa_out, pb_out)
            resid = lax.map(jax.checkpoint(one_sequence), (inputs[micro_step], image_spans[micro_step], masks[micro_step]))
            normed = rms_norm(resid, gain_moe)
            lowered = low(normed)
            doubled = jnp.repeat(lowered, 2, axis=1)
            slots = jnp.einsum('sen,snd->sed', tables[micro_step], doubled, precision=PRECISE)
            slots = low_back(slots)
            slots = slots.reshape(NSEQ, FFN_EXPERTS, CAP, D).transpose(1, 0, 2, 3).reshape(FFN_EXPERTS, NSEQ * CAP, D)
            slot_masks = jnp.broadcast_to(masks[micro_step][None, :, None, :], (FFN_EXPERTS, NSEQ, CAP, RANKS_ALL)).reshape(FFN_EXPERTS, NSEQ * CAP, RANKS_ALL)

            def one_expert(items):
                return expert_ffn(*items)
            outs_slots = lax.map(jax.checkpoint(one_expert), (slots, slot_masks, w_gate_up_f, w_down_f, pa_gu, pb_gu, pa_down, pb_down))
            outs_slots = outs_slots.reshape(FFN_EXPERTS, NSEQ, CAP, D).transpose(1, 0, 2, 3).reshape(NSEQ, FFN_EXPERTS * CAP, D)
            back = jnp.einsum('sen,sed->snd', tables[micro_step], outs_slots, precision=PRECISE).reshape(NSEQ, SEQ, 2, D)
            mixed = jax.vmap(mixture, in_axes=(0, 0, 0, 0, 0, None, None, None))(normed, lowered, back, routes[micro_step], prev_logits[micro_step], router_weight, const_gate, const_value)
            results_all.append(resid + mixed)
        return jnp.stack(results_all)
    output, pullback = jax.vjp(forward, hidden_in.astype(jnp.float32), trained)
    grad_x, grads = pullback(cotangent.astype(jnp.float32))
    return (output.astype(jnp.bfloat16), grad_x, grads[0], grads[1], grads[2], grads[3], grads[4], grads[5], grads[6], grads[7])
```

```python
import functools
import math

import jax
import jax.numpy as jnp
from jax import lax
from jax.experimental import pallas as pl
from jax.experimental.pallas import tpu as pltpu
from jax.sharding import Mesh
from jax.sharding import PartitionSpec as P

D = 768
HEADS = 12
HEAD = 64
FF = 2048
FFN_EXPERTS = 8
RANK = 16
RANKS = 128
CAP = 80
LANES = 128
SEQ = 256
SLOTS = FFN_EXPERTS * CAP
NEG = -1e30
EPS = 1e-05
BF = jnp.bfloat16
F32 = jnp.float32
VMEM_LIMIT = 60 * 1024 * 1024

QKV_BLOCKS, AQKV_BLOCKS, OUT_BLOCKS = 18, 3, 6
GU_BLOCKS, AGU_BLOCKS, DOWN_BLOCKS = 32, 2, 6


def dot(a, b):
    return lax.dot_general(a, b, (((1,), (0,)), ((), ())), preferred_element_type=F32)


def dot_nt(a, b):
    return lax.dot_general(a, b, (((1,), (1,)), ((), ())), preferred_element_type=F32)


def dot_tn(a, b):
    return lax.dot_general(a, b, (((0,), (0,)), ((), ())), preferred_element_type=F32)


def exact_dot(a, b):
    return lax.dot_general(
        a, b, (((1,), (0,)), ((), ())), precision=lax.Precision.HIGHEST, preferred_element_type=F32
    )


def exact_dot_nt(a, b):
    return lax.dot_general(
        a, b, (((1,), (1,)), ((), ())), precision=lax.Precision.HIGHEST, preferred_element_type=F32
    )


def lanes_cat(parts):
    return parts[0] if len(parts) == 1 else jnp.concatenate(parts, axis=1)


def iota(shape, dim):
    return lax.broadcasted_iota(jnp.int32, shape, dim)


def sigmoid(v):
    return 1.0 / (1.0 + jnp.exp(-v))


def whole(shape):
    return pl.BlockSpec(tuple(shape), lambda i, meta: (0,) * len(shape))


def one_micro(shape, micro):
    return pl.BlockSpec((1,) + tuple(shape), lambda i, meta: (micro,) + (0,) * len(shape))


ANYWHERE = pl.BlockSpec(memory_space=pl.ANY)


def call(body, meta, args, specs, outs, scratch=()):
    out_specs = [whole(o.shape) for o in outs]
    return pl.pallas_call(
        body,
        out_shape=outs,
        grid_spec=pltpu.PrefetchScalarGridSpec(
            num_scalar_prefetch=1,
            grid=(1,),
            in_specs=specs,
            out_specs=out_specs,
            scratch_shapes=list(scratch),
        ),
        compiler_params=pltpu.CompilerParams(
            dimension_semantics=("arbitrary",), vmem_limit_bytes=VMEM_LIMIT
        ),
    )(meta, *args)


def shape(dims, dtype):
    return jax.ShapeDtypeStruct(tuple(dims), dtype)


def put_blocks(out, row, src):
    height, width = src.shape
    for j in range(width // LANES):
        out[row : row + height, :] = src[:, j * LANES : (j + 1) * LANES]
        row += height
    return row


def pack_attn_body(meta, w_qkv, a_qkv, w_out, a_out, b_qkv, b_out, out):
    row = 0
    for ref in (w_qkv, a_qkv, w_out, a_out, b_qkv, b_out):
        row = put_blocks(out, row, ref[...])


def pack_experts_body(rel_shape, meta, w_gu, a_gu, w_down, a_down, b_gu, b_down, *outs):
    for rel in range(rel_shape):
        member = meta[0] ^ rel
        row = 0
        for ref in (w_gu, a_gu, w_down, a_down, b_gu, b_down):
            row = put_blocks(outs[rel], row, ref[member])


def slots_body(micros, members, meta, tok, cot, dy0, dy1, info, sid_row, sid_col):
    strict = (iota((SEQ, SEQ), 0) < iota((SEQ, SEQ), 1)).astype(BF)
    experts = iota((FFN_EXPERTS, SEQ), 0)
    for micro, dy in zip(range(micros), (dy0, dy1)):
        turned = tok[micro].T
        route = [turned[16 + k : 17 + k, :].astype(jnp.int32) for k in range(2)]
        hot = [(experts == route[k]).astype(F32) for k in range(2)]
        before = dot((hot[0] + hot[1]).astype(BF), strict)
        sids = []
        for k in range(2):
            rank = jnp.sum(before * hot[k], axis=0, keepdims=True).astype(jnp.int32)
            sids.append(jnp.where(route[k] < FFN_EXPERTS, route[k] * CAP + rank, -1))
        rows = jnp.concatenate(sids + [jnp.zeros((6, SEQ), jnp.int32)], axis=0)
        sid_row[micro] = rows
        sid_col[micro] = rows.astype(F32).T.astype(jnp.int32)
        all_routes = iota((16, SEQ), 0)
        prev = turned[0:16, :]
        named = [
            jnp.sum(jnp.where(all_routes == route[k], prev, 0.0), axis=0, keepdims=True)
            for k in range(2)
        ]
        own_id = jnp.full((1, SEQ), 1, jnp.int32) * meta[members + micro]
        fields = [
            jnp.concatenate(
                [
                    named[1 - k] - named[k],
                    route[1 - k].astype(F32),
                    own_id.astype(F32),
                    jnp.zeros((5, SEQ), F32),
                ],
                axis=0,
            )
            for k in range(2)
        ]
        cotangent = cot[micro, 0]
        for e in range(FFN_EXPERTS):
            at = iota((LANES, SEQ), 0)
            at = jnp.where(at < CAP, at + e * CAP, -2)
            hits = [(at == sids[k]).astype(F32) for k in range(2)]
            info[e, 8 * micro : 8 * micro + 8, :] = exact_dot_nt(fields[0], hits[0]) + exact_dot_nt(
                fields[1], hits[1]
            )
            info[e, 8 * micro + 2 : 8 * micro + 3, :] = jnp.full((1, LANES), 1.0, F32) * (
                meta[members + micro].astype(F32)
            )
            dy[e] = dot((hits[0] + hits[1])[:CAP].astype(BF), cotangent).astype(BF)


def load_wall(pieces, wall, sems, meta, first):
    copies = [
        pltpu.make_async_copy(piece, wall.at[meta[first + i]], sems.at[i])
        for i, piece in enumerate(pieces)
    ]
    for copy in copies:
        copy.start()
    return copies


class AttnWall:
    def __init__(self, wall, n_src):
        self.wall = wall
        self.n_src = n_src
        self.rows = D // n_src
        self.low = RANKS // n_src
        self.base = (QKV_BLOCKS + AQKV_BLOCKS + OUT_BLOCKS + 1) * self.rows

    def block(self, j, count=1):
        return lanes_cat(
            [
                self.wall[:, (j + i) * self.rows : (j + i + 1) * self.rows, :].reshape(D, LANES)
                for i in range(count)
            ]
        )

    def rank_block(self, j, count=1):
        return lanes_cat(
            [
                self.wall[
                    :, self.base + (j + i) * self.low : self.base + (j + i + 1) * self.low, :
                ].reshape(RANKS, LANES)
                for i in range(count)
            ]
        )

    def qkv(self, j, count=1):
        return self.block(j, count)

    def a_qkv(self, j=0, count=3):
        return self.block(QKV_BLOCKS + j, count)

    def w_out(self):
        return self.block(QKV_BLOCKS + AQKV_BLOCKS, OUT_BLOCKS)

    def a_out(self):
        return self.block(QKV_BLOCKS + AQKV_BLOCKS + OUT_BLOCKS)

    def b_qkv(self, j, count=1):
        return self.rank_block(j, count)

    def b_out(self):
        return self.rank_block(QKV_BLOCKS, OUT_BLOCKS)


def turn(v, cos, sin):
    ahead = pltpu.roll(v, LANES - HEAD // 2, axis=1)
    behind = pltpu.roll(v, HEAD // 2, axis=1)
    first = (iota(v.shape, 1) % HEAD) < HEAD // 2
    return v * cos + jnp.where(first, ahead, behind) * sin


def rank_mask(which):
    return ((iota((1, RANKS), 1) // RANK) == which).astype(F32)


def allowed_bias(meta, at):
    t = iota((SEQ, SEQ), 0)
    u = iota((SEQ, SEQ), 1)
    ok = t >= u
    for j in range(2):
        start, end = meta[at + 2 * j], meta[at + 2 * j + 1]
        ok = ok | ((t >= start) & (t < end) & (u >= start) & (u < end))
    return jnp.concatenate([ok, ok], axis=0)


def split_heads(v):
    low = (iota((1, LANES), 1) < HEAD).astype(v.dtype)
    return jnp.concatenate([v * low, v * (1 - low).astype(v.dtype)], axis=0)


def join_heads(v):
    low = iota((SEQ, LANES), 1) < HEAD
    return jnp.where(low, v[:SEQ], v[SEQ:])


def attn_forward_body(
    micro, n_src, meta, hid, cos_ref, sin_ref, gain_a, gain_m, sid_row, *refs
):
    pieces = refs[:n_src]
    qkv, attended, ranks, resid, lse, send, wall_ref, sems = refs[n_src:]
    copies = load_wall(pieces, wall_ref, sems, meta, 0)
    wall = AttnWall(wall_ref, n_src)
    at_id = n_src + 1 + micro
    at_span = n_src + 3 + 4 * micro
    hidden = hid[0, 0].astype(F32)
    scale = lax.rsqrt(jnp.mean(hidden * hidden, axis=-1, keepdims=True) + EPS)
    normed = (hidden * scale * gain_a[...]).astype(BF)
    mask = rank_mask(meta[at_id])
    ok = allowed_bias(meta, at_span)
    cos, sin = cos_ref[...], sin_ref[...]
    for copy in copies:
        copy.wait()
    proj = dot(normed, wall.a_qkv())
    ranks_in = [(proj[:, j * RANKS : (j + 1) * RANKS] * mask).astype(BF) for j in range(3)]
    for j in range(3):
        ranks[:, j * RANKS : (j + 1) * RANKS] = ranks_in[j]
    for j in range(3):
        for pair in range(3):
            at = j * 6 + pair * 2
            part = dot(normed, wall.qkv(at, 2)) + dot(ranks_in[j], wall.b_qkv(at, 2))
            for half in range(2):
                one = part[:, half * LANES : (half + 1) * LANES]
                if j < 2:
                    one = turn(one, cos, sin)
                qkv[:, (at + half) * LANES : (at + half + 1) * LANES] = one.astype(BF)
    lse_cols = []
    for pair in range(6):
        query = qkv[:, pair * LANES : (pair + 1) * LANES]
        key = qkv[:, (6 + pair) * LANES : (7 + pair) * LANES]
        value = qkv[:, (12 + pair) * LANES : (13 + pair) * LANES]
        scores = jnp.where(ok, dot_nt(split_heads(query), key) * (1.0 / math.sqrt(HEAD)), NEG)
        top = jnp.max(scores, axis=-1, keepdims=True)
        expo = jnp.exp(scores - top)
        total = jnp.sum(expo, axis=-1, keepdims=True)
        probs = (expo * (1.0 / total)).astype(BF)
        attended[:, pair * LANES : (pair + 1) * LANES] = join_heads(dot(probs, value)).astype(BF)
        logs = top + jnp.log(total)
        lse[:, pair : pair + 1] = logs
    mixed = attended[...]
    ranks_out = (dot(mixed, wall.a_out()) * mask).astype(BF)
    ranks[:, 3 * RANKS :] = ranks_out
    out = hidden + dot(mixed, wall.w_out()) + dot(ranks_out, wall.b_out())
    resid[...] = out
    scale_m = lax.rsqrt(jnp.mean(out * out, axis=-1, keepdims=True) + EPS)
    lowered = (out * scale_m * gain_m[...]).astype(BF)
    sids = sid_row[0]
    at = iota((SLOTS, SEQ), 0)
    table = ((at == sids[0:1, :]) | (at == sids[1:2, :])).astype(F32).astype(BF)
    send[...] = dot(table, lowered).astype(BF).reshape(FFN_EXPERTS, CAP, D)


class ExpertWall:
    def __init__(self, wall, n_src):
        self.wall = wall
        self.n_src = n_src
        self.rows = D // n_src
        self.ff = FF // n_src
        self.low = RANKS // n_src
        self.down_at = (GU_BLOCKS + AGU_BLOCKS) * self.rows
        self.rank_at = self.down_at + (DOWN_BLOCKS + 1) * self.ff

    def block(self, j):
        start = j * self.rows
        if not isinstance(j, int):
            start = pl.multiple_of(start, self.rows)
        return self.wall[:, pl.ds(start, self.rows), :].reshape(D, LANES)

    def gate_up(self, j, count):
        return lanes_cat([self.block(j + i) for i in range(count)])

    def a_gate_up(self):
        return lanes_cat([self.block(GU_BLOCKS + i) for i in range(AGU_BLOCKS)])

    def rank_block(self, j):
        start = self.rank_at + j * self.low
        if not isinstance(j, int):
            start = pl.multiple_of(start, self.low)
        return self.wall[:, pl.ds(start, self.low), :].reshape(RANKS, LANES)

    def b_gate_up(self, j, count):
        return lanes_cat([self.rank_block(j + i) for i in range(count)])

    def b_down(self):
        return lanes_cat([self.rank_block(GU_BLOCKS + i) for i in range(DOWN_BLOCKS)])

    def down(self, src, count):
        return lanes_cat(
            [
                self.wall[
                    pl.ds(src, count), self.down_at + i * self.ff : self.down_at + (i + 1) * self.ff, :
                ].reshape(count * self.ff, LANES)
                for i in range(DOWN_BLOCKS)
            ]
        )

    def a_down(self, src, count):
        start = self.down_at + DOWN_BLOCKS * self.ff
        return self.wall[pl.ds(src, count), start : start + self.ff, :].reshape(
            count * self.ff, LANES
        )


CHUNK = 512


def expert_body(micro, n_src, carried, meta, tin, dyp, info, route_w, *refs):
    if carried:
        before, refs = refs[0], refs[1:]
    pieces = refs[:n_src]
    fo, dtin, grads, wall_ref, sems, fo_acc, dt_acc, pd_acc, dug_acc = refs[n_src:]
    copies = load_wall(pieces, wall_ref, sems, meta, 0)
    wall = ExpertWall(wall_ref, n_src)
    own = meta[n_src]
    tokens = tin[...].reshape(SLOTS, D)
    cols = jnp.concatenate(
        [info[s, 8 * micro : 8 * micro + 8, :].T[:CAP] for s in range(FFN_EXPERTS)], axis=0
    )
    logits = exact_dot(tokens.astype(F32), route_w[...])
    lane = iota((SLOTS, LANES), 1)
    gap = jnp.sum(
        jnp.where(lane == own, logits, 0.0)
        - jnp.where(lane == cols[:, 1:2].astype(jnp.int32), logits, 0.0),
        axis=1,
        keepdims=True,
    )
    gate = sigmoid(gap - cols[:, 0:1])
    mask = ((lane // RANK) == cols[:, 2:3].astype(jnp.int32)).astype(F32)
    d_out = (dyp[...].reshape(SLOTS, D).astype(F32) * gate).astype(BF)
    for copy in copies:
        copy.wait()

    def total(at, part):
        return part

    a_gu = wall.a_gate_up()
    proj = dot(tokens, a_gu)
    ranks_in = [(proj[:, j * RANKS : (j + 1) * RANKS] * mask).astype(BF) for j in range(2)]
    d_ranks_down = (dot_nt(d_out, wall.b_down()) * mask).astype(BF)
    fo_acc[...] = jnp.zeros_like(fo_acc)
    dt_acc[...] = jnp.zeros_like(dt_acc)
    pd_acc[...] = jnp.zeros_like(pd_acc)
    dug_acc[...] = jnp.zeros_like(dug_acc)
    blocks = CHUNK // LANES
    srcs = max(1, CHUNK // wall.ff)
    gb_at = AGU_BLOCKS * wall.rows
    ad_at = gb_at + GU_BLOCKS * wall.low
    bd_at = ad_at + wall.ff

    def step(f, carry):
        j = f * blocks
        wg = wall.gate_up(j, blocks)
        wu = wall.gate_up(j + GU_BLOCKS // 2, blocks)
        bg = wall.b_gate_up(j, blocks)
        bu = wall.b_gate_up(j + GU_BLOCKS // 2, blocks)
        wd = wall.down(f * srcs, srcs)
        ad = wall.a_down(f * srcs, srcs)
        g = dot(tokens, wg) + dot(ranks_in[0], bg)
        u = dot(tokens, wu) + dot(ranks_in[1], bu)
        d_hidden = dot_nt(d_out, wd) + dot_nt(d_ranks_down, ad)
        sg = sigmoid(g)
        act = g * sg
        hidden = (act * u).astype(BF)
        d_gate = (d_hidden * u * (sg * (1.0 + g * (1.0 - sg)))).astype(BF)
        d_up = (d_hidden * act).astype(BF)
        fo_acc[...] += dot(hidden, wd)
        pd_acc[...] += dot(hidden, ad)
        dt_acc[...] += dot_nt(d_gate, wg) + dot_nt(d_up, wu)
        dug_acc[:, :RANKS] += dot_nt(d_gate, bg)
        dug_acc[:, RANKS:] += dot_nt(d_up, bu)
        for k, (rank, grad) in enumerate(((ranks_in[0], d_gate), (ranks_in[1], d_up))):
            part = dot_tn(rank, grad)
            for i in range(blocks):
                at = gb_at + (j + k * (GU_BLOCKS // 2) + i) * wall.low
                rows = pl.ds(at if isinstance(at, int) else pl.multiple_of(at, 8), wall.low)
                one = part[:, i * LANES : (i + 1) * LANES].reshape(n_src, wall.low, LANES)
                grads[:, rows, :] = one
        part = dot_tn(hidden, d_ranks_down).reshape(srcs, wall.ff, LANES)
        grads[pl.ds(f * srcs, srcs), ad_at : ad_at + wall.ff, :] = part
        return carry

    if wall.low % 8:
        for f in range(FF // CHUNK):
            step(f, 0)
    else:
        lax.fori_loop(0, FF // CHUNK, step, 0)
    ranks_down = (pd_acc[...] * mask).astype(BF)
    fo[...] = (fo_acc[...] + dot(ranks_down, wall.b_down())).astype(BF).reshape(
        FFN_EXPERTS, CAP, D
    )
    part = dot_tn(ranks_down, d_out)
    for i in range(DOWN_BLOCKS):
        grads[:, bd_at + i * wall.low : bd_at + (i + 1) * wall.low, :] = part[
            :, i * LANES : (i + 1) * LANES
        ].reshape(n_src, wall.low, LANES)
    d_ranks = [(dug_acc[:, k * RANKS : (k + 1) * RANKS] * mask).astype(BF) for k in range(2)]
    both = lanes_cat(d_ranks)
    dtin[...] = (dt_acc[...] + dot_nt(both, a_gu)).astype(BF).reshape(FFN_EXPERTS, CAP, D)
    part = dot_tn(tokens, both)
    for i in range(AGU_BLOCKS):
        grads[:, i * wall.rows : (i + 1) * wall.rows, :] = part[
            :, i * LANES : (i + 1) * LANES
        ].reshape(n_src, wall.rows, LANES)
    if carried:
        grads[...] = grads[...] + before[...]


def attn_backward_body(micro, n_src, carried, meta, hid, cot, resid_ref, qkv, attended, ranks, lse,
                       fo, dtin, tok, sid_col, gain_a, gain_m, route_w, consts, cos_ref, sin_ref,
                       *refs):
    if carried:
        before, refs = refs[0], refs[1:]
    pieces = refs[:n_src]
    block_out, grad_in, grads, wall_ref, sems, dqkv = refs[n_src:]
    copies = load_wall(pieces, wall_ref, sems, meta, 0)
    wall = AttnWall(wall_ref, n_src)
    at_id = n_src + 1 + micro
    at_span = n_src + 3 + 4 * micro
    mask = rank_mask(meta[at_id])
    resid = resid_ref[...]
    dy = cot[0, 0].astype(F32)
    scale_m = lax.rsqrt(jnp.mean(resid * resid, axis=-1, keepdims=True) + EPS)
    gain = gain_m[...]
    normed = resid * scale_m * gain
    lowered = normed.astype(BF).astype(F32)
    weights = route_w[...]
    scores = exact_dot(lowered, weights)
    token = tok[0]
    lane = iota((SEQ, LANES), 1)
    route = [token[:, 16 + k : 17 + k].astype(jnp.int32) for k in range(2)]
    logits = scores + token
    chosen = [
        jnp.sum(jnp.where(lane == route[k], logits, 0.0), axis=1, keepdims=True) for k in range(2)
    ]
    gate = [sigmoid(chosen[k] - chosen[1 - k]) for k in range(2)]
    keep = [sigmoid(scores[:, 12 + j : 13 + j]) for j in range(2)]
    slot = iota((SEQ, SLOTS), 1)
    hits = [(slot == sid_col[0][:, k : k + 1]).astype(F32).astype(BF) for k in range(2)]
    returned = fo[...].reshape(SLOTS, D)
    from_experts = [dot(hits[k], returned) for k in range(2)]
    value = [consts[j : j + 1, :] for j in range(2)]
    is_copy = [(route[k] == FFN_EXPERTS + 1).astype(F32) for k in range(2)]
    is_const = [
        [(route[k] == FFN_EXPERTS + 2 + j).astype(F32) for j in range(2)] for k in range(2)
    ]
    share = sum(
        gate[k] * (is_copy[k] + is_const[k][0] * keep[0] + is_const[k][1] * keep[1])
        for k in range(2)
    )
    named = [gate[0] * is_const[0][j] + gate[1] * is_const[1][j] for j in range(2)]
    out = resid + gate[0] * from_experts[0] + gate[1] * from_experts[1] + share * normed
    out = out + (named[0] * (1.0 - keep[0])) * value[0] + (named[1] * (1.0 - keep[1])) * value[1]
    block_out[...] = out.astype(BF)
    dy_normed = jnp.sum(dy * normed, axis=1, keepdims=True)
    dy_value = [jnp.sum(dy * value[j], axis=1, keepdims=True) for j in range(2)]
    d_gate = []
    for k in range(2):
        one = jnp.sum(dy * from_experts[k], axis=1, keepdims=True) + is_copy[k] * dy_normed
        for j in range(2):
            one = one + is_const[k][j] * (keep[j] * dy_normed + (1.0 - keep[j]) * dy_value[j])
        d_gate.append(one)
    centre = gate[0] * d_gate[0] + gate[1] * d_gate[1]
    d_logits = jnp.zeros((SEQ, LANES), F32)
    for k in range(2):
        d_logits = d_logits + jnp.where(lane == route[k], gate[k] * (d_gate[k] - centre), 0.0)
    for j in range(2):
        d_keep = named[j] * (dy_normed - dy_value[j])
        d_logits = d_logits + jnp.where(
            lane == 12 + j, d_keep * keep[j] * (1.0 - keep[j]), 0.0
        )
    d_normed = share * dy + exact_dot_nt(d_logits, weights)
    d_normed = d_normed + dot(hits[0] + hits[1], dtin[...].reshape(SLOTS, D))
    scaled = gain * d_normed
    d_resid = (
        dy
        + scale_m * scaled
        - resid * (scale_m * scale_m * scale_m) * jnp.mean(scaled * resid, axis=-1, keepdims=True)
    )
    d_branch = d_resid.astype(BF)
    for copy in copies:
        copy.wait()
    d_ranks_out = (dot_nt(d_branch, wall.b_out()) * mask).astype(BF)
    d_mixed = (dot_nt(d_branch, wall.w_out()) + dot_nt(d_ranks_out, wall.a_out())).astype(BF)
    a_rows, b_rows = wall.rows, wall.low
    gb_at = AQKV_BLOCKS * a_rows
    ao_at = gb_at + QKV_BLOCKS * b_rows
    bo_at = ao_at + a_rows
    part = dot_tn(ranks[:, 3 * RANKS :], d_branch)
    for i in range(OUT_BLOCKS):
        grads[:, bo_at + i * b_rows : bo_at + (i + 1) * b_rows, :] = part[
            :, i * LANES : (i + 1) * LANES
        ].reshape(n_src, b_rows, LANES)
    grads[:, ao_at : ao_at + a_rows, :] = dot_tn(attended[...], d_ranks_out).reshape(
        n_src, a_rows, LANES
    )
    ok = allowed_bias(meta, at_span)
    cos, sin = cos_ref[...], -sin_ref[...]
    inv = 1.0 / math.sqrt(HEAD)
    for pair in range(6):
        query = split_heads(qkv[:, pair * LANES : (pair + 1) * LANES])
        key = qkv[:, (6 + pair) * LANES : (7 + pair) * LANES]
        val = qkv[:, (12 + pair) * LANES : (13 + pair) * LANES]
        d_heads = split_heads(d_mixed[:, pair * LANES : (pair + 1) * LANES])
        sc = jnp.where(ok, dot_nt(query, key) * inv, NEG)
        probs = jnp.exp(sc - lse[:, pair : pair + 1])
        d_probs = dot_nt(d_heads, val)
        row_dot = jnp.sum(probs * d_probs, axis=-1, keepdims=True)
        d_scores = (probs * (d_probs - row_dot)).astype(BF)
        d_query = join_heads(dot(d_scores, key)) * inv
        d_key = dot_tn(d_scores, query) * inv
        d_value = dot_tn(probs.astype(BF), d_heads)
        dqkv[:, pair * LANES : (pair + 1) * LANES] = turn(d_query, cos, sin).astype(BF)
        dqkv[:, (6 + pair) * LANES : (7 + pair) * LANES] = turn(d_key, cos, sin).astype(BF)
        dqkv[:, (12 + pair) * LANES : (13 + pair) * LANES] = d_value.astype(BF)
    hidden = hid[0, 0].astype(F32)
    scale = lax.rsqrt(jnp.mean(hidden * hidden, axis=-1, keepdims=True) + EPS)
    first = gain_a[...]
    normed_low = (hidden * scale * first).astype(BF)
    d_in = jnp.zeros((SEQ, D), F32)
    d_ranks = []
    for j in range(3):
        part = dqkv[:, j * D : (j + 1) * D]
        d_ranks.append((dot_nt(part, wall.b_qkv(j * 6, 6)) * mask).astype(BF))
        d_in = d_in + dot_nt(part, wall.qkv(j * 6, 6))
        gb = dot_tn(ranks[:, j * RANKS : (j + 1) * RANKS], part)
        for i in range(6):
            at = gb_at + (j * 6 + i) * b_rows
            grads[:, at : at + b_rows, :] = gb[:, i * LANES : (i + 1) * LANES].reshape(
                n_src, b_rows, LANES
            )
    ranks_all = lanes_cat(d_ranks)
    d_in = d_in + dot_nt(ranks_all, wall.a_qkv())
    ga = dot_tn(normed_low, ranks_all)
    for i in range(3):
        grads[:, i * a_rows : (i + 1) * a_rows, :] = ga[:, i * LANES : (i + 1) * LANES].reshape(
            n_src, a_rows, LANES
        )
    scaled = first * d_in
    grad_in[...] = (
        d_resid
        + scale * scaled
        - hidden * (scale * scale * scale) * jnp.mean(scaled * hidden, axis=-1, keepdims=True)
    )
    if carried:
        grads[...] = grads[...] + before[...]


def flip(values, axis, bit, size):
    return lax.ppermute(values, axis, [(i, i ^ bit) for i in range(size)])


def bits(size):
    return [1 << i for i in range(size.bit_length() - 1)]


def halve_sum(values, axis, size):
    place = lax.axis_index(axis)
    for bit in reversed(bits(size)):
        pair = values.reshape((2, values.shape[0] // 2) + values.shape[1:])
        side = (place // bit) % 2
        away = lax.dynamic_index_in_dim(pair, 1 - side, 0, keepdims=False).astype(BF)
        kept = lax.dynamic_index_in_dim(pair, side, 0, keepdims=False)
        values = kept + flip(away, axis, bit, size).astype(F32)
    return values


def body(members, hidden_in, prev_logits, routes, adapter_ids, image_spans, cotangent, gain_attn,
         gain_moe, router_weight, const_gate, const_value, w_qkv, w_out, a_qkv, b_qkv, a_out, b_out,
         w_gate_up, w_down, a_gate_up, b_gate_up, a_down, b_down):
    rest = lax.axis_size("y")
    peers = lax.axis_size("z")
    n_src = rest * members * 2
    micros = hidden_in.shape[0]
    y, x, c, z = (lax.axis_index(name) for name in ("y", "x", "c", "z"))
    place = (y * members + x) * 2 + c

    attn_rows = (QKV_BLOCKS + AQKV_BLOCKS + OUT_BLOCKS + 1) * (D // n_src) + (
        QKV_BLOCKS + OUT_BLOCKS
    ) * (RANKS // n_src)
    expert_rows = (
        (GU_BLOCKS + AGU_BLOCKS) * (D // n_src)
        + (DOWN_BLOCKS + 1) * (FF // n_src)
        + (GU_BLOCKS + DOWN_BLOCKS) * (RANKS // n_src)
    )
    none = jnp.zeros((1,), jnp.int32)
    args = (w_qkv, a_qkv, w_out, a_out, b_qkv, b_out)
    (attn_own,) = call(
        pack_attn_body, none, args, [whole(a.shape) for a in args], [shape((attn_rows, LANES), BF)]
    )
    args = (w_gate_up, a_gate_up, w_down, a_down, b_gate_up, b_down)
    expert_own = call(
        functools.partial(pack_experts_body, members),
        x.reshape(1).astype(jnp.int32),
        args,
        [whole(a.shape) for a in args],
        [shape((expert_rows, LANES), BF)] * members,
    )

    attn_pieces = [(attn_own, 0)]
    for bit in bits(rest):
        attn_pieces += [
            (flip(v, "y", bit, rest), m ^ (bit * members * 2)) for v, m in attn_pieces
        ]
    for bit in bits(members):
        attn_pieces += [(flip(v, "x", bit, members), m ^ (bit * 2)) for v, m in attn_pieces]
    attn_link = [v for v, m in attn_pieces]
    attn_pieces += [(flip(v, "c", 1, 2), m ^ 1) for v, m in attn_pieces]

    expert_pieces = [(expert_own[0], 0)]
    for rel in range(1, members):
        expert_pieces.append(
            (lax.ppermute(expert_own[rel], "x", [(i, i ^ rel) for i in range(members)]), rel * 2)
        )
    for bit in bits(rest):
        expert_pieces += [
            (flip(v, "y", bit, rest), m ^ (bit * members * 2)) for v, m in expert_pieces
        ]
    expert_pieces += [(flip(v, "c", 1, 2), m ^ 1) for v, m in expert_pieces]

    meta_attn = jnp.concatenate(
        [
            place ^ jnp.array([m for v, m in attn_pieces], jnp.int32),
            jnp.zeros((1,), jnp.int32),
            adapter_ids.reshape(-1),
            image_spans.reshape(-1),
        ]
    ).astype(jnp.int32)
    meta_expert = jnp.concatenate(
        [
            place ^ jnp.array([m for v, m in expert_pieces], jnp.int32),
            (z * members + x).reshape(1),
        ]
    ).astype(jnp.int32)
    attn_bufs = [v for v, m in attn_pieces]
    expert_bufs = [v for v, m in expert_pieces]

    tok = jnp.concatenate(
        [
            prev_logits[:, 0],
            jnp.zeros((micros, SEQ, 4), F32),
            routes[:, 0].astype(F32),
            jnp.zeros((micros, SEQ, LANES - 18), F32),
        ],
        axis=2,
    )
    route_w = jnp.concatenate(
        [router_weight, const_gate, jnp.zeros((D, LANES - 14), F32)], axis=1
    )
    half = HEAD // 2
    freqs = jnp.exp(jnp.arange(half, dtype=F32) * (-2.0 * math.log(10000.0) / HEAD))
    angles = jnp.arange(SEQ, dtype=F32)[:, None] * freqs[None, :]
    cos = jnp.tile(jnp.cos(angles), (1, 4))
    sin = jnp.sin(angles)
    sin = jnp.tile(jnp.concatenate([-sin, sin], axis=1), (1, 2))
    gain_a = gain_attn.reshape(1, D)
    gain_m = gain_moe.reshape(1, D)

    packet = shape((FFN_EXPERTS, CAP, D), BF)
    *dy_send, info, sid_row, sid_col = call(
        functools.partial(slots_body, micros, 0),
        adapter_ids.reshape(-1),
        (tok, cotangent),
        [whole(tok.shape), whole(cotangent.shape)],
        [
            packet,
            packet,
            shape((FFN_EXPERTS, 8 * micros, LANES), F32),
            shape((micros, 8, SEQ), jnp.int32),
            shape((micros, SEQ, 8), jnp.int32),
        ],
    )

    group = ("z", "x") if members > 1 else "z"

    def trade(values):
        return lax.all_to_all(values, group, 0, 0, tiled=True)

    info = trade(info)
    dy_got = [trade(v) for v in dy_send]

    saved = []
    for micro in range(micros):
        args = (hidden_in, cos, sin, gain_a, gain_m, sid_row, *attn_bufs)
        specs = [
            one_micro((1, SEQ, D), micro),
            whole(cos.shape),
            whole(sin.shape),
            whole(gain_a.shape),
            whole(gain_m.shape),
            one_micro((8, SEQ), micro),
        ] + [ANYWHERE] * n_src
        saved.append(
            call(
                functools.partial(attn_forward_body, micro, n_src),
                meta_attn,
                args,
                specs,
                [
                    shape((SEQ, 3 * D), BF),
                    shape((SEQ, D), BF),
                    shape((SEQ, 4 * RANKS), BF),
                    shape((SEQ, D), F32),
                    shape((2 * SEQ, 8), F32),
                    packet,
                ],
                [
                    pltpu.VMEM((n_src, attn_rows, LANES), BF),
                    pltpu.SemaphoreType.DMA((n_src,)),
                ],
            )
        )
    tin = [trade(parts[-1]) for parts in saved]

    expert_grad_rows = (
        AGU_BLOCKS * (D // n_src)
        + (GU_BLOCKS + DOWN_BLOCKS) * (RANKS // n_src)
        + FF // n_src
    )
    grads_e = None
    returned = []
    for micro in range(micros):
        carried = grads_e is not None
        args = (tin[micro], dy_got[micro], info, route_w)
        if carried:
            args += (grads_e,)
        specs = [whole(a.shape) for a in args] + [ANYWHERE] * n_src
        fo, dtin, grads_e = call(
            functools.partial(expert_body, micro, n_src, carried),
            meta_expert,
            args + tuple(expert_bufs),
            specs,
            [packet, packet, shape((n_src, expert_grad_rows, LANES), F32)],
            [
                pltpu.VMEM((n_src, expert_rows, LANES), BF),
                pltpu.SemaphoreType.DMA((n_src,)),
                pltpu.VMEM((SLOTS, D), F32),
                pltpu.VMEM((SLOTS, D), F32),
                pltpu.VMEM((SLOTS, RANKS), F32),
                pltpu.VMEM((SLOTS, 2 * RANKS), F32),
            ],
        )
        returned.append((trade(fo), trade(dtin)))

    attn_grad_rows = (AQKV_BLOCKS + 1) * (D // n_src) + (QKV_BLOCKS + OUT_BLOCKS) * (
        RANKS // n_src
    )
    grads_a = None
    block_rows, grad_rows = [], []
    for micro in range(micros):
        carried = grads_a is not None
        qkv, attended, ranks, resid, lse, _ = saved[micro]
        args = (hidden_in, cotangent, resid, qkv, attended, ranks, lse, *returned[micro], tok,
                sid_col, gain_a, gain_m, route_w, const_value, cos, sin)
        specs = [whole(a.shape) for a in args]
        specs[0] = one_micro((1, SEQ, D), micro)
        specs[1] = one_micro((1, SEQ, D), micro)
        specs[9] = one_micro((SEQ, LANES), micro)
        specs[10] = one_micro((SEQ, 8), micro)
        if carried:
            args += (grads_a,)
            specs.append(whole(grads_a.shape))
        specs += [ANYWHERE] * n_src
        block_out, grad_in, grads_a = call(
            functools.partial(attn_backward_body, micro, n_src, carried),
            meta_attn,
            args + tuple(attn_bufs),
            specs,
            [
                shape((SEQ, D), BF),
                shape((SEQ, D), F32),
                shape((n_src, attn_grad_rows, LANES), F32),
            ],
            [
                pltpu.VMEM((n_src, attn_rows, LANES), BF),
                pltpu.SemaphoreType.DMA((n_src,)),
                pltpu.VMEM((SEQ, 3 * D), BF),
            ],
        )
        block_rows.append(block_out)
        grad_rows.append(grad_in)

    total = grads_e.reshape((rest, members, 2) + grads_e.shape[1:])
    total = halve_sum(jnp.moveaxis(total, 2, 0), "c", 2)
    total = total.reshape((rest, members) + grads_e.shape[1:])
    total = halve_sum(total, "y", rest).reshape((members,) + grads_e.shape[1:])
    owned = lax.dynamic_index_in_dim(total, x, 0, keepdims=True)
    for rel in range(1, members):
        away = lax.dynamic_index_in_dim(total, x ^ rel, 0, keepdims=True).astype(BF)
        got = lax.ppermute(away, "x", [(i, i ^ rel) for i in range(members)])
        owned = jnp.concatenate([owned, got.astype(F32)], axis=0)
    if members > 1:
        owned = owned[x ^ jnp.arange(members)]

    def blocks_of(values, row, count, height):
        part = values[:, row : row + count * height].reshape(-1, count, height, LANES)
        return jnp.moveaxis(part, 1, 2).reshape(-1, height, count * LANES)

    rows, low, ff = D // n_src, RANKS // n_src, FF // n_src
    at = 0
    grad_agu = blocks_of(owned, at, AGU_BLOCKS, rows)
    at += AGU_BLOCKS * rows
    grad_bgu = blocks_of(owned, at, GU_BLOCKS, low)
    at += GU_BLOCKS * low
    grad_ad = blocks_of(owned, at, 1, ff)
    at += ff
    grad_bd = blocks_of(owned, at, DOWN_BLOCKS, low)

    total = grads_a.reshape((rest, members, 2) + grads_a.shape[1:])
    total = halve_sum(jnp.moveaxis(total, 2, 0), "c", 2)
    total = total.reshape((rest, members) + grads_a.shape[1:])
    total = halve_sum(total, "y", rest).reshape((members,) + grads_a.shape[1:])
    total = halve_sum(total, "x", members).reshape((1,) + grads_a.shape[1:])
    for bit in bits(peers):
        sent = total.astype(BF)
        total = sent.astype(F32) + flip(sent, "z", bit, peers).astype(F32)
    at = 0
    grad_aq = blocks_of(total, at, AQKV_BLOCKS, rows)[0]
    at += AQKV_BLOCKS * rows
    grad_bq = blocks_of(total, at, QKV_BLOCKS, low)[0]
    at += QKV_BLOCKS * low
    grad_ao = blocks_of(total, at, 1, rows)[0]
    at += rows
    grad_bo = blocks_of(total, at, OUT_BLOCKS, low)[0]

    return (jnp.stack(block_rows)[:, None], jnp.stack(grad_rows)[:, None], grad_aq, grad_bq,
            grad_ao, grad_bo, grad_agu, grad_bgu, grad_ad, grad_bd)


def solution(mesh):
    dp, expert = mesh.shape["dp"], mesh.shape["expert"]
    members = FFN_EXPERTS // expert
    fine = Mesh(
        mesh.devices.reshape(dp // (2 * members), members, 2, expert), ("y", "x", "c", "z")
    )
    owners = ("y", "x", "c")
    seqs = ("y", "x", "c", "z")
    tokens = P(None, seqs, None, None)
    rows = P(owners, None)
    expert_rows = P("z", owners, None)
    in_specs = (
        (tokens, tokens, tokens, P(None, seqs), tokens, tokens)
        + (P(),) * 5
        + (rows,) * 6
        + (expert_rows,) * 6
    )
    out_specs = (tokens, tokens) + (rows,) * 4 + (expert_rows,) * 4
    return jax.shard_map(
        functools.partial(body, members),
        mesh=fine,
        in_specs=in_specs,
        out_specs=out_specs,
        check_vma=False,
    )
```

```python
import functools
import math

import jax
import jax.numpy as jnp
from jax import lax
from jax.experimental import pallas as pl
from jax.experimental.pallas import tpu as pltpu
from jax.sharding import Mesh
from jax.sharding import PartitionSpec as P

D = 768
HEADS = 12
HEAD = 64
FF = 2048
FFN_EXPERTS = 8
RANK = 16
RANKS = 128
CAP = 80
LANES = 128
SEQ = 256
SLOTS = FFN_EXPERTS * CAP
BLOCKS, SIDE = D // LANES, 8
NEG = -1e30
EPS = 1e-05
BF = jnp.bfloat16
F32 = jnp.float32
VMEM_LIMIT = 60 * 1024 * 1024
FLOPS_PER_US, BYTES_PER_US = 10**9, 10**6
FORWARD_HINT = 12

QKV_BLOCKS, AQKV_BLOCKS, OUT_BLOCKS = 18, 3, 6
GU_BLOCKS, AGU_BLOCKS, DOWN_BLOCKS = 32, 2, 6


def dot(a, b):
    return lax.dot_general(a, b, (((1,), (0,)), ((), ())), preferred_element_type=F32)


def dot_nt(a, b):
    return lax.dot_general(a, b, (((1,), (1,)), ((), ())), preferred_element_type=F32)


def dot_tn(a, b):
    return lax.dot_general(a, b, (((0,), (0,)), ((), ())), preferred_element_type=F32)


def exact_dot(a, b):
    return lax.dot_general(
        a, b, (((1,), (0,)), ((), ())), precision=lax.Precision.HIGHEST, preferred_element_type=F32
    )


def exact_dot_nt(a, b):
    return lax.dot_general(
        a, b, (((1,), (1,)), ((), ())), precision=lax.Precision.HIGHEST, preferred_element_type=F32
    )


def lanes_cat(parts):
    return parts[0] if len(parts) == 1 else jnp.concatenate(parts, axis=1)


def iota(shape, dim):
    return lax.broadcasted_iota(jnp.int32, shape, dim)


def sigmoid(v):
    return 1.0 / (1.0 + jnp.exp(-v))


def whole(shape):
    return pl.BlockSpec(tuple(shape), lambda i, meta: (0,) * len(shape))


def one_micro(shape, micro):
    return pl.BlockSpec((1,) + tuple(shape), lambda i, meta: (micro,) + (0,) * len(shape))


ANYWHERE = pl.BlockSpec(memory_space=pl.ANY)


def call(body, meta, args, specs, outs, scratch=(), us=1, after=()):
    out_specs = [whole(o.shape) for o in outs]

    def late(meta_ref, *refs):
        body(meta_ref, *refs[len(after) :])

    args = tuple(after) + tuple(args)
    specs = [ANYWHERE] * len(after) + list(specs)
    return pl.pallas_call(
        late if after else body,
        out_shape=outs,
        cost_estimate=pl.CostEstimate(
            flops=us * FLOPS_PER_US, transcendentals=0, bytes_accessed=us * BYTES_PER_US
        ),
        grid_spec=pltpu.PrefetchScalarGridSpec(
            num_scalar_prefetch=1,
            grid=(1,),
            in_specs=specs,
            out_specs=out_specs,
            scratch_shapes=list(scratch),
        ),
        compiler_params=pltpu.CompilerParams(
            dimension_semantics=("arbitrary",), vmem_limit_bytes=VMEM_LIMIT
        ),
    )(meta, *args)


def shape(dims, dtype):
    return jax.ShapeDtypeStruct(tuple(dims), dtype)


def put_blocks(out, row, src):
    height, width = src.shape
    for j in range(width // LANES):
        out[row : row + height, :] = src[:, j * LANES : (j + 1) * LANES]
        row += height
    return row


def pack_attn_body(meta, w_qkv, a_qkv, w_out, a_out, b_qkv, b_out, out):
    row = 0
    for ref in (w_qkv, a_qkv, w_out, a_out, b_qkv, b_out):
        row = put_blocks(out, row, ref[...])


def pack_experts_body(rel_shape, meta, w_gu, a_gu, w_down, a_down, b_gu, b_down, *outs):
    for rel in range(rel_shape):
        member = meta[0] ^ rel
        row = 0
        for ref in (w_gu, a_gu, w_down, a_down, b_gu, b_down):
            row = put_blocks(outs[rel], row, ref[member])


def three_parts(v):
    high = v.astype(BF).astype(F32)
    mid = (v - high).astype(BF).astype(F32)
    return [high, mid, v - high - mid]


def put_packet(out, e, rows):
    for j in range(BLOCKS):
        out[e, j * CAP : (j + 1) * CAP, :] = rows[:, j * LANES : (j + 1) * LANES]


def packet_rows(packets):
    return lanes_cat(
        [packets[:, j * CAP : (j + 1) * CAP, :].reshape(SLOTS, LANES) for j in range(BLOCKS)]
    )


def slots_body(micros, meta, tok, cot, *refs):
    dy, (sid_row, sid_col) = refs[:micros], refs[micros:]
    strict = (iota((SEQ, SEQ), 0) < iota((SEQ, SEQ), 1)).astype(BF)
    experts = iota((FFN_EXPERTS, SEQ), 0)
    for micro in range(micros):
        turned = tok[micro].T
        route = [turned[16 + k : 17 + k, :].astype(jnp.int32) for k in range(2)]
        hot = [(experts == route[k]).astype(F32) for k in range(2)]
        before = dot((hot[0] + hot[1]).astype(BF), strict)
        sids = []
        for k in range(2):
            rank = jnp.sum(before * hot[k], axis=0, keepdims=True).astype(jnp.int32)
            sids.append(jnp.where(route[k] < FFN_EXPERTS, route[k] * CAP + rank, -1))
        rows = jnp.concatenate(sids + [jnp.zeros((6, SEQ), jnp.int32)], axis=0)
        sid_row[micro] = rows
        sid_col[micro] = rows.astype(F32).T.astype(jnp.int32)
        all_routes = iota((16, SEQ), 0)
        prev = turned[0:16, :]
        named = [
            jnp.sum(jnp.where(all_routes == route[k], prev, 0.0), axis=0, keepdims=True)
            for k in range(2)
        ]
        fields = [
            jnp.concatenate(
                three_parts(named[1 - k] - named[k])
                + [route[1 - k].astype(F32), jnp.zeros((SIDE - 4, SEQ), F32)],
                axis=0,
            ).astype(BF)
            for k in range(2)
        ]
        at = iota((FFN_EXPERTS * LANES, SEQ), 0)
        at = jnp.where(at % LANES < CAP, at // LANES * CAP + at % LANES, -2)
        hits = [(at == sids[k]).astype(F32).astype(BF) for k in range(2)]
        side = dot_nt(fields[0], hits[0]) + dot_nt(fields[1], hits[1])
        own_id = jnp.full((SIDE, LANES), 1.0, F32) * meta[micro].astype(F32)
        slot = iota((SLOTS, SEQ), 0)
        table = ((slot == sids[0]) | (slot == sids[1])).astype(F32).astype(BF)
        rows = dot(table, cot[micro, 0]).astype(BF)
        fourth = iota((SIDE, LANES), 0) == 4
        for e in range(FFN_EXPERTS):
            put_packet(dy[micro], e, rows[e * CAP : (e + 1) * CAP])
            one = jnp.where(fourth, own_id, side[:, e * LANES : (e + 1) * LANES])
            dy[micro][e, BLOCKS * CAP :, :] = one.astype(BF)


def load_wall(pieces, wall, sems, meta, first):
    copies = [
        pltpu.make_async_copy(piece, wall.at[meta[first + i]], sems.at[i])
        for i, piece in enumerate(pieces)
    ]
    for copy in copies:
        copy.start()
    return copies


class AttnWall:
    def __init__(self, wall, n_src):
        self.wall = wall
        self.n_src = n_src
        self.rows = D // n_src
        self.low = RANKS // n_src
        self.base = (QKV_BLOCKS + AQKV_BLOCKS + OUT_BLOCKS + 1) * self.rows

    def block(self, j, count=1):
        return lanes_cat(
            [
                self.wall[:, (j + i) * self.rows : (j + i + 1) * self.rows, :].reshape(D, LANES)
                for i in range(count)
            ]
        )

    def rank_block(self, j, count=1):
        return lanes_cat(
            [
                self.wall[
                    :, self.base + (j + i) * self.low : self.base + (j + i + 1) * self.low, :
                ].reshape(RANKS, LANES)
                for i in range(count)
            ]
        )

    def qkv(self, j, count=1):
        return self.block(j, count)

    def a_qkv(self, j=0, count=3):
        return self.block(QKV_BLOCKS + j, count)

    def w_out(self):
        return self.block(QKV_BLOCKS + AQKV_BLOCKS, OUT_BLOCKS)

    def a_out(self):
        return self.block(QKV_BLOCKS + AQKV_BLOCKS + OUT_BLOCKS)

    def b_qkv(self, j, count=1):
        return self.rank_block(j, count)

    def b_out(self):
        return self.rank_block(QKV_BLOCKS, OUT_BLOCKS)


def turn(v, cos, sin):
    ahead = pltpu.roll(v, LANES - HEAD // 2, axis=1)
    behind = pltpu.roll(v, HEAD // 2, axis=1)
    first = (iota(v.shape, 1) % HEAD) < HEAD // 2
    return v * cos + jnp.where(first, ahead, behind) * sin


def rank_mask(which):
    return ((iota((1, RANKS), 1) // RANK) == which).astype(F32)


def allowed_bias(meta, at):
    t = iota((SEQ, SEQ), 0)
    u = iota((SEQ, SEQ), 1)
    ok = t >= u
    for j in range(2):
        start, end = meta[at + 2 * j], meta[at + 2 * j + 1]
        ok = ok | ((t >= start) & (t < end) & (u >= start) & (u < end))
    return jnp.concatenate([ok, ok], axis=0)


def split_heads(v):
    low = (iota((1, LANES), 1) < HEAD).astype(v.dtype)
    return jnp.concatenate([v * low, v * (1 - low).astype(v.dtype)], axis=0)


def join_heads(v):
    low = iota((SEQ, LANES), 1) < HEAD
    return jnp.where(low, v[:SEQ], v[SEQ:])


def attn_forward_body(
    micro, n_src, meta, hid, cos_ref, sin_ref, gain_a, gain_m, sid_row, *refs
):
    pieces = refs[:n_src]
    qkv, attended, ranks, resid, lse, send, wall_ref, sems = refs[n_src:]
    copies = load_wall(pieces, wall_ref, sems, meta, 0)
    wall = AttnWall(wall_ref, n_src)
    at_id = n_src + 1 + micro
    at_span = n_src + 3 + 4 * micro
    hidden = hid[0, 0].astype(F32)
    scale = lax.rsqrt(jnp.mean(hidden * hidden, axis=-1, keepdims=True) + EPS)
    normed = (hidden * scale * gain_a[...]).astype(BF)
    mask = rank_mask(meta[at_id])
    ok = allowed_bias(meta, at_span)
    cos, sin = cos_ref[...], sin_ref[...]
    for copy in copies:
        copy.wait()
    proj = dot(normed, wall.a_qkv())
    ranks_in = [(proj[:, j * RANKS : (j + 1) * RANKS] * mask).astype(BF) for j in range(3)]
    for j in range(3):
        ranks[:, j * RANKS : (j + 1) * RANKS] = ranks_in[j]
    for j in range(3):
        for pair in range(3):
            at = j * 6 + pair * 2
            part = dot(normed, wall.qkv(at, 2)) + dot(ranks_in[j], wall.b_qkv(at, 2))
            for half in range(2):
                one = part[:, half * LANES : (half + 1) * LANES]
                if j < 2:
                    one = turn(one, cos, sin)
                qkv[:, (at + half) * LANES : (at + half + 1) * LANES] = one.astype(BF)
    lse_cols = []
    for pair in range(6):
        query = qkv[:, pair * LANES : (pair + 1) * LANES]
        key = qkv[:, (6 + pair) * LANES : (7 + pair) * LANES]
        value = qkv[:, (12 + pair) * LANES : (13 + pair) * LANES]
        scores = jnp.where(ok, dot_nt(split_heads(query), key) * (1.0 / math.sqrt(HEAD)), NEG)
        top = jnp.max(scores, axis=-1, keepdims=True)
        expo = jnp.exp(scores - top)
        total = jnp.sum(expo, axis=-1, keepdims=True)
        probs = (expo * (1.0 / total)).astype(BF)
        attended[:, pair * LANES : (pair + 1) * LANES] = join_heads(dot(probs, value)).astype(BF)
        logs = top + jnp.log(total)
        lse[:, pair : pair + 1] = logs
    mixed = attended[...]
    ranks_out = (dot(mixed, wall.a_out()) * mask).astype(BF)
    ranks[:, 3 * RANKS :] = ranks_out
    out = hidden + dot(mixed, wall.w_out()) + dot(ranks_out, wall.b_out())
    resid[...] = out
    scale_m = lax.rsqrt(jnp.mean(out * out, axis=-1, keepdims=True) + EPS)
    lowered = (out * scale_m * gain_m[...]).astype(BF)
    sids = sid_row[0]
    at = iota((SLOTS, SEQ), 0)
    table = ((at == sids[0:1, :]) | (at == sids[1:2, :])).astype(F32).astype(BF)
    send[...] = dot(table, lowered).astype(BF).reshape(FFN_EXPERTS, CAP, D)


class ExpertWall:
    def __init__(self, wall, n_src):
        self.wall = wall
        self.n_src = n_src
        self.rows = D // n_src
        self.ff = FF // n_src
        self.low = RANKS // n_src
        self.down_at = (GU_BLOCKS + AGU_BLOCKS) * self.rows
        self.rank_at = self.down_at + (DOWN_BLOCKS + 1) * self.ff

    def block(self, j):
        start = j * self.rows
        if not isinstance(j, int):
            start = pl.multiple_of(start, self.rows)
        return self.wall[:, pl.ds(start, self.rows), :].reshape(D, LANES)

    def gate_up(self, j, count):
        return lanes_cat([self.block(j + i) for i in range(count)])

    def a_gate_up(self):
        return lanes_cat([self.block(GU_BLOCKS + i) for i in range(AGU_BLOCKS)])

    def rank_block(self, j):
        start = self.rank_at + j * self.low
        if not isinstance(j, int):
            start = pl.multiple_of(start, self.low)
        return self.wall[:, pl.ds(start, self.low), :].reshape(RANKS, LANES)

    def b_gate_up(self, j, count):
        return lanes_cat([self.rank_block(j + i) for i in range(count)])

    def b_down(self):
        return lanes_cat([self.rank_block(GU_BLOCKS + i) for i in range(DOWN_BLOCKS)])

    def down(self, src, count):
        return lanes_cat(
            [
                self.wall[
                    pl.ds(src, count), self.down_at + i * self.ff : self.down_at + (i + 1) * self.ff, :
                ].reshape(count * self.ff, LANES)
                for i in range(DOWN_BLOCKS)
            ]
        )

    def a_down(self, src, count):
        start = self.down_at + DOWN_BLOCKS * self.ff
        return self.wall[pl.ds(src, count), start : start + self.ff, :].reshape(
            count * self.ff, LANES
        )


CHUNK = 512


def expert_body(n_src, carried, meta, tin, dyp, route_w, *refs):
    if carried:
        before, refs = refs[0], refs[1:]
    pieces = refs[:n_src]
    fo, dtin, grads, wall_ref, sems, fo_acc, dt_acc, pd_acc, dug_acc = refs[n_src:]
    copies = load_wall(pieces, wall_ref, sems, meta, 0)
    wall = ExpertWall(wall_ref, n_src)
    own = meta[n_src]
    tokens = tin[...].reshape(SLOTS, D)
    cot = packet_rows(dyp).astype(F32)
    cols = jnp.concatenate(
        [dyp[s, BLOCKS * CAP :, :].astype(F32).T[:CAP] for s in range(FFN_EXPERTS)], axis=0
    )
    logits = exact_dot(tokens.astype(F32), route_w[...])
    lane = iota((SLOTS, LANES), 1)
    gap = jnp.sum(
        jnp.where(lane == own, logits, 0.0)
        - jnp.where(lane == cols[:, 3:4].astype(jnp.int32), logits, 0.0),
        axis=1,
        keepdims=True,
    )
    gate = sigmoid(gap - (cols[:, 0:1] + cols[:, 1:2] + cols[:, 2:3]))
    mask = ((lane // RANK) == cols[:, 4:5].astype(jnp.int32)).astype(F32)
    d_out = (cot * gate).astype(BF)
    for copy in copies:
        copy.wait()

    a_gu = wall.a_gate_up()
    proj = dot(tokens, a_gu)
    ranks_in = [(proj[:, j * RANKS : (j + 1) * RANKS] * mask).astype(BF) for j in range(2)]
    d_ranks_down = (dot_nt(d_out, wall.b_down()) * mask).astype(BF)
    fo_acc[...] = jnp.zeros_like(fo_acc)
    dt_acc[...] = jnp.zeros_like(dt_acc)
    pd_acc[...] = jnp.zeros_like(pd_acc)
    dug_acc[...] = jnp.zeros_like(dug_acc)
    blocks = CHUNK // LANES
    srcs = max(1, CHUNK // wall.ff)
    gb_at = AGU_BLOCKS * wall.rows
    ad_at = gb_at + GU_BLOCKS * wall.low
    bd_at = ad_at + wall.ff

    def step(f, carry):
        j = f * blocks
        wg = wall.gate_up(j, blocks)
        wu = wall.gate_up(j + GU_BLOCKS // 2, blocks)
        bg = wall.b_gate_up(j, blocks)
        bu = wall.b_gate_up(j + GU_BLOCKS // 2, blocks)
        wd = wall.down(f * srcs, srcs)
        ad = wall.a_down(f * srcs, srcs)
        g = dot(tokens, wg) + dot(ranks_in[0], bg)
        u = dot(tokens, wu) + dot(ranks_in[1], bu)
        d_hidden = dot_nt(d_out, wd) + dot_nt(d_ranks_down, ad)
        sg = sigmoid(g)
        act = g * sg
        hidden = (act * u).astype(BF)
        d_gate = (d_hidden * u * (sg * (1.0 + g * (1.0 - sg)))).astype(BF)
        d_up = (d_hidden * act).astype(BF)
        fo_acc[...] += dot(hidden, wd)
        pd_acc[...] += dot(hidden, ad)
        dt_acc[...] += dot_nt(d_gate, wg) + dot_nt(d_up, wu)
        dug_acc[:, :RANKS] += dot_nt(d_gate, bg)
        dug_acc[:, RANKS:] += dot_nt(d_up, bu)
        for k, (rank, grad) in enumerate(((ranks_in[0], d_gate), (ranks_in[1], d_up))):
            part = dot_tn(rank, grad)
            for i in range(blocks):
                at = gb_at + (j + k * (GU_BLOCKS // 2) + i) * wall.low
                rows = pl.ds(at if isinstance(at, int) else pl.multiple_of(at, 8), wall.low)
                one = part[:, i * LANES : (i + 1) * LANES].reshape(n_src, wall.low, LANES)
                grads[:, rows, :] = one
        part = dot_tn(hidden, d_ranks_down).reshape(srcs, wall.ff, LANES)
        grads[pl.ds(f * srcs, srcs), ad_at : ad_at + wall.ff, :] = part
        return carry

    if wall.low % 8:
        for f in range(FF // CHUNK):
            step(f, 0)
    else:
        lax.fori_loop(0, FF // CHUNK, step, 0)
    ranks_down = (pd_acc[...] * mask).astype(BF)
    result = (fo_acc[...] + dot(ranks_down, wall.b_down())).astype(BF)
    along = jnp.sum(cot * result.astype(F32), axis=1, keepdims=True)
    parts = three_parts(along)
    along = jnp.where(lane == 0, parts[0], jnp.where(lane == 1, parts[1], 0.0))
    along = jnp.where(lane == 2, parts[2], along).astype(BF)
    eye = (iota((CAP, LANES), 0) == iota((CAP, LANES), 1)).astype(F32).astype(BF)
    fo[...] = result.reshape(FFN_EXPERTS, CAP, D)
    for r in range(FFN_EXPERTS):
        side = dot_tn(along[r * CAP : (r + 1) * CAP], eye)[:SIDE]
        dtin[r, BLOCKS * CAP :, :] = side.astype(BF)
    part = dot_tn(ranks_down, d_out)
    for i in range(DOWN_BLOCKS):
        grads[:, bd_at + i * wall.low : bd_at + (i + 1) * wall.low, :] = part[
            :, i * LANES : (i + 1) * LANES
        ].reshape(n_src, wall.low, LANES)
    d_ranks = [(dug_acc[:, k * RANKS : (k + 1) * RANKS] * mask).astype(BF) for k in range(2)]
    both = lanes_cat(d_ranks)
    d_tokens = (dt_acc[...] + dot_nt(both, a_gu)).astype(BF)
    for r in range(FFN_EXPERTS):
        put_packet(dtin, r, d_tokens[r * CAP : (r + 1) * CAP])
    part = dot_tn(tokens, both)
    for i in range(AGU_BLOCKS):
        grads[:, i * wall.rows : (i + 1) * wall.rows, :] = part[
            :, i * LANES : (i + 1) * LANES
        ].reshape(n_src, wall.rows, LANES)
    if carried:
        grads[...] = grads[...] + before[...]


def attn_backward_body(micro, n_src, carried, meta, hid, cot, resid_ref, qkv, attended, ranks, lse,
                       dtin, tok, sid_col, gain_a, gain_m, route_w, consts, cos_ref, sin_ref,
                       *refs):
    if carried:
        before, refs = refs[0], refs[1:]
    pieces = refs[:n_src]
    base, gates, grad_in, grads, wall_ref, sems, dqkv = refs[n_src:]
    copies = load_wall(pieces, wall_ref, sems, meta, 0)
    wall = AttnWall(wall_ref, n_src)
    at_id = n_src + 1 + micro
    at_span = n_src + 3 + 4 * micro
    mask = rank_mask(meta[at_id])
    resid = resid_ref[...]
    dy = cot[0, 0].astype(F32)
    scale_m = lax.rsqrt(jnp.mean(resid * resid, axis=-1, keepdims=True) + EPS)
    gain = gain_m[...]
    normed = resid * scale_m * gain
    lowered = normed.astype(BF).astype(F32)
    weights = route_w[...]
    scores = exact_dot(lowered, weights)
    token = tok[0]
    lane = iota((SEQ, LANES), 1)
    route = [token[:, 16 + k : 17 + k].astype(jnp.int32) for k in range(2)]
    logits = scores + token
    chosen = [
        jnp.sum(jnp.where(lane == route[k], logits, 0.0), axis=1, keepdims=True) for k in range(2)
    ]
    gate = [sigmoid(chosen[k] - chosen[1 - k]) for k in range(2)]
    keep = [sigmoid(scores[:, 12 + j : 13 + j]) for j in range(2)]
    slot = iota((SEQ, SLOTS), 1)
    hits = [(slot == sid_col[0][:, k : k + 1]).astype(F32).astype(BF) for k in range(2)]
    spread = iota((SEQ, FFN_EXPERTS * LANES), 1)
    spread = jnp.where(spread % LANES < CAP, spread // LANES * CAP + spread % LANES, -2)
    side = lanes_cat([dtin[e, BLOCKS * CAP :, :] for e in range(FFN_EXPERTS)])
    along = []
    for k in range(2):
        found = (spread == sid_col[0][:, k : k + 1]).astype(F32).astype(BF)
        parts = dot_nt(found, side)
        along.append(parts[:, 0:1] + parts[:, 1:2] + parts[:, 2:3])
    value = [consts[j : j + 1, :] for j in range(2)]
    is_copy = [(route[k] == FFN_EXPERTS + 1).astype(F32) for k in range(2)]
    is_const = [
        [(route[k] == FFN_EXPERTS + 2 + j).astype(F32) for j in range(2)] for k in range(2)
    ]
    share = sum(
        gate[k] * (is_copy[k] + is_const[k][0] * keep[0] + is_const[k][1] * keep[1])
        for k in range(2)
    )
    named = [gate[0] * is_const[0][j] + gate[1] * is_const[1][j] for j in range(2)]
    out = resid + share * normed
    out = out + (named[0] * (1.0 - keep[0])) * value[0] + (named[1] * (1.0 - keep[1])) * value[1]
    base[...] = out
    gates[...] = jnp.where(lane == 0, gate[0], jnp.where(lane == 1, gate[1], 0.0))
    dy_normed = jnp.sum(dy * normed, axis=1, keepdims=True)
    dy_value = [jnp.sum(dy * value[j], axis=1, keepdims=True) for j in range(2)]
    d_gate = []
    for k in range(2):
        one = along[k] + is_copy[k] * dy_normed
        for j in range(2):
            one = one + is_const[k][j] * (keep[j] * dy_normed + (1.0 - keep[j]) * dy_value[j])
        d_gate.append(one)
    centre = gate[0] * d_gate[0] + gate[1] * d_gate[1]
    d_logits = jnp.zeros((SEQ, LANES), F32)
    for k in range(2):
        d_logits = d_logits + jnp.where(lane == route[k], gate[k] * (d_gate[k] - centre), 0.0)
    for j in range(2):
        d_keep = named[j] * (dy_normed - dy_value[j])
        d_logits = d_logits + jnp.where(
            lane == 12 + j, d_keep * keep[j] * (1.0 - keep[j]), 0.0
        )
    d_normed = share * dy + exact_dot_nt(d_logits, weights)
    d_normed = d_normed + dot(hits[0] + hits[1], packet_rows(dtin))
    scaled = gain * d_normed
    d_resid = (
        dy
        + scale_m * scaled
        - resid * (scale_m * scale_m * scale_m) * jnp.mean(scaled * resid, axis=-1, keepdims=True)
    )
    d_branch = d_resid.astype(BF)
    for copy in copies:
        copy.wait()
    d_ranks_out = (dot_nt(d_branch, wall.b_out()) * mask).astype(BF)
    d_mixed = (dot_nt(d_branch, wall.w_out()) + dot_nt(d_ranks_out, wall.a_out())).astype(BF)
    a_rows, b_rows = wall.rows, wall.low
    gb_at = AQKV_BLOCKS * a_rows
    ao_at = gb_at + QKV_BLOCKS * b_rows
    bo_at = ao_at + a_rows
    part = dot_tn(ranks[:, 3 * RANKS :], d_branch)
    for i in range(OUT_BLOCKS):
        grads[:, bo_at + i * b_rows : bo_at + (i + 1) * b_rows, :] = part[
            :, i * LANES : (i + 1) * LANES
        ].reshape(n_src, b_rows, LANES)
    grads[:, ao_at : ao_at + a_rows, :] = dot_tn(attended[...], d_ranks_out).reshape(
        n_src, a_rows, LANES
    )
    ok = allowed_bias(meta, at_span)
    cos, sin = cos_ref[...], -sin_ref[...]
    inv = 1.0 / math.sqrt(HEAD)
    for pair in range(6):
        query = split_heads(qkv[:, pair * LANES : (pair + 1) * LANES])
        key = qkv[:, (6 + pair) * LANES : (7 + pair) * LANES]
        val = qkv[:, (12 + pair) * LANES : (13 + pair) * LANES]
        d_heads = split_heads(d_mixed[:, pair * LANES : (pair + 1) * LANES])
        sc = jnp.where(ok, dot_nt(query, key) * inv, NEG)
        probs = jnp.exp(sc - lse[:, pair : pair + 1])
        d_probs = dot_nt(d_heads, val)
        row_dot = jnp.sum(probs * d_probs, axis=-1, keepdims=True)
        d_scores = (probs * (d_probs - row_dot)).astype(BF)
        d_query = join_heads(dot(d_scores, key)) * inv
        d_key = dot_tn(d_scores, query) * inv
        d_value = dot_tn(probs.astype(BF), d_heads)
        dqkv[:, pair * LANES : (pair + 1) * LANES] = turn(d_query, cos, sin).astype(BF)
        dqkv[:, (6 + pair) * LANES : (7 + pair) * LANES] = turn(d_key, cos, sin).astype(BF)
        dqkv[:, (12 + pair) * LANES : (13 + pair) * LANES] = d_value.astype(BF)
    hidden = hid[0, 0].astype(F32)
    scale = lax.rsqrt(jnp.mean(hidden * hidden, axis=-1, keepdims=True) + EPS)
    first = gain_a[...]
    normed_low = (hidden * scale * first).astype(BF)
    d_in = jnp.zeros((SEQ, D), F32)
    d_ranks = []
    for j in range(3):
        part = dqkv[:, j * D : (j + 1) * D]
        d_ranks.append((dot_nt(part, wall.b_qkv(j * 6, 6)) * mask).astype(BF))
        d_in = d_in + dot_nt(part, wall.qkv(j * 6, 6))
        gb = dot_tn(ranks[:, j * RANKS : (j + 1) * RANKS], part)
        for i in range(6):
            at = gb_at + (j * 6 + i) * b_rows
            grads[:, at : at + b_rows, :] = gb[:, i * LANES : (i + 1) * LANES].reshape(
                n_src, b_rows, LANES
            )
    ranks_all = lanes_cat(d_ranks)
    d_in = d_in + dot_nt(ranks_all, wall.a_qkv())
    ga = dot_tn(normed_low, ranks_all)
    for i in range(3):
        grads[:, i * a_rows : (i + 1) * a_rows, :] = ga[:, i * LANES : (i + 1) * LANES].reshape(
            n_src, a_rows, LANES
        )
    scaled = first * d_in
    grad_in[...] = (
        d_resid
        + scale * scaled
        - hidden * (scale * scale * scale) * jnp.mean(scaled * hidden, axis=-1, keepdims=True)
    )
    if carried:
        grads[...] = grads[...] + before[...]


def output_body(meta, base, gates, sid_col, fo, out):
    arrived = fo[...].reshape(SLOTS, D)
    slot = iota((SEQ, SLOTS), 1)
    total = base[...]
    for k in range(2):
        hits = (slot == sid_col[0][:, k : k + 1]).astype(F32).astype(BF)
        total = total + gates[:, k : k + 1] * dot(hits, arrived)
    out[...] = total.astype(BF)


def flip(values, axis, bit, size):
    return lax.ppermute(values, axis, [(i, i ^ bit) for i in range(size)])


def later(values, others):
    return lax.optimization_barrier((values, others))[0]


def bits(size):
    return [1 << i for i in range(size.bit_length() - 1)]


def halve_sum(values, axis, size):
    place = lax.axis_index(axis)
    for bit in reversed(bits(size)):
        pair = values.reshape((2, values.shape[0] // 2) + values.shape[1:])
        side = (place // bit) % 2
        away = lax.dynamic_index_in_dim(pair, 1 - side, 0, keepdims=False).astype(BF)
        kept = lax.dynamic_index_in_dim(pair, side, 0, keepdims=False)
        values = kept + flip(away, axis, bit, size).astype(F32)
    return values


def body(members, hidden_in, prev_logits, routes, adapter_ids, image_spans, cotangent, gain_attn,
         gain_moe, router_weight, const_gate, const_value, w_qkv, w_out, a_qkv, b_qkv, a_out, b_out,
         w_gate_up, w_down, a_gate_up, b_gate_up, a_down, b_down):
    rest = lax.axis_size("y")
    peers = lax.axis_size("z")
    n_src = rest * members * 2
    micros = hidden_in.shape[0]
    y, x, c, z = (lax.axis_index(name) for name in ("y", "x", "c", "z"))
    place = (y * members + x) * 2 + c

    attn_rows = (QKV_BLOCKS + AQKV_BLOCKS + OUT_BLOCKS + 1) * (D // n_src) + (
        QKV_BLOCKS + OUT_BLOCKS
    ) * (RANKS // n_src)
    expert_rows = (
        (GU_BLOCKS + AGU_BLOCKS) * (D // n_src)
        + (DOWN_BLOCKS + 1) * (FF // n_src)
        + (GU_BLOCKS + DOWN_BLOCKS) * (RANKS // n_src)
    )
    none = jnp.zeros((1,), jnp.int32)
    args = (w_qkv, a_qkv, w_out, a_out, b_qkv, b_out)
    (attn_own,) = call(
        pack_attn_body,
        none,
        args,
        [whole(a.shape) for a in args],
        [shape((attn_rows, LANES), BF)],
        us=2,
    )
    args = (w_gate_up, a_gate_up, w_down, a_down, b_gate_up, b_down)
    expert_own = call(
        functools.partial(pack_experts_body, members),
        x.reshape(1).astype(jnp.int32),
        args,
        [whole(a.shape) for a in args],
        [shape((expert_rows, LANES), BF)] * members,
        us=4,
        after=(attn_own,),
    )

    tok = jnp.concatenate(
        [
            prev_logits[:, 0],
            jnp.zeros((micros, SEQ, 4), F32),
            routes[:, 0].astype(F32),
            jnp.zeros((micros, SEQ, LANES - 18), F32),
        ],
        axis=2,
    )
    route_w = jnp.concatenate(
        [router_weight, const_gate, jnp.zeros((D, LANES - 14), F32)], axis=1
    )
    half = HEAD // 2
    freqs = jnp.exp(jnp.arange(half, dtype=F32) * (-2.0 * math.log(10000.0) / HEAD))
    angles = jnp.arange(SEQ, dtype=F32)[:, None] * freqs[None, :]
    cos = jnp.tile(jnp.cos(angles), (1, 4))
    sin = jnp.sin(angles)
    sin = jnp.tile(jnp.concatenate([-sin, sin], axis=1), (1, 2))
    gain_a = gain_attn.reshape(1, D)
    gain_m = gain_moe.reshape(1, D)

    packet = shape((FFN_EXPERTS, CAP, D), BF)
    wide_packet = shape((FFN_EXPERTS, BLOCKS * CAP + SIDE, LANES), BF)
    *dy_send, sid_row, sid_col = call(
        functools.partial(slots_body, micros),
        adapter_ids.reshape(-1),
        (tok, cotangent),
        [whole(tok.shape), whole(cotangent.shape)],
        [wide_packet] * micros
        + [shape((micros, 8, SEQ), jnp.int32), shape((micros, SEQ, 8), jnp.int32)],
        us=4,
        after=(expert_own[0],),
    )

    attn_pieces = [(attn_own, 0)]
    for bit in bits(members):
        attn_pieces += [(flip(v, "x", bit, members), m ^ (bit * 2)) for v, m in attn_pieces]
    for bit in bits(rest):
        way = bit * members * 2
        beside = flip(attn_own, "y", bit, rest)
        attn_pieces += [(beside, way)] + [
            (flip(later(v, (sid_row, beside)), "y", bit, rest), m ^ way)
            for v, m in attn_pieces[1:]
        ]
    attn_near, attn_far = attn_pieces[1][0], attn_pieces[-1][0]
    attn_pieces += [
        (flip(v if v is attn_far else later(v, attn_far), "c", 1, 2), m ^ 1)
        for v, m in attn_pieces
    ]
    attn_bufs = [v for v, m in attn_pieces]
    meta_attn = jnp.concatenate(
        [
            place ^ jnp.array([m for v, m in attn_pieces], jnp.int32),
            jnp.zeros((1,), jnp.int32),
            adapter_ids.reshape(-1),
            image_spans.reshape(-1),
        ]
    ).astype(jnp.int32)

    group = ("z", "x") if members > 1 else "z"

    def trade(values):
        return lax.all_to_all(values, group, 0, 0, tiled=True)

    expert_pieces = [(expert_own[0], 0)]
    for rel in range(1, members):
        pairs = [(i, i ^ rel) for i in range(members)]
        away = later(expert_own[rel], attn_near)
        expert_pieces.append((lax.ppermute(away, "x", pairs), rel * 2))
    first = bits(rest)[0]
    own = later(expert_own[0], attn_far)
    beside = (flip(own, "y", first, rest), first * members * 2)
    near = [[v for v, m in expert_pieces[1:]] + [beside[0]]]

    saved, tin, dy_got = [], [], []
    for micro in range(micros):
        args = (hidden_in, cos, sin, gain_a, gain_m, sid_row, *attn_bufs)
        specs = [
            one_micro((1, SEQ, D), micro),
            whole(cos.shape),
            whole(sin.shape),
            whole(gain_a.shape),
            whole(gain_m.shape),
            one_micro((8, SEQ), micro),
        ] + [ANYWHERE] * n_src
        saved.append(
            call(
                functools.partial(attn_forward_body, micro, n_src),
                meta_attn,
                args,
                specs,
                [
                    shape((SEQ, 3 * D), BF),
                    shape((SEQ, D), BF),
                    shape((SEQ, 4 * RANKS), BF),
                    shape((SEQ, D), F32),
                    shape((2 * SEQ, 8), F32),
                    packet,
                ],
                [
                    pltpu.VMEM((n_src, attn_rows, LANES), BF),
                    pltpu.SemaphoreType.DMA((n_src,)),
                ],
                us=FORWARD_HINT,
                after=tuple(near[micro]) if micro < len(near) else (),
            )
        )
        if micro == 0:
            for bit in bits(rest):
                relay = expert_pieces[1:] if bit == first else expert_pieces
                more = [
                    (flip(later(v, saved[0][4]), "y", bit, rest), m ^ (bit * members * 2))
                    for v, m in relay
                ]
                expert_pieces += ([beside] if bit == first else []) + more
        dy_got.append(trade(dy_send[micro]))
        send = saved[micro][5]
        tin.append(trade(send if micro == 0 else later(send, expert_pieces[-1][0])))
    expert_pieces += [
        (flip(later(v, saved[-1][4]), "c", 1, 2), m ^ 1) for v, m in expert_pieces
    ]
    expert_bufs = [v for v, m in expert_pieces]
    meta_expert = jnp.concatenate(
        [
            place ^ jnp.array([m for v, m in expert_pieces], jnp.int32),
            (z * members + x).reshape(1),
        ]
    ).astype(jnp.int32)

    expert_grad_rows = (
        AGU_BLOCKS * (D // n_src)
        + (GU_BLOCKS + DOWN_BLOCKS) * (RANKS // n_src)
        + FF // n_src
    )
    grads_e = None
    fo_send, dtin = [], []
    for micro in range(micros):
        carried = grads_e is not None
        args = (tin[micro], dy_got[micro], route_w)
        if carried:
            args += (grads_e,)
        specs = [whole(a.shape) for a in args] + [ANYWHERE] * n_src
        fo, d_tokens, grads_e = call(
            functools.partial(expert_body, n_src, carried),
            meta_expert,
            args + tuple(expert_bufs),
            specs,
            [packet, wide_packet, shape((n_src, expert_grad_rows, LANES), F32)],
            [
                pltpu.VMEM((n_src, expert_rows, LANES), BF),
                pltpu.SemaphoreType.DMA((n_src,)),
                pltpu.VMEM((SLOTS, D), F32),
                pltpu.VMEM((SLOTS, D), F32),
                pltpu.VMEM((SLOTS, RANKS), F32),
                pltpu.VMEM((SLOTS, 2 * RANKS), F32),
            ],
            us=31,
        )
        fo_send.append(fo)
        dtin.append(trade(d_tokens))

    total = grads_e.reshape((rest, members, 2) + grads_e.shape[1:])
    half_e = halve_sum(jnp.moveaxis(total, 2, 0), "c", 2)

    attn_grad_rows = (AQKV_BLOCKS + 1) * (D // n_src) + (QKV_BLOCKS + OUT_BLOCKS) * (
        RANKS // n_src
    )
    grads_a = None
    block_rows, grad_rows = [], []
    for micro in range(micros):
        carried = grads_a is not None
        qkv, attended, ranks, resid, lse = saved[micro][:5]
        args = (hidden_in, cotangent, resid, qkv, attended, ranks, lse, dtin[micro], tok, sid_col,
                gain_a, gain_m, route_w, const_value, cos, sin)
        specs = [whole(a.shape) for a in args]
        specs[0] = one_micro((1, SEQ, D), micro)
        specs[1] = one_micro((1, SEQ, D), micro)
        specs[8] = one_micro((SEQ, LANES), micro)
        specs[9] = one_micro((SEQ, 8), micro)
        if carried:
            args += (grads_a,)
            specs.append(whole(grads_a.shape))
        specs += [ANYWHERE] * n_src
        base, gates, grad_in, grads_a = call(
            functools.partial(attn_backward_body, micro, n_src, carried),
            meta_attn,
            args + tuple(attn_bufs),
            specs,
            [
                shape((SEQ, D), F32),
                shape((SEQ, LANES), F32),
                shape((SEQ, D), F32),
                shape((n_src, attn_grad_rows, LANES), F32),
            ],
            [
                pltpu.VMEM((n_src, attn_rows, LANES), BF),
                pltpu.SemaphoreType.DMA((n_src,)),
                pltpu.VMEM((SEQ, 3 * D), BF),
            ],
            us=19,
            after=(half_e,) if carried else (),
        )
        grad_rows.append(grad_in)
        fo = trade(later(fo_send[micro], base))
        if not carried:
            half_e = later(half_e, base)
            total = half_e.reshape((rest, members) + grads_e.shape[1:])
            total = halve_sum(total, "y", rest).reshape((members,) + grads_e.shape[1:])
            held = (fo, total)
        (block_out,) = call(
            output_body,
            none,
            (base, gates, sid_col, fo),
            [whole(base.shape), whole(gates.shape), one_micro((SEQ, 8), micro), whole(fo.shape)],
            [shape((SEQ, D), BF)],
            us=3,
        )
        block_rows.append(block_out)
    owned = lax.dynamic_index_in_dim(total, x, 0, keepdims=True)
    for rel in range(1, members):
        away = lax.dynamic_index_in_dim(total, x ^ rel, 0, keepdims=True).astype(BF)
        got = lax.ppermute(away, "x", [(i, i ^ rel) for i in range(members)])
        owned = jnp.concatenate([owned, got.astype(F32)], axis=0)
    if members > 1:
        owned = owned[x ^ jnp.arange(members)]

    def blocks_of(values, row, count, height):
        part = values[:, row : row + count * height].reshape(-1, count, height, LANES)
        return jnp.moveaxis(part, 1, 2).reshape(-1, height, count * LANES)

    rows, low, ff = D // n_src, RANKS // n_src, FF // n_src
    at = 0
    grad_agu = blocks_of(owned, at, AGU_BLOCKS, rows)
    at += AGU_BLOCKS * rows
    grad_bgu = blocks_of(owned, at, GU_BLOCKS, low)
    at += GU_BLOCKS * low
    grad_ad = blocks_of(owned, at, 1, ff)
    at += ff
    grad_bd = blocks_of(owned, at, DOWN_BLOCKS, low)

    total = grads_a.reshape((rest, members, 2) + grads_a.shape[1:])
    total = halve_sum(jnp.moveaxis(total, 2, 0), "c", 2)
    if micros > 1:
        total = later(total, held)
    total = total.reshape((rest, members) + grads_a.shape[1:])
    total = halve_sum(total, "y", rest).reshape((members,) + grads_a.shape[1:])
    total = halve_sum(total, "x", members).reshape((1,) + grads_a.shape[1:])
    for bit in bits(peers):
        sent = total.astype(BF)
        total = sent.astype(F32) + flip(sent, "z", bit, peers).astype(F32)
    at = 0
    grad_aq = blocks_of(total, at, AQKV_BLOCKS, rows)[0]
    at += AQKV_BLOCKS * rows
    grad_bq = blocks_of(total, at, QKV_BLOCKS, low)[0]
    at += QKV_BLOCKS * low
    grad_ao = blocks_of(total, at, 1, rows)[0]
    at += rows
    grad_bo = blocks_of(total, at, OUT_BLOCKS, low)[0]

    return (jnp.stack(block_rows)[:, None], jnp.stack(grad_rows)[:, None], grad_aq, grad_bq,
            grad_ao, grad_bo, grad_agu, grad_bgu, grad_ad, grad_bd)


def solution(mesh):
    dp, expert = mesh.shape["dp"], mesh.shape["expert"]
    members = FFN_EXPERTS // expert
    fine = Mesh(
        mesh.devices.reshape(dp // (2 * members), members, 2, expert), ("y", "x", "c", "z")
    )
    owners = ("y", "x", "c")
    seqs = ("y", "x", "c", "z")
    tokens = P(None, seqs, None, None)
    rows = P(owners, None)
    expert_rows = P("z", owners, None)
    in_specs = (
        (tokens, tokens, tokens, P(None, seqs), tokens, tokens)
        + (P(),) * 5
        + (rows,) * 6
        + (expert_rows,) * 6
    )
    out_specs = (tokens, tokens) + (rows,) * 4 + (expert_rows,) * 4
    return jax.shard_map(
        functools.partial(body, members),
        mesh=fine,
        in_specs=in_specs,
        out_specs=out_specs,
        check_vma=False,
    )
```

```python
import functools
import math

import jax
import jax.numpy as jnp
from jax import lax
from jax.experimental import pallas as pl
from jax.experimental.pallas import tpu as pltpu
from jax.sharding import Mesh
from jax.sharding import PartitionSpec as P

D = 768
HEADS = 12
HEAD = 64
FF = 2048
FFN_EXPERTS = 8
RANK = 16
RANKS = 128
CAP = 80
LANES = 128
SEQ = 256
SLOTS = FFN_EXPERTS * CAP
BLOCKS, SIDE = D // LANES, 8
WIDE = BLOCKS * CAP + SIDE
NEG = -1e30
EPS = 1e-05
BF = jnp.bfloat16
F32 = jnp.float32
VMEM_LIMIT = 60 * 1024 * 1024
FLOPS_PER_US, BYTES_PER_US = 10**9, 10**6
FORWARD_HINT = 12

QKV_BLOCKS, AQKV_BLOCKS, OUT_BLOCKS = 18, 3, 6
GU_BLOCKS, AGU_BLOCKS, DOWN_BLOCKS = 32, 2, 6


def dot(a, b):
    return lax.dot_general(a, b, (((1,), (0,)), ((), ())), preferred_element_type=F32)


def dot_nt(a, b):
    return lax.dot_general(a, b, (((1,), (1,)), ((), ())), preferred_element_type=F32)


def dot_tn(a, b):
    return lax.dot_general(a, b, (((0,), (0,)), ((), ())), preferred_element_type=F32)


def exact_dot(a, b):
    return lax.dot_general(
        a, b, (((1,), (0,)), ((), ())), precision=lax.Precision.HIGHEST, preferred_element_type=F32
    )


def exact_dot_nt(a, b):
    return lax.dot_general(
        a, b, (((1,), (1,)), ((), ())), precision=lax.Precision.HIGHEST, preferred_element_type=F32
    )


def lanes_cat(parts):
    return parts[0] if len(parts) == 1 else jnp.concatenate(parts, axis=1)


def iota(shape, dim):
    return lax.broadcasted_iota(jnp.int32, shape, dim)


def sigmoid(v):
    return 1.0 / (1.0 + jnp.exp(-v))


def whole(shape):
    return pl.BlockSpec(tuple(shape), lambda i, meta: (0,) * len(shape))


def one_micro(shape, micro):
    return pl.BlockSpec((1,) + tuple(shape), lambda i, meta: (micro,) + (0,) * len(shape))


ANYWHERE = pl.BlockSpec(memory_space=pl.ANY)


def call(body, meta, args, specs, outs, scratch=(), us=1, after=()):
    out_specs = [whole(o.shape) for o in outs]

    def late(meta_ref, *refs):
        body(meta_ref, *refs[len(after) :])

    args = tuple(after) + tuple(args)
    specs = [ANYWHERE] * len(after) + list(specs)
    return pl.pallas_call(
        late if after else body,
        out_shape=outs,
        cost_estimate=pl.CostEstimate(
            flops=us * FLOPS_PER_US, transcendentals=0, bytes_accessed=us * BYTES_PER_US
        ),
        grid_spec=pltpu.PrefetchScalarGridSpec(
            num_scalar_prefetch=1,
            grid=(1,),
            in_specs=specs,
            out_specs=out_specs,
            scratch_shapes=list(scratch),
        ),
        compiler_params=pltpu.CompilerParams(
            dimension_semantics=("arbitrary",), vmem_limit_bytes=VMEM_LIMIT
        ),
    )(meta, *args)


def shape(dims, dtype):
    return jax.ShapeDtypeStruct(tuple(dims), dtype)


def put_blocks(out, row, src):
    height, width = src.shape
    for j in range(width // LANES):
        out[row : row + height, :] = src[:, j * LANES : (j + 1) * LANES]
        row += height
    return row


def pack_attn_body(meta, w_qkv, a_qkv, w_out, a_out, b_qkv, b_out, out):
    row = 0
    for ref in (w_qkv, a_qkv, w_out, a_out, b_qkv, b_out):
        row = put_blocks(out, row, ref[...])


def pack_experts_body(rel_shape, meta, w_gu, a_gu, w_down, a_down, b_gu, b_down, *outs):
    for rel in range(rel_shape):
        member = meta[0] ^ rel
        row = 0
        for ref in (w_gu, a_gu, w_down, a_down, b_gu, b_down):
            row = put_blocks(outs[rel], row, ref[member])


def three_parts(v):
    high = v.astype(BF).astype(F32)
    mid = (v - high).astype(BF).astype(F32)
    return [high, mid, v - high - mid]


def put_packet(out, e, rows, at=0):
    for j in range(BLOCKS):
        out[e, at + j * CAP : at + (j + 1) * CAP, :] = rows[:, j * LANES : (j + 1) * LANES]


def packet_rows(packets):
    return lanes_cat(
        [packets[:, j * CAP : (j + 1) * CAP, :].reshape(SLOTS, LANES) for j in range(BLOCKS)]
    )


def slots_body(micros, meta, tok, cot, *refs):
    dy, sid_row, sid_col = refs
    strict = (iota((SEQ, SEQ), 0) < iota((SEQ, SEQ), 1)).astype(BF)
    experts = iota((FFN_EXPERTS, SEQ), 0)
    for micro in range(micros):
        turned = tok[micro].T
        route = [turned[16 + k : 17 + k, :].astype(jnp.int32) for k in range(2)]
        hot = [(experts == route[k]).astype(F32) for k in range(2)]
        before = dot((hot[0] + hot[1]).astype(BF), strict)
        sids = []
        for k in range(2):
            rank = jnp.sum(before * hot[k], axis=0, keepdims=True).astype(jnp.int32)
            sids.append(jnp.where(route[k] < FFN_EXPERTS, route[k] * CAP + rank, -1))
        rows = jnp.concatenate(sids + [jnp.zeros((6, SEQ), jnp.int32)], axis=0)
        sid_row[micro] = rows
        sid_col[micro] = rows.astype(F32).T.astype(jnp.int32)
        all_routes = iota((16, SEQ), 0)
        prev = turned[0:16, :]
        named = [
            jnp.sum(jnp.where(all_routes == route[k], prev, 0.0), axis=0, keepdims=True)
            for k in range(2)
        ]
        fields = [
            jnp.concatenate(
                three_parts(named[1 - k] - named[k])
                + [route[1 - k].astype(F32), jnp.zeros((SIDE - 4, SEQ), F32)],
                axis=0,
            ).astype(BF)
            for k in range(2)
        ]
        at = iota((FFN_EXPERTS * LANES, SEQ), 0)
        at = jnp.where(at % LANES < CAP, at // LANES * CAP + at % LANES, -2)
        hits = [(at == sids[k]).astype(F32).astype(BF) for k in range(2)]
        side = dot_nt(fields[0], hits[0]) + dot_nt(fields[1], hits[1])
        own_id = jnp.full((SIDE, LANES), 1.0, F32) * meta[micro].astype(F32)
        slot = iota((SLOTS, SEQ), 0)
        table = ((slot == sids[0]) | (slot == sids[1])).astype(F32).astype(BF)
        rows = dot(table, cot[micro, 0]).astype(BF)
        fourth = iota((SIDE, LANES), 0) == 4
        for e in range(FFN_EXPERTS):
            put_packet(dy, e, rows[e * CAP : (e + 1) * CAP], micro * WIDE)
            one = jnp.where(fourth, own_id, side[:, e * LANES : (e + 1) * LANES])
            dy[e, micro * WIDE + BLOCKS * CAP : (micro + 1) * WIDE, :] = one.astype(BF)


def load_wall(pieces, wall, sems, meta, first):
    copies = [
        pltpu.make_async_copy(piece, wall.at[meta[first + i]], sems.at[i])
        for i, piece in enumerate(pieces)
    ]
    for copy in copies:
        copy.start()
    return copies


class AttnWall:
    def __init__(self, wall, n_src):
        self.wall = wall
        self.n_src = n_src
        self.rows = D // n_src
        self.low = RANKS // n_src
        self.base = (QKV_BLOCKS + AQKV_BLOCKS + OUT_BLOCKS + 1) * self.rows

    def block(self, j, count=1):
        return lanes_cat(
            [
                self.wall[:, (j + i) * self.rows : (j + i + 1) * self.rows, :].reshape(D, LANES)
                for i in range(count)
            ]
        )

    def rank_block(self, j, count=1):
        return lanes_cat(
            [
                self.wall[
                    :, self.base + (j + i) * self.low : self.base + (j + i + 1) * self.low, :
                ].reshape(RANKS, LANES)
                for i in range(count)
            ]
        )

    def qkv(self, j, count=1):
        return self.block(j, count)

    def a_qkv(self, j=0, count=3):
        return self.block(QKV_BLOCKS + j, count)

    def w_out(self):
        return self.block(QKV_BLOCKS + AQKV_BLOCKS, OUT_BLOCKS)

    def a_out(self):
        return self.block(QKV_BLOCKS + AQKV_BLOCKS + OUT_BLOCKS)

    def b_qkv(self, j, count=1):
        return self.rank_block(j, count)

    def b_out(self):
        return self.rank_block(QKV_BLOCKS, OUT_BLOCKS)


def turn(v, cos, sin):
    ahead = pltpu.roll(v, LANES - HEAD // 2, axis=1)
    behind = pltpu.roll(v, HEAD // 2, axis=1)
    first = (iota(v.shape, 1) % HEAD) < HEAD // 2
    return v * cos + jnp.where(first, ahead, behind) * sin


def rank_mask(which):
    return ((iota((1, RANKS), 1) // RANK) == which).astype(F32)


def allowed_bias(meta, at):
    t = iota((SEQ, SEQ), 0)
    u = iota((SEQ, SEQ), 1)
    ok = t >= u
    for j in range(2):
        start, end = meta[at + 2 * j], meta[at + 2 * j + 1]
        ok = ok | ((t >= start) & (t < end) & (u >= start) & (u < end))
    return jnp.concatenate([ok, ok], axis=0)


def split_heads(v):
    low = (iota((1, LANES), 1) < HEAD).astype(v.dtype)
    return jnp.concatenate([v * low, v * (1 - low).astype(v.dtype)], axis=0)


def join_heads(v):
    low = iota((SEQ, LANES), 1) < HEAD
    return jnp.where(low, v[:SEQ], v[SEQ:])


def attn_forward_body(
    micro, n_src, meta, hid, cos_ref, sin_ref, gain_a, gain_m, sid_row, *refs
):
    pieces = refs[:n_src]
    qkv, attended, ranks, resid, lse, send, wall_ref, sems = refs[n_src:]
    copies = load_wall(pieces, wall_ref, sems, meta, 0)
    wall = AttnWall(wall_ref, n_src)
    at_id = n_src + 1 + micro
    at_span = n_src + 3 + 4 * micro
    hidden = hid[0, 0].astype(F32)
    scale = lax.rsqrt(jnp.mean(hidden * hidden, axis=-1, keepdims=True) + EPS)
    normed = (hidden * scale * gain_a[...]).astype(BF)
    mask = rank_mask(meta[at_id])
    ok = allowed_bias(meta, at_span)
    cos, sin = cos_ref[...], sin_ref[...]
    for copy in copies:
        copy.wait()
    proj = dot(normed, wall.a_qkv())
    ranks_in = [(proj[:, j * RANKS : (j + 1) * RANKS] * mask).astype(BF) for j in range(3)]
    for j in range(3):
        ranks[:, j * RANKS : (j + 1) * RANKS] = ranks_in[j]
    for j in range(3):
        for pair in range(3):
            at = j * 6 + pair * 2
            part = dot(normed, wall.qkv(at, 2)) + dot(ranks_in[j], wall.b_qkv(at, 2))
            for half in range(2):
                one = part[:, half * LANES : (half + 1) * LANES]
                if j < 2:
                    one = turn(one, cos, sin)
                qkv[:, (at + half) * LANES : (at + half + 1) * LANES] = one.astype(BF)
    lse_cols = []
    for pair in range(6):
        query = qkv[:, pair * LANES : (pair + 1) * LANES]
        key = qkv[:, (6 + pair) * LANES : (7 + pair) * LANES]
        value = qkv[:, (12 + pair) * LANES : (13 + pair) * LANES]
        scores = jnp.where(ok, dot_nt(split_heads(query), key) * (1.0 / math.sqrt(HEAD)), NEG)
        top = jnp.max(scores, axis=-1, keepdims=True)
        expo = jnp.exp(scores - top)
        total = jnp.sum(expo, axis=-1, keepdims=True)
        probs = (expo * (1.0 / total)).astype(BF)
        attended[:, pair * LANES : (pair + 1) * LANES] = join_heads(dot(probs, value)).astype(BF)
        logs = top + jnp.log(total)
        lse[:, pair : pair + 1] = logs
    mixed = attended[...]
    ranks_out = (dot(mixed, wall.a_out()) * mask).astype(BF)
    ranks[:, 3 * RANKS :] = ranks_out
    out = hidden + dot(mixed, wall.w_out()) + dot(ranks_out, wall.b_out())
    resid[...] = out
    scale_m = lax.rsqrt(jnp.mean(out * out, axis=-1, keepdims=True) + EPS)
    lowered = (out * scale_m * gain_m[...]).astype(BF)
    sids = sid_row[0]
    at = iota((SLOTS, SEQ), 0)
    table = ((at == sids[0:1, :]) | (at == sids[1:2, :])).astype(F32).astype(BF)
    send[...] = dot(table, lowered).astype(BF).reshape(FFN_EXPERTS, CAP, D)


class ExpertWall:
    def __init__(self, wall, n_src):
        self.wall = wall
        self.n_src = n_src
        self.rows = D // n_src
        self.ff = FF // n_src
        self.low = RANKS // n_src
        self.down_at = (GU_BLOCKS + AGU_BLOCKS) * self.rows
        self.rank_at = self.down_at + (DOWN_BLOCKS + 1) * self.ff

    def block(self, j):
        start = j * self.rows
        if not isinstance(j, int):
            start = pl.multiple_of(start, self.rows)
        return self.wall[:, pl.ds(start, self.rows), :].reshape(D, LANES)

    def gate_up(self, j, count):
        return lanes_cat([self.block(j + i) for i in range(count)])

    def a_gate_up(self):
        return lanes_cat([self.block(GU_BLOCKS + i) for i in range(AGU_BLOCKS)])

    def rank_block(self, j):
        start = self.rank_at + j * self.low
        if not isinstance(j, int):
            start = pl.multiple_of(start, self.low)
        return self.wall[:, pl.ds(start, self.low), :].reshape(RANKS, LANES)

    def b_gate_up(self, j, count):
        return lanes_cat([self.rank_block(j + i) for i in range(count)])

    def b_down(self):
        return lanes_cat([self.rank_block(GU_BLOCKS + i) for i in range(DOWN_BLOCKS)])

    def down(self, src, count):
        return lanes_cat(
            [
                self.wall[
                    pl.ds(src, count), self.down_at + i * self.ff : self.down_at + (i + 1) * self.ff, :
                ].reshape(count * self.ff, LANES)
                for i in range(DOWN_BLOCKS)
            ]
        )

    def a_down(self, src, count):
        start = self.down_at + DOWN_BLOCKS * self.ff
        return self.wall[pl.ds(src, count), start : start + self.ff, :].reshape(
            count * self.ff, LANES
        )


CHUNK = 512


def expert_body(n_src, carried, meta, tin, dyp, route_w, *refs):
    if carried:
        before, refs = refs[0], refs[1:]
    pieces = refs[:n_src]
    fo, dtin, grads, wall_ref, sems, fo_acc, dt_acc, pd_acc, dug_acc, *more = refs[n_src:]
    copies = load_wall(pieces, wall_ref, sems, meta, 0)
    wall = ExpertWall(wall_ref, n_src)
    if carried:
        earlier = pltpu.make_async_copy(before, more[0], more[1])
        earlier.start()
    own = meta[n_src]
    tokens = tin[...].reshape(SLOTS, D)
    cot = packet_rows(dyp).astype(F32)
    cols = jnp.concatenate(
        [dyp[s, BLOCKS * CAP :, :].astype(F32).T[:CAP] for s in range(FFN_EXPERTS)], axis=0
    )
    logits = exact_dot(tokens.astype(F32), route_w[...])
    lane = iota((SLOTS, LANES), 1)
    gap = jnp.sum(
        jnp.where(lane == own, logits, 0.0)
        - jnp.where(lane == cols[:, 3:4].astype(jnp.int32), logits, 0.0),
        axis=1,
        keepdims=True,
    )
    gate = sigmoid(gap - (cols[:, 0:1] + cols[:, 1:2] + cols[:, 2:3]))
    mask = ((lane // RANK) == cols[:, 4:5].astype(jnp.int32)).astype(F32)
    d_out = (cot * gate).astype(BF)
    for copy in copies:
        copy.wait()

    a_gu = wall.a_gate_up()
    proj = dot(tokens, a_gu)
    ranks_in = [(proj[:, j * RANKS : (j + 1) * RANKS] * mask).astype(BF) for j in range(2)]
    d_ranks_down = (dot_nt(d_out, wall.b_down()) * mask).astype(BF)
    fo_acc[...] = jnp.zeros_like(fo_acc)
    dt_acc[...] = jnp.zeros_like(dt_acc)
    pd_acc[...] = jnp.zeros_like(pd_acc)
    dug_acc[...] = jnp.zeros_like(dug_acc)
    blocks = CHUNK // LANES
    srcs = max(1, CHUNK // wall.ff)
    gb_at = AGU_BLOCKS * wall.rows
    ad_at = gb_at + GU_BLOCKS * wall.low
    bd_at = ad_at + wall.ff

    def step(f, carry):
        j = f * blocks
        wg = wall.gate_up(j, blocks)
        wu = wall.gate_up(j + GU_BLOCKS // 2, blocks)
        bg = wall.b_gate_up(j, blocks)
        bu = wall.b_gate_up(j + GU_BLOCKS // 2, blocks)
        wd = wall.down(f * srcs, srcs)
        ad = wall.a_down(f * srcs, srcs)
        g = dot(tokens, wg) + dot(ranks_in[0], bg)
        u = dot(tokens, wu) + dot(ranks_in[1], bu)
        d_hidden = dot_nt(d_out, wd) + dot_nt(d_ranks_down, ad)
        sg = sigmoid(g)
        act = g * sg
        hidden = (act * u).astype(BF)
        d_gate = (d_hidden * u * (sg * (1.0 + g * (1.0 - sg)))).astype(BF)
        d_up = (d_hidden * act).astype(BF)
        fo_acc[...] += dot(hidden, wd)
        pd_acc[...] += dot(hidden, ad)
        dt_acc[...] += dot_nt(d_gate, wg) + dot_nt(d_up, wu)
        dug_acc[:, :RANKS] += dot_nt(d_gate, bg)
        dug_acc[:, RANKS:] += dot_nt(d_up, bu)
        for k, (rank, grad) in enumerate(((ranks_in[0], d_gate), (ranks_in[1], d_up))):
            part = dot_tn(rank, grad)
            for i in range(blocks):
                at = gb_at + (j + k * (GU_BLOCKS // 2) + i) * wall.low
                rows = pl.ds(at if isinstance(at, int) else pl.multiple_of(at, 8), wall.low)
                one = part[:, i * LANES : (i + 1) * LANES].reshape(n_src, wall.low, LANES)
                grads[:, rows, :] = one
        part = dot_tn(hidden, d_ranks_down).reshape(srcs, wall.ff, LANES)
        grads[pl.ds(f * srcs, srcs), ad_at : ad_at + wall.ff, :] = part
        return carry

    if wall.low % 8:
        for f in range(FF // CHUNK):
            step(f, 0)
    else:
        lax.fori_loop(0, FF // CHUNK, step, 0)
    ranks_down = (pd_acc[...] * mask).astype(BF)
    result = (fo_acc[...] + dot(ranks_down, wall.b_down())).astype(BF)
    along = jnp.sum(cot * result.astype(F32), axis=1, keepdims=True)
    parts = three_parts(along)
    along = jnp.where(lane == 0, parts[0], jnp.where(lane == 1, parts[1], 0.0))
    along = jnp.where(lane == 2, parts[2], along).astype(BF)
    eye = (iota((CAP, LANES), 0) == iota((CAP, LANES), 1)).astype(F32).astype(BF)
    fo[...] = result.reshape(FFN_EXPERTS, CAP, D)
    for r in range(FFN_EXPERTS):
        side = dot_tn(along[r * CAP : (r + 1) * CAP], eye)[:SIDE]
        dtin[r, BLOCKS * CAP :, :] = side.astype(BF)
    part = dot_tn(ranks_down, d_out)
    for i in range(DOWN_BLOCKS):
        grads[:, bd_at + i * wall.low : bd_at + (i + 1) * wall.low, :] = part[
            :, i * LANES : (i + 1) * LANES
        ].reshape(n_src, wall.low, LANES)
    d_ranks = [(dug_acc[:, k * RANKS : (k + 1) * RANKS] * mask).astype(BF) for k in range(2)]
    both = lanes_cat(d_ranks)
    d_tokens = (dt_acc[...] + dot_nt(both, a_gu)).astype(BF)
    for r in range(FFN_EXPERTS):
        put_packet(dtin, r, d_tokens[r * CAP : (r + 1) * CAP])
    part = dot_tn(tokens, both)
    for i in range(AGU_BLOCKS):
        grads[:, i * wall.rows : (i + 1) * wall.rows, :] = part[
            :, i * LANES : (i + 1) * LANES
        ].reshape(n_src, wall.rows, LANES)
    if carried:
        earlier.wait()
        grads[...] = grads[...] + more[0][...]


def attn_backward_body(micro, n_src, carried, meta, hid, cot, resid_ref, qkv, attended, ranks, lse,
                       dtin, tok, sid_col, gain_a, gain_m, route_w, consts, cos_ref, sin_ref,
                       *refs):
    if carried:
        before, refs = refs[0], refs[1:]
    pieces = refs[:n_src]
    base, gates, grad_in, grads, wall_ref, sems, dqkv, *more = refs[n_src:]
    copies = load_wall(pieces, wall_ref, sems, meta, 0)
    if carried:
        earlier = pltpu.make_async_copy(before, more[0], more[1])
        earlier.start()
    wall = AttnWall(wall_ref, n_src)
    at_id = n_src + 1 + micro
    at_span = n_src + 3 + 4 * micro
    mask = rank_mask(meta[at_id])
    resid = resid_ref[...]
    dy = cot[0, 0].astype(F32)
    scale_m = lax.rsqrt(jnp.mean(resid * resid, axis=-1, keepdims=True) + EPS)
    gain = gain_m[...]
    normed = resid * scale_m * gain
    lowered = normed.astype(BF).astype(F32)
    weights = route_w[...]
    scores = exact_dot(lowered, weights)
    token = tok[0]
    lane = iota((SEQ, LANES), 1)
    route = [token[:, 16 + k : 17 + k].astype(jnp.int32) for k in range(2)]
    logits = scores + token
    chosen = [
        jnp.sum(jnp.where(lane == route[k], logits, 0.0), axis=1, keepdims=True) for k in range(2)
    ]
    gate = [sigmoid(chosen[k] - chosen[1 - k]) for k in range(2)]
    keep = [sigmoid(scores[:, 12 + j : 13 + j]) for j in range(2)]
    slot = iota((SEQ, SLOTS), 1)
    hits = [(slot == sid_col[0][:, k : k + 1]).astype(F32).astype(BF) for k in range(2)]
    spread = iota((SEQ, FFN_EXPERTS * LANES), 1)
    spread = jnp.where(spread % LANES < CAP, spread // LANES * CAP + spread % LANES, -2)
    side = lanes_cat([dtin[e, BLOCKS * CAP :, :] for e in range(FFN_EXPERTS)])
    along = []
    for k in range(2):
        found = (spread == sid_col[0][:, k : k + 1]).astype(F32).astype(BF)
        parts = dot_nt(found, side)
        along.append(parts[:, 0:1] + parts[:, 1:2] + parts[:, 2:3])
    value = [consts[j : j + 1, :] for j in range(2)]
    is_copy = [(route[k] == FFN_EXPERTS + 1).astype(F32) for k in range(2)]
    is_const = [
        [(route[k] == FFN_EXPERTS + 2 + j).astype(F32) for j in range(2)] for k in range(2)
    ]
    share = sum(
        gate[k] * (is_copy[k] + is_const[k][0] * keep[0] + is_const[k][1] * keep[1])
        for k in range(2)
    )
    named = [gate[0] * is_const[0][j] + gate[1] * is_const[1][j] for j in range(2)]
    out = resid + share * normed
    out = out + (named[0] * (1.0 - keep[0])) * value[0] + (named[1] * (1.0 - keep[1])) * value[1]
    base[...] = out
    gates[...] = jnp.where(lane == 0, gate[0], jnp.where(lane == 1, gate[1], 0.0))
    dy_normed = jnp.sum(dy * normed, axis=1, keepdims=True)
    dy_value = [jnp.sum(dy * value[j], axis=1, keepdims=True) for j in range(2)]
    d_gate = []
    for k in range(2):
        one = along[k] + is_copy[k] * dy_normed
        for j in range(2):
            one = one + is_const[k][j] * (keep[j] * dy_normed + (1.0 - keep[j]) * dy_value[j])
        d_gate.append(one)
    centre = gate[0] * d_gate[0] + gate[1] * d_gate[1]
    d_logits = jnp.zeros((SEQ, LANES), F32)
    for k in range(2):
        d_logits = d_logits + jnp.where(lane == route[k], gate[k] * (d_gate[k] - centre), 0.0)
    for j in range(2):
        d_keep = named[j] * (dy_normed - dy_value[j])
        d_logits = d_logits + jnp.where(
            lane == 12 + j, d_keep * keep[j] * (1.0 - keep[j]), 0.0
        )
    d_normed = share * dy + exact_dot_nt(d_logits, weights)
    d_normed = d_normed + dot(hits[0] + hits[1], packet_rows(dtin))
    scaled = gain * d_normed
    d_resid = (
        dy
        + scale_m * scaled
        - resid * (scale_m * scale_m * scale_m) * jnp.mean(scaled * resid, axis=-1, keepdims=True)
    )
    d_branch = d_resid.astype(BF)
    for copy in copies:
        copy.wait()
    d_ranks_out = (dot_nt(d_branch, wall.b_out()) * mask).astype(BF)
    d_mixed = (dot_nt(d_branch, wall.w_out()) + dot_nt(d_ranks_out, wall.a_out())).astype(BF)
    a_rows, b_rows = wall.rows, wall.low
    gb_at = AQKV_BLOCKS * a_rows
    ao_at = gb_at + QKV_BLOCKS * b_rows
    bo_at = ao_at + a_rows
    part = dot_tn(ranks[:, 3 * RANKS :], d_branch)
    for i in range(OUT_BLOCKS):
        grads[:, bo_at + i * b_rows : bo_at + (i + 1) * b_rows, :] = part[
            :, i * LANES : (i + 1) * LANES
        ].reshape(n_src, b_rows, LANES)
    grads[:, ao_at : ao_at + a_rows, :] = dot_tn(attended[...], d_ranks_out).reshape(
        n_src, a_rows, LANES
    )
    ok = allowed_bias(meta, at_span)
    cos, sin = cos_ref[...], -sin_ref[...]
    inv = 1.0 / math.sqrt(HEAD)
    for pair in range(6):
        query = split_heads(qkv[:, pair * LANES : (pair + 1) * LANES])
        key = qkv[:, (6 + pair) * LANES : (7 + pair) * LANES]
        val = qkv[:, (12 + pair) * LANES : (13 + pair) * LANES]
        d_heads = split_heads(d_mixed[:, pair * LANES : (pair + 1) * LANES])
        sc = jnp.where(ok, dot_nt(query, key) * inv, NEG)
        probs = jnp.exp(sc - lse[:, pair : pair + 1])
        d_probs = dot_nt(d_heads, val)
        row_dot = jnp.sum(probs * d_probs, axis=-1, keepdims=True)
        d_scores = (probs * (d_probs - row_dot)).astype(BF)
        d_query = join_heads(dot(d_scores, key)) * inv
        d_key = dot_tn(d_scores, query) * inv
        d_value = dot_tn(probs.astype(BF), d_heads)
        dqkv[:, pair * LANES : (pair + 1) * LANES] = turn(d_query, cos, sin).astype(BF)
        dqkv[:, (6 + pair) * LANES : (7 + pair) * LANES] = turn(d_key, cos, sin).astype(BF)
        dqkv[:, (12 + pair) * LANES : (13 + pair) * LANES] = d_value.astype(BF)
    hidden = hid[0, 0].astype(F32)
    scale = lax.rsqrt(jnp.mean(hidden * hidden, axis=-1, keepdims=True) + EPS)
    first = gain_a[...]
    normed_low = (hidden * scale * first).astype(BF)
    d_in = jnp.zeros((SEQ, D), F32)
    d_ranks = []
    for j in range(3):
        part = dqkv[:, j * D : (j + 1) * D]
        d_ranks.append((dot_nt(part, wall.b_qkv(j * 6, 6)) * mask).astype(BF))
        d_in = d_in + dot_nt(part, wall.qkv(j * 6, 6))
        gb = dot_tn(ranks[:, j * RANKS : (j + 1) * RANKS], part)
        for i in range(6):
            at = gb_at + (j * 6 + i) * b_rows
            grads[:, at : at + b_rows, :] = gb[:, i * LANES : (i + 1) * LANES].reshape(
                n_src, b_rows, LANES
            )
    ranks_all = lanes_cat(d_ranks)
    d_in = d_in + dot_nt(ranks_all, wall.a_qkv())
    ga = dot_tn(normed_low, ranks_all)
    for i in range(3):
        grads[:, i * a_rows : (i + 1) * a_rows, :] = ga[:, i * LANES : (i + 1) * LANES].reshape(
            n_src, a_rows, LANES
        )
    scaled = first * d_in
    grad_in[...] = (
        d_resid
        + scale * scaled
        - hidden * (scale * scale * scale) * jnp.mean(scaled * hidden, axis=-1, keepdims=True)
    )
    if carried:
        earlier.wait()
        grads[...] = grads[...] + more[0][...]


def output_body(micros, meta, *refs):
    sid_col, outs = refs[3 * micros], refs[3 * micros + 1 :]
    slot = iota((SEQ, SLOTS), 1)
    for micro in range(micros):
        total, gates, fo = (refs[3 * micro + i][...] for i in range(3))
        for k in range(2):
            hits = (slot == sid_col[micro, :, k : k + 1]).astype(F32).astype(BF)
            total = total + gates[:, k : k + 1] * dot(hits, fo.reshape(SLOTS, D))
        outs[micro][...] = total.astype(BF)


def flip(values, axis, bit, size):
    return lax.ppermute(values, axis, [(i, i ^ bit) for i in range(size)])


def later(values, others):
    return lax.optimization_barrier((values, others))[0]


def bits(size):
    return [1 << i for i in range(size.bit_length() - 1)]


def halve_sum(values, axis, size):
    place = lax.axis_index(axis)
    for bit in reversed(bits(size)):
        pair = values.reshape((2, values.shape[0] // 2) + values.shape[1:])
        side = (place // bit) % 2
        away = lax.dynamic_index_in_dim(pair, 1 - side, 0, keepdims=False).astype(BF)
        kept = lax.dynamic_index_in_dim(pair, side, 0, keepdims=False)
        values = kept + flip(away, axis, bit, size).astype(F32)
    return values


def body(members, hidden_in, prev_logits, routes, adapter_ids, image_spans, cotangent, gain_attn,
         gain_moe, router_weight, const_gate, const_value, w_qkv, w_out, a_qkv, b_qkv, a_out, b_out,
         w_gate_up, w_down, a_gate_up, b_gate_up, a_down, b_down):
    rest = lax.axis_size("y")
    peers = lax.axis_size("z")
    n_src = rest * members * 2
    micros = hidden_in.shape[0]
    y, x, c, z = (lax.axis_index(name) for name in ("y", "x", "c", "z"))
    place = (y * members + x) * 2 + c

    attn_rows = (QKV_BLOCKS + AQKV_BLOCKS + OUT_BLOCKS + 1) * (D // n_src) + (
        QKV_BLOCKS + OUT_BLOCKS
    ) * (RANKS // n_src)
    expert_rows = (
        (GU_BLOCKS + AGU_BLOCKS) * (D // n_src)
        + (DOWN_BLOCKS + 1) * (FF // n_src)
        + (GU_BLOCKS + DOWN_BLOCKS) * (RANKS // n_src)
    )
    none = jnp.zeros((1,), jnp.int32)
    args = (w_qkv, a_qkv, w_out, a_out, b_qkv, b_out)
    (attn_own,) = call(
        pack_attn_body,
        none,
        args,
        [whole(a.shape) for a in args],
        [shape((attn_rows, LANES), BF)],
        us=2,
    )
    tok = jnp.concatenate(
        [
            prev_logits[:, 0],
            jnp.zeros((micros, SEQ, 4), F32),
            routes[:, 0].astype(F32),
            jnp.zeros((micros, SEQ, LANES - 18), F32),
        ],
        axis=2,
    )
    route_w = jnp.concatenate(
        [router_weight, const_gate, jnp.zeros((D, LANES - 14), F32)], axis=1
    )
    half = HEAD // 2
    freqs = jnp.exp(jnp.arange(half, dtype=F32) * (-2.0 * math.log(10000.0) / HEAD))
    angles = jnp.arange(SEQ, dtype=F32)[:, None] * freqs[None, :]
    cos = jnp.tile(jnp.cos(angles), (1, 4))
    sin = jnp.sin(angles)
    sin = jnp.tile(jnp.concatenate([-sin, sin], axis=1), (1, 2))
    gain_a = gain_attn.reshape(1, D)
    gain_m = gain_moe.reshape(1, D)

    packet = shape((FFN_EXPERTS, CAP, D), BF)
    wide_packet = shape((FFN_EXPERTS, WIDE, LANES), BF)
    dy_send, sid_row, sid_col = call(
        functools.partial(slots_body, micros),
        adapter_ids.reshape(-1),
        (tok, cotangent),
        [whole(tok.shape), whole(cotangent.shape)],
        [
            shape((FFN_EXPERTS, micros * WIDE, LANES), BF),
            shape((micros, 8, SEQ), jnp.int32),
            shape((micros, SEQ, 8), jnp.int32),
        ],
        us=4,
        after=(attn_own,),
    )

    args = (w_gate_up, a_gate_up, w_down, a_down, b_gate_up, b_down)
    expert_own = call(
        functools.partial(pack_experts_body, members),
        x.reshape(1).astype(jnp.int32),
        args,
        [whole(a.shape) for a in args],
        [shape((expert_rows, LANES), BF)] * members,
        us=4,
        after=(sid_row,),
    )

    attn_pieces = [(attn_own, 0)]
    for bit in bits(members):
        attn_pieces += [(flip(v, "x", bit, members), m ^ (bit * 2)) for v, m in attn_pieces]
    for bit in bits(rest):
        way = bit * members * 2
        beside = flip(attn_own, "y", bit, rest)
        attn_pieces += [(beside, way)] + [
            (flip(later(v, (sid_row, beside)), "y", bit, rest), m ^ way)
            for v, m in attn_pieces[1:]
        ]
    attn_near, attn_far = attn_pieces[1][0], attn_pieces[-1][0]
    attn_beside = attn_pieces[members][0]
    attn_pieces += [
        (flip(v if v is attn_far else later(v, attn_far), "c", 1, 2), m ^ 1)
        for v, m in attn_pieces
    ]
    attn_bufs = [v for v, m in attn_pieces]
    meta_attn = jnp.concatenate(
        [
            place ^ jnp.array([m for v, m in attn_pieces], jnp.int32),
            jnp.zeros((1,), jnp.int32),
            adapter_ids.reshape(-1),
            image_spans.reshape(-1),
        ]
    ).astype(jnp.int32)

    group = ("z", "x") if members > 1 else "z"

    def trade(values):
        return lax.all_to_all(values, group, 0, 0, tiled=True)

    expert_pieces = [(expert_own[0], 0)]
    for rel in range(1, members):
        pairs = [(i, i ^ rel) for i in range(members)]
        away = later(expert_own[rel], attn_near)
        expert_pieces.append((lax.ppermute(away, "x", pairs), rel * 2))
    first = bits(rest)[0]
    own = later(expert_own[0], attn_beside)
    beside = (flip(own, "y", first, rest), first * members * 2)
    near = [[v for v, m in expert_pieces[1:]] + [beside[0]]]

    dy_got = trade(dy_send)
    saved, tin = [], []
    for micro in range(micros):
        args = (hidden_in, cos, sin, gain_a, gain_m, sid_row, *attn_bufs)
        specs = [
            one_micro((1, SEQ, D), micro),
            whole(cos.shape),
            whole(sin.shape),
            whole(gain_a.shape),
            whole(gain_m.shape),
            one_micro((8, SEQ), micro),
        ] + [ANYWHERE] * n_src
        saved.append(
            call(
                functools.partial(attn_forward_body, micro, n_src),
                meta_attn,
                args,
                specs,
                [
                    shape((SEQ, 3 * D), BF),
                    shape((SEQ, D), BF),
                    shape((SEQ, 4 * RANKS), BF),
                    shape((SEQ, D), F32),
                    shape((2 * SEQ, 8), F32),
                    packet,
                ],
                [
                    pltpu.VMEM((n_src, attn_rows, LANES), BF),
                    pltpu.SemaphoreType.DMA((n_src,)),
                ],
                us=FORWARD_HINT,
                after=tuple(near[micro]) if micro < len(near) else (),
            )
        )
        if micro == 0:
            for bit in bits(rest):
                relay = expert_pieces[1:] if bit == first else expert_pieces
                more = [
                    (flip(v, "y", bit, rest), m ^ (bit * members * 2)) for v, m in relay
                ]
                expert_pieces += ([beside] if bit == first else []) + more
        send = saved[micro][5]
        tin.append(trade(send if micro == 0 else later(send, expert_pieces[-1][0])))
    expert_pieces += [
        (flip(later(v, saved[-1][4]), "c", 1, 2), m ^ 1) for v, m in expert_pieces
    ]
    expert_bufs = [v for v, m in expert_pieces]
    meta_expert = jnp.concatenate(
        [
            place ^ jnp.array([m for v, m in expert_pieces], jnp.int32),
            (z * members + x).reshape(1),
        ]
    ).astype(jnp.int32)

    expert_grad_rows = (
        AGU_BLOCKS * (D // n_src)
        + (GU_BLOCKS + DOWN_BLOCKS) * (RANKS // n_src)
        + FF // n_src
    )
    grads_e = None
    fo_send, dtin = [], []
    for micro in range(micros):
        carried = grads_e is not None
        args = (tin[micro], dy_got, route_w)
        specs = [whole(a.shape) for a in args]
        specs[1] = pl.BlockSpec(
            (FFN_EXPERTS, WIDE, LANES), lambda i, meta, micro=micro: (0, micro, 0)
        )
        if carried:
            args += (grads_e,)
            specs.append(ANYWHERE)
        specs += [ANYWHERE] * n_src
        fo, d_tokens, grads_e = call(
            functools.partial(expert_body, n_src, carried),
            meta_expert,
            args + tuple(expert_bufs),
            specs,
            [
                packet,
                wide_packet,
                shape((n_src, expert_grad_rows, LANES), F32),
            ],
            [
                pltpu.VMEM((n_src, expert_rows, LANES), BF),
                pltpu.SemaphoreType.DMA((n_src,)),
                pltpu.VMEM((SLOTS, D), F32),
                pltpu.VMEM((SLOTS, D), F32),
                pltpu.VMEM((SLOTS, RANKS), F32),
                pltpu.VMEM((SLOTS, 2 * RANKS), F32),
            ]
            + ([pltpu.VMEM(grads_e.shape, F32), pltpu.SemaphoreType.DMA] if carried else []),
            us=31,
        )
        fo_send.append(fo)
        dtin.append(trade(d_tokens))

    attn_grad_rows = (AQKV_BLOCKS + 1) * (D // n_src) + (QKV_BLOCKS + OUT_BLOCKS) * (
        RANKS // n_src
    )
    grads_a = None
    mixed, grad_rows = [], []
    for micro in range(micros):
        carried = grads_a is not None
        qkv, attended, ranks, resid, lse = saved[micro][:5]
        args = (hidden_in, cotangent, resid, qkv, attended, ranks, lse, dtin[micro], tok, sid_col,
                gain_a, gain_m, route_w, const_value, cos, sin)
        specs = [whole(a.shape) for a in args]
        specs[0] = one_micro((1, SEQ, D), micro)
        specs[1] = one_micro((1, SEQ, D), micro)
        specs[8] = one_micro((SEQ, LANES), micro)
        specs[9] = one_micro((SEQ, 8), micro)
        if carried:
            args += (grads_a,)
            specs.append(ANYWHERE)
        specs += [ANYWHERE] * n_src
        base, gates, grad_in, grads_a = call(
            functools.partial(attn_backward_body, micro, n_src, carried),
            meta_attn,
            args + tuple(attn_bufs),
            specs,
            [
                shape((SEQ, D), F32),
                shape((SEQ, LANES), F32),
                shape((SEQ, D), F32),
                shape((n_src, attn_grad_rows, LANES), F32),
            ],
            [
                pltpu.VMEM((n_src, attn_rows, LANES), BF),
                pltpu.SemaphoreType.DMA((n_src,)),
                pltpu.VMEM((SEQ, 3 * D), BF),
            ]
            + ([pltpu.VMEM(grads_a.shape, F32), pltpu.SemaphoreType.DMA] if carried else []),
            us=19,
            after=(half_e,) if carried else (),
        )
        grad_rows.append(grad_in)
        mixed.append((base, gates, trade(later(fo_send[micro], base))))
        if not carried:
            total = later(grads_e, base).reshape((rest, members, 2) + grads_e.shape[1:])
            half_e = halve_sum(jnp.moveaxis(total, 2, 0), "c", 2)
            total = half_e.reshape((rest, members) + grads_e.shape[1:])
            total = halve_sum(total, "y", rest).reshape((members,) + grads_e.shape[1:])
            held = (mixed[0][2], total)
    args = tuple(v for parts in mixed for v in parts) + (sid_col,)
    block_rows = call(
        functools.partial(output_body, micros),
        none,
        args,
        [whole(a.shape) for a in args],
        [shape((SEQ, D), BF)] * micros,
        us=5,
    )
    owned = lax.dynamic_index_in_dim(total, x, 0, keepdims=True)
    for rel in range(1, members):
        away = lax.dynamic_index_in_dim(total, x ^ rel, 0, keepdims=True).astype(BF)
        got = lax.ppermute(away, "x", [(i, i ^ rel) for i in range(members)])
        owned = jnp.concatenate([owned, got.astype(F32)], axis=0)
    if members > 1:
        owned = owned[x ^ jnp.arange(members)]

    def blocks_of(values, row, count, height):
        part = values[:, row : row + count * height].reshape(-1, count, height, LANES)
        return jnp.moveaxis(part, 1, 2).reshape(-1, height, count * LANES)

    rows, low, ff = D // n_src, RANKS // n_src, FF // n_src
    at = 0
    grad_agu = blocks_of(owned, at, AGU_BLOCKS, rows)
    at += AGU_BLOCKS * rows
    grad_bgu = blocks_of(owned, at, GU_BLOCKS, low)
    at += GU_BLOCKS * low
    grad_ad = blocks_of(owned, at, 1, ff)
    at += ff
    grad_bd = blocks_of(owned, at, DOWN_BLOCKS, low)

    total = grads_a.reshape((rest, members, 2) + grads_a.shape[1:])
    total = halve_sum(jnp.moveaxis(total, 2, 0), "c", 2)
    if micros > 1:
        total = later(total, held)
    total = total.reshape((rest, members) + grads_a.shape[1:])
    total = halve_sum(total, "y", rest).reshape((members,) + grads_a.shape[1:])
    total = halve_sum(total, "x", members).reshape((1,) + grads_a.shape[1:])
    for bit in bits(peers):
        sent = total.astype(BF)
        total = sent.astype(F32) + flip(sent, "z", bit, peers).astype(F32)
    at = 0
    grad_aq = blocks_of(total, at, AQKV_BLOCKS, rows)[0]
    at += AQKV_BLOCKS * rows
    grad_bq = blocks_of(total, at, QKV_BLOCKS, low)[0]
    at += QKV_BLOCKS * low
    grad_ao = blocks_of(total, at, 1, rows)[0]
    at += rows
    grad_bo = blocks_of(total, at, OUT_BLOCKS, low)[0]

    return (jnp.stack(block_rows)[:, None], jnp.stack(grad_rows)[:, None], grad_aq, grad_bq,
            grad_ao, grad_bo, grad_agu, grad_bgu, grad_ad, grad_bd)


def solution(mesh):
    dp, expert = mesh.shape["dp"], mesh.shape["expert"]
    members = FFN_EXPERTS // expert
    fine = Mesh(
        mesh.devices.reshape(dp // (2 * members), members, 2, expert), ("y", "x", "c", "z")
    )
    owners = ("y", "x", "c")
    seqs = ("y", "x", "c", "z")
    tokens = P(None, seqs, None, None)
    rows = P(owners, None)
    expert_rows = P("z", owners, None)
    in_specs = (
        (tokens, tokens, tokens, P(None, seqs), tokens, tokens)
        + (P(),) * 5
        + (rows,) * 6
        + (expert_rows,) * 6
    )
    out_specs = (tokens, tokens) + (rows,) * 4 + (expert_rows,) * 4
    return jax.shard_map(
        functools.partial(body, members),
        mesh=fine,
        in_specs=in_specs,
        out_specs=out_specs,
        check_vma=False,
    )
```

```python
import functools
import math

import jax
import jax.numpy as jnp
from jax import lax
from jax.experimental import pallas as pl
from jax.experimental.pallas import tpu as pltpu
from jax.sharding import Mesh
from jax.sharding import PartitionSpec as P

D = 768
HEADS = 12
HEAD = 64
FF = 2048
FFN_EXPERTS = 8
RANK = 16
RANKS = 128
CAP = 80
LANES = 128
SEQ = 256
SLOTS = FFN_EXPERTS * CAP
BLOCKS, SIDE = D // LANES, 8
WIDE = BLOCKS * CAP + SIDE
NEG = -1e30
EPS = 1e-05
BF = jnp.bfloat16
F32 = jnp.float32
VMEM_LIMIT = 60 * 1024 * 1024
FLOPS_PER_US, BYTES_PER_US = 10**9, 10**6
FORWARD_HINT = 12

QKV_BLOCKS, AQKV_BLOCKS, OUT_BLOCKS = 18, 3, 6
GU_BLOCKS, AGU_BLOCKS, DOWN_BLOCKS = 32, 2, 6


def dot(a, b):
    return lax.dot_general(a, b, (((1,), (0,)), ((), ())), preferred_element_type=F32)


def dot_nt(a, b):
    return lax.dot_general(a, b, (((1,), (1,)), ((), ())), preferred_element_type=F32)


def dot_tn(a, b):
    return lax.dot_general(a, b, (((0,), (0,)), ((), ())), preferred_element_type=F32)


def exact_dot(a, b):
    return lax.dot_general(
        a, b, (((1,), (0,)), ((), ())), precision=lax.Precision.HIGHEST, preferred_element_type=F32
    )


def exact_dot_nt(a, b):
    return lax.dot_general(
        a, b, (((1,), (1,)), ((), ())), precision=lax.Precision.HIGHEST, preferred_element_type=F32
    )


def lanes_cat(parts):
    return parts[0] if len(parts) == 1 else jnp.concatenate(parts, axis=1)


def iota(shape, dim):
    return lax.broadcasted_iota(jnp.int32, shape, dim)


def sigmoid(v):
    return 1.0 / (1.0 + jnp.exp(-v))


def whole(shape):
    return pl.BlockSpec(tuple(shape), lambda i, meta: (0,) * len(shape))


def one_micro(shape, micro):
    return pl.BlockSpec((1,) + tuple(shape), lambda i, meta: (micro,) + (0,) * len(shape))


ANYWHERE = pl.BlockSpec(memory_space=pl.ANY)


def call(body, meta, args, specs, outs, scratch=(), us=1, after=()):
    out_specs = [whole(o.shape) for o in outs]

    def late(meta_ref, *refs):
        body(meta_ref, *refs[len(after) :])

    args = tuple(after) + tuple(args)
    specs = [ANYWHERE] * len(after) + list(specs)
    return pl.pallas_call(
        late if after else body,
        out_shape=outs,
        cost_estimate=pl.CostEstimate(
            flops=us * FLOPS_PER_US, transcendentals=0, bytes_accessed=us * BYTES_PER_US
        ),
        grid_spec=pltpu.PrefetchScalarGridSpec(
            num_scalar_prefetch=1,
            grid=(1,),
            in_specs=specs,
            out_specs=out_specs,
            scratch_shapes=list(scratch),
        ),
        compiler_params=pltpu.CompilerParams(
            dimension_semantics=("arbitrary",), vmem_limit_bytes=VMEM_LIMIT
        ),
    )(meta, *args)


def shape(dims, dtype):
    return jax.ShapeDtypeStruct(tuple(dims), dtype)


def put_blocks(out, row, src):
    height, width = src.shape
    for j in range(width // LANES):
        out[row : row + height, :] = src[:, j * LANES : (j + 1) * LANES]
        row += height
    return row


def pack_attn_body(meta, w_qkv, a_qkv, w_out, a_out, b_qkv, b_out, out):
    row = 0
    for ref in (w_qkv, a_qkv, w_out, a_out, b_qkv, b_out):
        row = put_blocks(out, row, ref[...])


def pack_experts_body(rel_shape, meta, w_gu, a_gu, w_down, a_down, b_gu, b_down, *outs):
    for rel in range(rel_shape):
        member = meta[0] ^ rel
        row = 0
        for ref in (w_gu, a_gu, w_down, a_down, b_gu, b_down):
            row = put_blocks(outs[rel], row, ref[member])


def three_parts(v):
    high = v.astype(BF).astype(F32)
    mid = (v - high).astype(BF).astype(F32)
    return [high, mid, v - high - mid]


def put_packet(out, e, rows, at=0):
    for j in range(BLOCKS):
        out[e, at + j * CAP : at + (j + 1) * CAP, :] = rows[:, j * LANES : (j + 1) * LANES]


def packet_rows(packets):
    return lanes_cat(
        [packets[:, j * CAP : (j + 1) * CAP, :].reshape(SLOTS, LANES) for j in range(BLOCKS)]
    )


def slots_body(micros, meta, tok, cot, *refs):
    dy, sid_row, sid_col = refs
    strict = (iota((SEQ, SEQ), 0) < iota((SEQ, SEQ), 1)).astype(BF)
    experts = iota((FFN_EXPERTS, SEQ), 0)
    for micro in range(micros):
        turned = tok[micro].T
        route = [turned[16 + k : 17 + k, :].astype(jnp.int32) for k in range(2)]
        hot = [(experts == route[k]).astype(F32) for k in range(2)]
        before = dot((hot[0] + hot[1]).astype(BF), strict)
        sids = []
        for k in range(2):
            rank = jnp.sum(before * hot[k], axis=0, keepdims=True).astype(jnp.int32)
            sids.append(jnp.where(route[k] < FFN_EXPERTS, route[k] * CAP + rank, -1))
        rows = jnp.concatenate(sids + [jnp.zeros((6, SEQ), jnp.int32)], axis=0)
        sid_row[micro] = rows
        sid_col[micro] = rows.astype(F32).T.astype(jnp.int32)
        all_routes = iota((16, SEQ), 0)
        prev = turned[0:16, :]
        named = [
            jnp.sum(jnp.where(all_routes == route[k], prev, 0.0), axis=0, keepdims=True)
            for k in range(2)
        ]
        fields = [
            jnp.concatenate(
                three_parts(named[1 - k] - named[k])
                + [route[1 - k].astype(F32), jnp.zeros((SIDE - 4, SEQ), F32)],
                axis=0,
            ).astype(BF)
            for k in range(2)
        ]
        at = iota((FFN_EXPERTS * LANES, SEQ), 0)
        at = jnp.where(at % LANES < CAP, at // LANES * CAP + at % LANES, -2)
        hits = [(at == sids[k]).astype(F32).astype(BF) for k in range(2)]
        side = dot_nt(fields[0], hits[0]) + dot_nt(fields[1], hits[1])
        own_id = jnp.full((SIDE, LANES), 1.0, F32) * meta[micro].astype(F32)
        slot = iota((SLOTS, SEQ), 0)
        table = ((slot == sids[0]) | (slot == sids[1])).astype(F32).astype(BF)
        rows = dot(table, cot[micro, 0]).astype(BF)
        fourth = iota((SIDE, LANES), 0) == 4
        for e in range(FFN_EXPERTS):
            put_packet(dy, e, rows[e * CAP : (e + 1) * CAP], micro * WIDE)
            one = jnp.where(fourth, own_id, side[:, e * LANES : (e + 1) * LANES])
            dy[e, micro * WIDE + BLOCKS * CAP : (micro + 1) * WIDE, :] = one.astype(BF)


def load_wall(pieces, wall, sems, meta, first):
    copies = [
        pltpu.make_async_copy(piece, wall.at[meta[first + i]], sems.at[i])
        for i, piece in enumerate(pieces)
    ]
    for copy in copies:
        copy.start()
    return copies


class AttnWall:
    def __init__(self, wall, n_src):
        self.wall = wall
        self.n_src = n_src
        self.rows = D // n_src
        self.low = RANKS // n_src
        self.base = (QKV_BLOCKS + AQKV_BLOCKS + OUT_BLOCKS + 1) * self.rows

    def block(self, j, count=1):
        return lanes_cat(
            [
                self.wall[:, (j + i) * self.rows : (j + i + 1) * self.rows, :].reshape(D, LANES)
                for i in range(count)
            ]
        )

    def rank_block(self, j, count=1):
        return lanes_cat(
            [
                self.wall[
                    :, self.base + (j + i) * self.low : self.base + (j + i + 1) * self.low, :
                ].reshape(RANKS, LANES)
                for i in range(count)
            ]
        )

    def qkv(self, j, count=1):
        return self.block(j, count)

    def a_qkv(self, j=0, count=3):
        return self.block(QKV_BLOCKS + j, count)

    def w_out(self):
        return self.block(QKV_BLOCKS + AQKV_BLOCKS, OUT_BLOCKS)

    def a_out(self):
        return self.block(QKV_BLOCKS + AQKV_BLOCKS + OUT_BLOCKS)

    def b_qkv(self, j, count=1):
        return self.rank_block(j, count)

    def b_out(self):
        return self.rank_block(QKV_BLOCKS, OUT_BLOCKS)


def turn(v, cos, sin):
    ahead = pltpu.roll(v, LANES - HEAD // 2, axis=1)
    behind = pltpu.roll(v, HEAD // 2, axis=1)
    first = (iota(v.shape, 1) % HEAD) < HEAD // 2
    return v * cos + jnp.where(first, ahead, behind) * sin


def rank_mask(which):
    return ((iota((1, RANKS), 1) // RANK) == which).astype(F32)


def allowed_bias(meta, at):
    t = iota((SEQ, SEQ), 0)
    u = iota((SEQ, SEQ), 1)
    ok = t >= u
    for j in range(2):
        start, end = meta[at + 2 * j], meta[at + 2 * j + 1]
        ok = ok | ((t >= start) & (t < end) & (u >= start) & (u < end))
    return jnp.concatenate([ok, ok], axis=0)


def split_heads(v):
    low = (iota((1, LANES), 1) < HEAD).astype(v.dtype)
    return jnp.concatenate([v * low, v * (1 - low).astype(v.dtype)], axis=0)


def join_heads(v):
    low = iota((SEQ, LANES), 1) < HEAD
    return jnp.where(low, v[:SEQ], v[SEQ:])


def attn_forward_body(
    micro, n_src, meta, hid, cos_ref, sin_ref, gain_a, gain_m, sid_row, *refs
):
    pieces = refs[:n_src]
    qkv, attended, ranks, resid, lse, send, wall_ref, sems = refs[n_src:]
    copies = load_wall(pieces, wall_ref, sems, meta, 0)
    wall = AttnWall(wall_ref, n_src)
    at_id = n_src + 1 + micro
    at_span = n_src + 3 + 4 * micro
    hidden = hid[0, 0].astype(F32)
    scale = lax.rsqrt(jnp.mean(hidden * hidden, axis=-1, keepdims=True) + EPS)
    normed = (hidden * scale * gain_a[...]).astype(BF)
    mask = rank_mask(meta[at_id])
    ok = allowed_bias(meta, at_span)
    cos, sin = cos_ref[...], sin_ref[...]
    for copy in copies:
        copy.wait()
    proj = dot(normed, wall.a_qkv())
    ranks_in = [(proj[:, j * RANKS : (j + 1) * RANKS] * mask).astype(BF) for j in range(3)]
    for j in range(3):
        ranks[:, j * RANKS : (j + 1) * RANKS] = ranks_in[j]
    for j in range(3):
        for pair in range(3):
            at = j * 6 + pair * 2
            part = dot(normed, wall.qkv(at, 2)) + dot(ranks_in[j], wall.b_qkv(at, 2))
            for half in range(2):
                one = part[:, half * LANES : (half + 1) * LANES]
                if j < 2:
                    one = turn(one, cos, sin)
                qkv[:, (at + half) * LANES : (at + half + 1) * LANES] = one.astype(BF)
    lse_cols = []
    for pair in range(6):
        query = qkv[:, pair * LANES : (pair + 1) * LANES]
        key = qkv[:, (6 + pair) * LANES : (7 + pair) * LANES]
        value = qkv[:, (12 + pair) * LANES : (13 + pair) * LANES]
        scores = jnp.where(ok, dot_nt(split_heads(query), key) * (1.0 / math.sqrt(HEAD)), NEG)
        top = jnp.max(scores, axis=-1, keepdims=True)
        expo = jnp.exp(scores - top)
        total = jnp.sum(expo, axis=-1, keepdims=True)
        probs = (expo * (1.0 / total)).astype(BF)
        attended[:, pair * LANES : (pair + 1) * LANES] = join_heads(dot(probs, value)).astype(BF)
        logs = top + jnp.log(total)
        lse[:, pair : pair + 1] = logs
    mixed = attended[...]
    ranks_out = (dot(mixed, wall.a_out()) * mask).astype(BF)
    ranks[:, 3 * RANKS :] = ranks_out
    out = hidden + dot(mixed, wall.w_out()) + dot(ranks_out, wall.b_out())
    resid[...] = out
    scale_m = lax.rsqrt(jnp.mean(out * out, axis=-1, keepdims=True) + EPS)
    lowered = (out * scale_m * gain_m[...]).astype(BF)
    sids = sid_row[0]
    at = iota((SLOTS, SEQ), 0)
    table = ((at == sids[0:1, :]) | (at == sids[1:2, :])).astype(F32).astype(BF)
    send[...] = dot(table, lowered).astype(BF).reshape(FFN_EXPERTS, CAP, D)


class ExpertWall:
    def __init__(self, wall, n_src):
        self.wall = wall
        self.n_src = n_src
        self.rows = D // n_src
        self.ff = FF // n_src
        self.low = RANKS // n_src
        self.down_at = (GU_BLOCKS + AGU_BLOCKS) * self.rows
        self.rank_at = self.down_at + (DOWN_BLOCKS + 1) * self.ff

    def block(self, j):
        start = j * self.rows
        if not isinstance(j, int):
            start = pl.multiple_of(start, self.rows)
        return self.wall[:, pl.ds(start, self.rows), :].reshape(D, LANES)

    def gate_up(self, j, count):
        return lanes_cat([self.block(j + i) for i in range(count)])

    def a_gate_up(self):
        return lanes_cat([self.block(GU_BLOCKS + i) for i in range(AGU_BLOCKS)])

    def rank_block(self, j):
        start = self.rank_at + j * self.low
        if not isinstance(j, int):
            start = pl.multiple_of(start, self.low)
        return self.wall[:, pl.ds(start, self.low), :].reshape(RANKS, LANES)

    def b_gate_up(self, j, count):
        return lanes_cat([self.rank_block(j + i) for i in range(count)])

    def b_down(self):
        return lanes_cat([self.rank_block(GU_BLOCKS + i) for i in range(DOWN_BLOCKS)])

    def down(self, src, count):
        return lanes_cat(
            [
                self.wall[
                    pl.ds(src, count), self.down_at + i * self.ff : self.down_at + (i + 1) * self.ff, :
                ].reshape(count * self.ff, LANES)
                for i in range(DOWN_BLOCKS)
            ]
        )

    def a_down(self, src, count):
        start = self.down_at + DOWN_BLOCKS * self.ff
        return self.wall[pl.ds(src, count), start : start + self.ff, :].reshape(
            count * self.ff, LANES
        )


CHUNK = 512


def expert_body(n_src, carried, meta, tin, dyp, route_w, *refs):
    if carried:
        before, refs = refs[0], refs[1:]
    pieces = refs[:n_src]
    fo, dtin, *refs = refs[n_src:]
    if carried:
        kept, away, *refs = refs
        *refs, grads = refs
        wall_ref, sems, fo_acc, dt_acc, pd_acc, dug_acc, *more = refs
    else:
        grads, wall_ref, sems, fo_acc, dt_acc, pd_acc, dug_acc = refs
    copies = load_wall(pieces, wall_ref, sems, meta, 0)
    wall = ExpertWall(wall_ref, n_src)
    if carried:
        earlier = pltpu.make_async_copy(before, more[0], more[1])
        earlier.start()
    own = meta[n_src]
    tokens = tin[...].reshape(SLOTS, D)
    cot = packet_rows(dyp).astype(F32)
    cols = jnp.concatenate(
        [dyp[s, BLOCKS * CAP :, :].astype(F32).T[:CAP] for s in range(FFN_EXPERTS)], axis=0
    )
    logits = exact_dot(tokens.astype(F32), route_w[...])
    lane = iota((SLOTS, LANES), 1)
    gap = jnp.sum(
        jnp.where(lane == own, logits, 0.0)
        - jnp.where(lane == cols[:, 3:4].astype(jnp.int32), logits, 0.0),
        axis=1,
        keepdims=True,
    )
    gate = sigmoid(gap - (cols[:, 0:1] + cols[:, 1:2] + cols[:, 2:3]))
    mask = ((lane // RANK) == cols[:, 4:5].astype(jnp.int32)).astype(F32)
    d_out = (cot * gate).astype(BF)
    for copy in copies:
        copy.wait()

    a_gu = wall.a_gate_up()
    proj = dot(tokens, a_gu)
    ranks_in = [(proj[:, j * RANKS : (j + 1) * RANKS] * mask).astype(BF) for j in range(2)]
    d_ranks_down = (dot_nt(d_out, wall.b_down()) * mask).astype(BF)
    fo_acc[...] = jnp.zeros_like(fo_acc)
    dt_acc[...] = jnp.zeros_like(dt_acc)
    pd_acc[...] = jnp.zeros_like(pd_acc)
    dug_acc[...] = jnp.zeros_like(dug_acc)
    blocks = CHUNK // LANES
    srcs = max(1, CHUNK // wall.ff)
    gb_at = AGU_BLOCKS * wall.rows
    ad_at = gb_at + GU_BLOCKS * wall.low
    bd_at = ad_at + wall.ff

    def step(f, carry):
        j = f * blocks
        wg = wall.gate_up(j, blocks)
        wu = wall.gate_up(j + GU_BLOCKS // 2, blocks)
        bg = wall.b_gate_up(j, blocks)
        bu = wall.b_gate_up(j + GU_BLOCKS // 2, blocks)
        wd = wall.down(f * srcs, srcs)
        ad = wall.a_down(f * srcs, srcs)
        g = dot(tokens, wg) + dot(ranks_in[0], bg)
        u = dot(tokens, wu) + dot(ranks_in[1], bu)
        d_hidden = dot_nt(d_out, wd) + dot_nt(d_ranks_down, ad)
        sg = sigmoid(g)
        act = g * sg
        hidden = (act * u).astype(BF)
        d_gate = (d_hidden * u * (sg * (1.0 + g * (1.0 - sg)))).astype(BF)
        d_up = (d_hidden * act).astype(BF)
        fo_acc[...] += dot(hidden, wd)
        pd_acc[...] += dot(hidden, ad)
        dt_acc[...] += dot_nt(d_gate, wg) + dot_nt(d_up, wu)
        dug_acc[:, :RANKS] += dot_nt(d_gate, bg)
        dug_acc[:, RANKS:] += dot_nt(d_up, bu)
        for k, (rank, grad) in enumerate(((ranks_in[0], d_gate), (ranks_in[1], d_up))):
            part = dot_tn(rank, grad)
            for i in range(blocks):
                at = gb_at + (j + k * (GU_BLOCKS // 2) + i) * wall.low
                rows = pl.ds(at if isinstance(at, int) else pl.multiple_of(at, 8), wall.low)
                one = part[:, i * LANES : (i + 1) * LANES].reshape(n_src, wall.low, LANES)
                grads[:, rows, :] = one
        part = dot_tn(hidden, d_ranks_down).reshape(srcs, wall.ff, LANES)
        grads[pl.ds(f * srcs, srcs), ad_at : ad_at + wall.ff, :] = part
        return carry

    if wall.low % 8:
        for f in range(FF // CHUNK):
            step(f, 0)
    else:
        lax.fori_loop(0, FF // CHUNK, step, 0)
    ranks_down = (pd_acc[...] * mask).astype(BF)
    result = (fo_acc[...] + dot(ranks_down, wall.b_down())).astype(BF)
    along = jnp.sum(cot * result.astype(F32), axis=1, keepdims=True)
    parts = three_parts(along)
    along = jnp.where(lane == 0, parts[0], jnp.where(lane == 1, parts[1], 0.0))
    along = jnp.where(lane == 2, parts[2], along).astype(BF)
    eye = (iota((CAP, LANES), 0) == iota((CAP, LANES), 1)).astype(F32).astype(BF)
    fo[...] = result.reshape(FFN_EXPERTS, CAP, D)
    for r in range(FFN_EXPERTS):
        side = dot_tn(along[r * CAP : (r + 1) * CAP], eye)[:SIDE]
        dtin[r, BLOCKS * CAP :, :] = side.astype(BF)
    part = dot_tn(ranks_down, d_out)
    for i in range(DOWN_BLOCKS):
        grads[:, bd_at + i * wall.low : bd_at + (i + 1) * wall.low, :] = part[
            :, i * LANES : (i + 1) * LANES
        ].reshape(n_src, wall.low, LANES)
    d_ranks = [(dug_acc[:, k * RANKS : (k + 1) * RANKS] * mask).astype(BF) for k in range(2)]
    both = lanes_cat(d_ranks)
    d_tokens = (dt_acc[...] + dot_nt(both, a_gu)).astype(BF)
    for r in range(FFN_EXPERTS):
        put_packet(dtin, r, d_tokens[r * CAP : (r + 1) * CAP])
    part = dot_tn(tokens, both)
    for i in range(AGU_BLOCKS):
        grads[:, i * wall.rows : (i + 1) * wall.rows, :] = part[
            :, i * LANES : (i + 1) * LANES
        ].reshape(n_src, wall.rows, LANES)
    if carried:
        earlier.wait()
        split_sums(grads, more[0], meta[n_src + 1], kept, away)


def split_sums(grads, before, core, keep, away):
    for i in range(keep.shape[0]):
        mine, theirs = pl.ds(2 * i + core, 1), pl.ds(2 * i + 1 - core, 1)
        keep[i : i + 1] = grads[mine] + before[mine]
        away[i : i + 1] = (grads[theirs] + before[theirs]).astype(BF)


def halves_body(meta, kept, got, keep, away):
    half = keep.shape[0]
    mine, theirs = pl.ds(meta[0] * half, half), pl.ds((1 - meta[0]) * half, half)
    keep[...] = kept[mine] + got[mine].astype(F32)
    away[...] = (kept[theirs] + got[theirs].astype(F32)).astype(BF)


def attn_backward_body(micro, n_src, carried, meta, hid, cot, resid_ref, qkv, attended, ranks, lse,
                       dtin, tok, sid_col, gain_a, gain_m, route_w, consts, cos_ref, sin_ref,
                       *refs):
    if carried:
        before, refs = refs[0], refs[1:]
    pieces = refs[:n_src]
    base, gates, grad_in, *refs = refs[n_src:]
    if carried:
        kept, away, *refs = refs
        *refs, grads = refs
        wall_ref, sems, dqkv, *more = refs
    else:
        grads, wall_ref, sems, dqkv = refs
    copies = load_wall(pieces, wall_ref, sems, meta, 0)
    if carried:
        earlier = pltpu.make_async_copy(before, more[0], more[1])
        earlier.start()
    wall = AttnWall(wall_ref, n_src)
    at_id = n_src + 1 + micro
    at_span = n_src + 3 + 4 * micro
    mask = rank_mask(meta[at_id])
    resid = resid_ref[...]
    dy = cot[0, 0].astype(F32)
    scale_m = lax.rsqrt(jnp.mean(resid * resid, axis=-1, keepdims=True) + EPS)
    gain = gain_m[...]
    normed = resid * scale_m * gain
    lowered = normed.astype(BF).astype(F32)
    weights = route_w[...]
    scores = exact_dot(lowered, weights)
    token = tok[0]
    lane = iota((SEQ, LANES), 1)
    route = [token[:, 16 + k : 17 + k].astype(jnp.int32) for k in range(2)]
    logits = scores + token
    chosen = [
        jnp.sum(jnp.where(lane == route[k], logits, 0.0), axis=1, keepdims=True) for k in range(2)
    ]
    gate = [sigmoid(chosen[k] - chosen[1 - k]) for k in range(2)]
    keep = [sigmoid(scores[:, 12 + j : 13 + j]) for j in range(2)]
    slot = iota((SEQ, SLOTS), 1)
    hits = [(slot == sid_col[0][:, k : k + 1]).astype(F32).astype(BF) for k in range(2)]
    spread = iota((SEQ, FFN_EXPERTS * LANES), 1)
    spread = jnp.where(spread % LANES < CAP, spread // LANES * CAP + spread % LANES, -2)
    side = lanes_cat([dtin[e, BLOCKS * CAP :, :] for e in range(FFN_EXPERTS)])
    along = []
    for k in range(2):
        found = (spread == sid_col[0][:, k : k + 1]).astype(F32).astype(BF)
        parts = dot_nt(found, side)
        along.append(parts[:, 0:1] + parts[:, 1:2] + parts[:, 2:3])
    value = [consts[j : j + 1, :] for j in range(2)]
    is_copy = [(route[k] == FFN_EXPERTS + 1).astype(F32) for k in range(2)]
    is_const = [
        [(route[k] == FFN_EXPERTS + 2 + j).astype(F32) for j in range(2)] for k in range(2)
    ]
    share = sum(
        gate[k] * (is_copy[k] + is_const[k][0] * keep[0] + is_const[k][1] * keep[1])
        for k in range(2)
    )
    named = [gate[0] * is_const[0][j] + gate[1] * is_const[1][j] for j in range(2)]
    out = resid + share * normed
    out = out + (named[0] * (1.0 - keep[0])) * value[0] + (named[1] * (1.0 - keep[1])) * value[1]
    base[...] = out
    gates[...] = jnp.where(lane == 0, gate[0], jnp.where(lane == 1, gate[1], 0.0))
    dy_normed = jnp.sum(dy * normed, axis=1, keepdims=True)
    dy_value = [jnp.sum(dy * value[j], axis=1, keepdims=True) for j in range(2)]
    d_gate = []
    for k in range(2):
        one = along[k] + is_copy[k] * dy_normed
        for j in range(2):
            one = one + is_const[k][j] * (keep[j] * dy_normed + (1.0 - keep[j]) * dy_value[j])
        d_gate.append(one)
    centre = gate[0] * d_gate[0] + gate[1] * d_gate[1]
    d_logits = jnp.zeros((SEQ, LANES), F32)
    for k in range(2):
        d_logits = d_logits + jnp.where(lane == route[k], gate[k] * (d_gate[k] - centre), 0.0)
    for j in range(2):
        d_keep = named[j] * (dy_normed - dy_value[j])
        d_logits = d_logits + jnp.where(
            lane == 12 + j, d_keep * keep[j] * (1.0 - keep[j]), 0.0
        )
    d_normed = share * dy + exact_dot_nt(d_logits, weights)
    d_normed = d_normed + dot(hits[0] + hits[1], packet_rows(dtin))
    scaled = gain * d_normed
    d_resid = (
        dy
        + scale_m * scaled
        - resid * (scale_m * scale_m * scale_m) * jnp.mean(scaled * resid, axis=-1, keepdims=True)
    )
    d_branch = d_resid.astype(BF)
    for copy in copies:
        copy.wait()
    d_ranks_out = (dot_nt(d_branch, wall.b_out()) * mask).astype(BF)
    d_mixed = (dot_nt(d_branch, wall.w_out()) + dot_nt(d_ranks_out, wall.a_out())).astype(BF)
    a_rows, b_rows = wall.rows, wall.low
    gb_at = AQKV_BLOCKS * a_rows
    ao_at = gb_at + QKV_BLOCKS * b_rows
    bo_at = ao_at + a_rows
    part = dot_tn(ranks[:, 3 * RANKS :], d_branch)
    for i in range(OUT_BLOCKS):
        grads[:, bo_at + i * b_rows : bo_at + (i + 1) * b_rows, :] = part[
            :, i * LANES : (i + 1) * LANES
        ].reshape(n_src, b_rows, LANES)
    grads[:, ao_at : ao_at + a_rows, :] = dot_tn(attended[...], d_ranks_out).reshape(
        n_src, a_rows, LANES
    )
    ok = allowed_bias(meta, at_span)
    cos, sin = cos_ref[...], -sin_ref[...]
    inv = 1.0 / math.sqrt(HEAD)
    for pair in range(6):
        query = split_heads(qkv[:, pair * LANES : (pair + 1) * LANES])
        key = qkv[:, (6 + pair) * LANES : (7 + pair) * LANES]
        val = qkv[:, (12 + pair) * LANES : (13 + pair) * LANES]
        d_heads = split_heads(d_mixed[:, pair * LANES : (pair + 1) * LANES])
        sc = jnp.where(ok, dot_nt(query, key) * inv, NEG)
        probs = jnp.exp(sc - lse[:, pair : pair + 1])
        d_probs = dot_nt(d_heads, val)
        row_dot = jnp.sum(probs * d_probs, axis=-1, keepdims=True)
        d_scores = (probs * (d_probs - row_dot)).astype(BF)
        d_query = join_heads(dot(d_scores, key)) * inv
        d_key = dot_tn(d_scores, query) * inv
        d_value = dot_tn(probs.astype(BF), d_heads)
        dqkv[:, pair * LANES : (pair + 1) * LANES] = turn(d_query, cos, sin).astype(BF)
        dqkv[:, (6 + pair) * LANES : (7 + pair) * LANES] = turn(d_key, cos, sin).astype(BF)
        dqkv[:, (12 + pair) * LANES : (13 + pair) * LANES] = d_value.astype(BF)
    hidden = hid[0, 0].astype(F32)
    scale = lax.rsqrt(jnp.mean(hidden * hidden, axis=-1, keepdims=True) + EPS)
    first = gain_a[...]
    normed_low = (hidden * scale * first).astype(BF)
    d_in = jnp.zeros((SEQ, D), F32)
    d_ranks = []
    for j in range(3):
        part = dqkv[:, j * D : (j + 1) * D]
        d_ranks.append((dot_nt(part, wall.b_qkv(j * 6, 6)) * mask).astype(BF))
        d_in = d_in + dot_nt(part, wall.qkv(j * 6, 6))
        gb = dot_tn(ranks[:, j * RANKS : (j + 1) * RANKS], part)
        for i in range(6):
            at = gb_at + (j * 6 + i) * b_rows
            grads[:, at : at + b_rows, :] = gb[:, i * LANES : (i + 1) * LANES].reshape(
                n_src, b_rows, LANES
            )
    ranks_all = lanes_cat(d_ranks)
    d_in = d_in + dot_nt(ranks_all, wall.a_qkv())
    ga = dot_tn(normed_low, ranks_all)
    for i in range(3):
        grads[:, i * a_rows : (i + 1) * a_rows, :] = ga[:, i * LANES : (i + 1) * LANES].reshape(
            n_src, a_rows, LANES
        )
    scaled = first * d_in
    grad_in[...] = (
        d_resid
        + scale * scaled
        - hidden * (scale * scale * scale) * jnp.mean(scaled * hidden, axis=-1, keepdims=True)
    )
    if carried:
        earlier.wait()
        split_sums(grads, more[0], meta[n_src], kept, away)


def output_body(micros, meta, *refs):
    sid_col, outs = refs[3 * micros], refs[3 * micros + 1 :]
    slot = iota((SEQ, SLOTS), 1)
    for micro in range(micros):
        total, gates, fo = (refs[3 * micro + i][...] for i in range(3))
        for k in range(2):
            hits = (slot == sid_col[micro, :, k : k + 1]).astype(F32).astype(BF)
            total = total + gates[:, k : k + 1] * dot(hits, fo.reshape(SLOTS, D))
        outs[micro][...] = total.astype(BF)


def flip(values, axis, bit, size):
    return lax.ppermute(values, axis, [(i, i ^ bit) for i in range(size)])


def later(values, others):
    return lax.optimization_barrier((values, others))[0]


def bits(size):
    return [1 << i for i in range(size.bit_length() - 1)]


def next_half(kept, got, side):
    half = (kept.shape[0] // 2,) + kept.shape[1:]
    return call(
        halves_body,
        side.reshape(1).astype(jnp.int32),
        (kept, got),
        [whole(kept.shape), whole(got.shape)],
        [shape(half, F32), shape(half, BF)],
        us=2,
    )


def sums_scratch(dims):
    return [pltpu.VMEM(dims, F32), pltpu.SemaphoreType.DMA, pltpu.VMEM(dims, F32)]


def body(members, hidden_in, prev_logits, routes, adapter_ids, image_spans, cotangent, gain_attn,
         gain_moe, router_weight, const_gate, const_value, w_qkv, w_out, a_qkv, b_qkv, a_out, b_out,
         w_gate_up, w_down, a_gate_up, b_gate_up, a_down, b_down):
    rest = lax.axis_size("y")
    peers = lax.axis_size("z")
    n_src = rest * members * 2
    micros = hidden_in.shape[0]
    y, x, c, z = (lax.axis_index(name) for name in ("y", "x", "c", "z"))
    place = (y * members + x) * 2 + c

    attn_rows = (QKV_BLOCKS + AQKV_BLOCKS + OUT_BLOCKS + 1) * (D // n_src) + (
        QKV_BLOCKS + OUT_BLOCKS
    ) * (RANKS // n_src)
    expert_rows = (
        (GU_BLOCKS + AGU_BLOCKS) * (D // n_src)
        + (DOWN_BLOCKS + 1) * (FF // n_src)
        + (GU_BLOCKS + DOWN_BLOCKS) * (RANKS // n_src)
    )
    none = jnp.zeros((1,), jnp.int32)
    args = (w_qkv, a_qkv, w_out, a_out, b_qkv, b_out)
    (attn_own,) = call(
        pack_attn_body,
        none,
        args,
        [whole(a.shape) for a in args],
        [shape((attn_rows, LANES), BF)],
        us=2,
    )
    tok = jnp.concatenate(
        [
            prev_logits[:, 0],
            jnp.zeros((micros, SEQ, 4), F32),
            routes[:, 0].astype(F32),
            jnp.zeros((micros, SEQ, LANES - 18), F32),
        ],
        axis=2,
    )
    route_w = jnp.concatenate(
        [router_weight, const_gate, jnp.zeros((D, LANES - 14), F32)], axis=1
    )
    half = HEAD // 2
    freqs = jnp.exp(jnp.arange(half, dtype=F32) * (-2.0 * math.log(10000.0) / HEAD))
    angles = jnp.arange(SEQ, dtype=F32)[:, None] * freqs[None, :]
    cos = jnp.tile(jnp.cos(angles), (1, 4))
    sin = jnp.sin(angles)
    sin = jnp.tile(jnp.concatenate([-sin, sin], axis=1), (1, 2))
    gain_a = gain_attn.reshape(1, D)
    gain_m = gain_moe.reshape(1, D)

    packet = shape((FFN_EXPERTS, CAP, D), BF)
    wide_packet = shape((FFN_EXPERTS, WIDE, LANES), BF)
    dy_send, sid_row, sid_col = call(
        functools.partial(slots_body, micros),
        adapter_ids.reshape(-1),
        (tok, cotangent),
        [whole(tok.shape), whole(cotangent.shape)],
        [
            shape((FFN_EXPERTS, micros * WIDE, LANES), BF),
            shape((micros, 8, SEQ), jnp.int32),
            shape((micros, SEQ, 8), jnp.int32),
        ],
        us=4,
        after=(attn_own,),
    )

    args = (w_gate_up, a_gate_up, w_down, a_down, b_gate_up, b_down)
    expert_own = call(
        functools.partial(pack_experts_body, members),
        x.reshape(1).astype(jnp.int32),
        args,
        [whole(a.shape) for a in args],
        [shape((expert_rows, LANES), BF)] * members,
        us=4,
        after=(sid_row,),
    )

    attn_pieces = [(attn_own, 0)]
    for bit in bits(members):
        attn_pieces += [(flip(v, "x", bit, members), m ^ (bit * 2)) for v, m in attn_pieces]
    for bit in bits(rest):
        way = bit * members * 2
        beside = flip(attn_own, "y", bit, rest)
        attn_pieces += [(beside, way)] + [
            (flip(later(v, (sid_row, beside)), "y", bit, rest), m ^ way)
            for v, m in attn_pieces[1:]
        ]
    attn_near, attn_far = attn_pieces[1][0], attn_pieces[-1][0]
    attn_beside = attn_pieces[members][0]
    attn_pieces += [
        (flip(v if v is attn_far else later(v, attn_far), "c", 1, 2), m ^ 1)
        for v, m in attn_pieces
    ]
    attn_bufs = [v for v, m in attn_pieces]
    meta_attn = jnp.concatenate(
        [
            place ^ jnp.array([m for v, m in attn_pieces], jnp.int32),
            c.reshape(1),
            adapter_ids.reshape(-1),
            image_spans.reshape(-1),
        ]
    ).astype(jnp.int32)

    group = ("z", "x") if members > 1 else "z"

    def trade(values):
        return lax.all_to_all(values, group, 0, 0, tiled=True)

    expert_pieces = [(expert_own[0], 0)]
    for rel in range(1, members):
        pairs = [(i, i ^ rel) for i in range(members)]
        away = later(expert_own[rel], attn_near)
        expert_pieces.append((lax.ppermute(away, "x", pairs), rel * 2))
    first = bits(rest)[0]
    own = later(expert_own[0], attn_beside)
    beside = (flip(own, "y", first, rest), first * members * 2)
    near = [[v for v, m in expert_pieces[1:]] + [beside[0]]]

    dy_got = trade(dy_send)
    saved, tin = [], []
    for micro in range(micros):
        args = (hidden_in, cos, sin, gain_a, gain_m, sid_row, *attn_bufs)
        specs = [
            one_micro((1, SEQ, D), micro),
            whole(cos.shape),
            whole(sin.shape),
            whole(gain_a.shape),
            whole(gain_m.shape),
            one_micro((8, SEQ), micro),
        ] + [ANYWHERE] * n_src
        saved.append(
            call(
                functools.partial(attn_forward_body, micro, n_src),
                meta_attn,
                args,
                specs,
                [
                    shape((SEQ, 3 * D), BF),
                    shape((SEQ, D), BF),
                    shape((SEQ, 4 * RANKS), BF),
                    shape((SEQ, D), F32),
                    shape((2 * SEQ, 8), F32),
                    packet,
                ],
                [
                    pltpu.VMEM((n_src, attn_rows, LANES), BF),
                    pltpu.SemaphoreType.DMA((n_src,)),
                ],
                us=FORWARD_HINT,
                after=tuple(near[micro]) if micro < len(near) else (),
            )
        )
        if micro == 0:
            for bit in bits(rest):
                relay = expert_pieces[1:] if bit == first else expert_pieces
                more = [
                    (flip(v, "y", bit, rest), m ^ (bit * members * 2)) for v, m in relay
                ]
                expert_pieces += ([beside] if bit == first else []) + more
        send = saved[micro][5]
        tin.append(trade(send if micro == 0 else later(send, expert_pieces[-1][0])))
    expert_pieces += [
        (flip(later(v, saved[-1][4]), "c", 1, 2), m ^ 1) for v, m in expert_pieces
    ]
    expert_bufs = [v for v, m in expert_pieces]
    meta_expert = jnp.concatenate(
        [
            place ^ jnp.array([m for v, m in expert_pieces], jnp.int32),
            (z * members + x).reshape(1),
            c.reshape(1),
        ]
    ).astype(jnp.int32)

    expert_grad_rows = (
        AGU_BLOCKS * (D // n_src)
        + (GU_BLOCKS + DOWN_BLOCKS) * (RANKS // n_src)
        + FF // n_src
    )
    grads_e = None
    fo_send, dtin = [], []
    for micro in range(micros):
        carried = grads_e is not None
        args = (tin[micro], dy_got, route_w)
        specs = [whole(a.shape) for a in args]
        specs[1] = pl.BlockSpec(
            (FFN_EXPERTS, WIDE, LANES), lambda i, meta, micro=micro: (0, micro, 0)
        )
        if carried:
            args += tuple(grads_e)
            specs.append(ANYWHERE)
        specs += [ANYWHERE] * n_src
        sums = (n_src, expert_grad_rows, LANES)
        halves = (n_src // 2, expert_grad_rows, LANES)
        fo, d_tokens, *grads_e = call(
            functools.partial(expert_body, n_src, carried),
            meta_expert,
            args + tuple(expert_bufs),
            specs,
            [
                packet,
                wide_packet,
            ]
            + ([shape(halves, F32), shape(halves, BF)] if carried else [shape(sums, F32)]),
            [
                pltpu.VMEM((n_src, expert_rows, LANES), BF),
                pltpu.SemaphoreType.DMA((n_src,)),
                pltpu.VMEM((SLOTS, D), F32),
                pltpu.VMEM((SLOTS, D), F32),
                pltpu.VMEM((SLOTS, RANKS), F32),
                pltpu.VMEM((SLOTS, 2 * RANKS), F32),
            ]
            + (sums_scratch(sums) if carried else []),
            us=31,
        )
        fo_send.append(fo)
        dtin.append(trade(d_tokens))

    attn_grad_rows = (AQKV_BLOCKS + 1) * (D // n_src) + (QKV_BLOCKS + OUT_BLOCKS) * (
        RANKS // n_src
    )
    grads_a = None
    mixed, grad_rows = [], []
    for micro in range(micros):
        carried = grads_a is not None
        qkv, attended, ranks, resid, lse = saved[micro][:5]
        args = (hidden_in, cotangent, resid, qkv, attended, ranks, lse, dtin[micro], tok, sid_col,
                gain_a, gain_m, route_w, const_value, cos, sin)
        specs = [whole(a.shape) for a in args]
        specs[0] = one_micro((1, SEQ, D), micro)
        specs[1] = one_micro((1, SEQ, D), micro)
        specs[8] = one_micro((SEQ, LANES), micro)
        specs[9] = one_micro((SEQ, 8), micro)
        if carried:
            args += tuple(grads_a)
            specs.append(ANYWHERE)
        specs += [ANYWHERE] * n_src
        sums = (n_src, attn_grad_rows, LANES)
        halves = (n_src // 2, attn_grad_rows, LANES)
        base, gates, grad_in, *grads_a = call(
            functools.partial(attn_backward_body, micro, n_src, carried),
            meta_attn,
            args + tuple(attn_bufs),
            specs,
            [
                shape((SEQ, D), F32),
                shape((SEQ, LANES), F32),
                shape((SEQ, D), F32),
            ]
            + ([shape(halves, F32), shape(halves, BF)] if carried else [shape(sums, F32)]),
            [
                pltpu.VMEM((n_src, attn_rows, LANES), BF),
                pltpu.SemaphoreType.DMA((n_src,)),
                pltpu.VMEM((SEQ, 3 * D), BF),
            ]
            + (sums_scratch(sums) if carried else []),
            us=19,
            after=(away,) if carried else (),
        )
        grad_rows.append(grad_in)
        mixed.append((base, gates, trade(later(fo_send[micro], base))))
        if not carried:
            kept, away = later(grads_e, base)
            got = flip(away, "c", 1, 2)
            for bit in reversed(bits(rest)):
                kept, away = next_half(kept, got, (y // bit) % 2)
                got = flip(away, "y", bit, rest)
            total = kept + got.astype(F32)
            held = (mixed[0][2], total)
    args = tuple(v for parts in mixed for v in parts) + (sid_col,)
    block_rows = call(
        functools.partial(output_body, micros),
        none,
        args,
        [whole(a.shape) for a in args],
        [shape((SEQ, D), BF)] * micros,
        us=5,
    )
    owned = lax.dynamic_index_in_dim(total, x, 0, keepdims=True)
    for rel in range(1, members):
        away = lax.dynamic_index_in_dim(total, x ^ rel, 0, keepdims=True).astype(BF)
        got = lax.ppermute(away, "x", [(i, i ^ rel) for i in range(members)])
        owned = jnp.concatenate([owned, got.astype(F32)], axis=0)
    if members > 1:
        owned = owned[x ^ jnp.arange(members)]

    def blocks_of(values, row, count, height):
        part = values[:, row : row + count * height].reshape(-1, count, height, LANES)
        return jnp.moveaxis(part, 1, 2).reshape(-1, height, count * LANES)

    rows, low, ff = D // n_src, RANKS // n_src, FF // n_src
    at = 0
    grad_agu = blocks_of(owned, at, AGU_BLOCKS, rows)
    at += AGU_BLOCKS * rows
    grad_bgu = blocks_of(owned, at, GU_BLOCKS, low)
    at += GU_BLOCKS * low
    grad_ad = blocks_of(owned, at, 1, ff)
    at += ff
    grad_bd = blocks_of(owned, at, DOWN_BLOCKS, low)

    kept, away = grads_a
    got = flip(away, "c", 1, 2)
    for axis, place_on, size in (("y", y, rest), ("x", x, members)):
        for bit in reversed(bits(size)):
            kept, away = next_half(kept, got, (place_on // bit) % 2)
            got = flip(away, axis, bit, size)
        if axis == "y":
            kept = later(kept, held)
    total = kept + got.astype(F32)
    for bit in bits(peers):
        sent = total.astype(BF)
        total = sent.astype(F32) + flip(sent, "z", bit, peers).astype(F32)
    at = 0
    grad_aq = blocks_of(total, at, AQKV_BLOCKS, rows)[0]
    at += AQKV_BLOCKS * rows
    grad_bq = blocks_of(total, at, QKV_BLOCKS, low)[0]
    at += QKV_BLOCKS * low
    grad_ao = blocks_of(total, at, 1, rows)[0]
    at += rows
    grad_bo = blocks_of(total, at, OUT_BLOCKS, low)[0]

    return (jnp.stack(block_rows)[:, None], jnp.stack(grad_rows)[:, None], grad_aq, grad_bq,
            grad_ao, grad_bo, grad_agu, grad_bgu, grad_ad, grad_bd)


def solution(mesh):
    dp, expert = mesh.shape["dp"], mesh.shape["expert"]
    members = FFN_EXPERTS // expert
    fine = Mesh(
        mesh.devices.reshape(dp // (2 * members), members, 2, expert), ("y", "x", "c", "z")
    )
    owners = ("y", "x", "c")
    seqs = ("y", "x", "c", "z")
    tokens = P(None, seqs, None, None)
    rows = P(owners, None)
    expert_rows = P("z", owners, None)
    in_specs = (
        (tokens, tokens, tokens, P(None, seqs), tokens, tokens)
        + (P(),) * 5
        + (rows,) * 6
        + (expert_rows,) * 6
    )
    out_specs = (tokens, tokens) + (rows,) * 4 + (expert_rows,) * 4
    return jax.shard_map(
        functools.partial(body, members),
        mesh=fine,
        in_specs=in_specs,
        out_specs=out_specs,
        check_vma=False,
    )
```

```python
import functools
import math

import jax
import jax.numpy as jnp
from jax import lax
from jax.experimental import pallas as pl
from jax.experimental.pallas import tpu as pltpu
from jax.sharding import Mesh
from jax.sharding import PartitionSpec as P

D = 768
HEADS = 12
HEAD = 64
FF = 2048
FFN_EXPERTS = 8
RANK = 16
RANKS = 128
CAP = 80
LANES = 128
SEQ = 256
SLOTS = FFN_EXPERTS * CAP
BLOCKS, SIDE = D // LANES, 8
WIDE = BLOCKS * CAP + SIDE
NEG = -1e30
EPS = 1e-05
BF = jnp.bfloat16
F32 = jnp.float32
VMEM_LIMIT = 60 * 1024 * 1024
FLOPS_PER_US, BYTES_PER_US = 10**9, 10**6
FORWARD_HINT = 12

QKV_BLOCKS, AQKV_BLOCKS, OUT_BLOCKS = 18, 3, 6
GU_BLOCKS, AGU_BLOCKS, DOWN_BLOCKS = 32, 2, 6


def dot(a, b):
    return lax.dot_general(a, b, (((1,), (0,)), ((), ())), preferred_element_type=F32)


def dot_nt(a, b):
    return lax.dot_general(a, b, (((1,), (1,)), ((), ())), preferred_element_type=F32)


def dot_tn(a, b):
    return lax.dot_general(a, b, (((0,), (0,)), ((), ())), preferred_element_type=F32)


def exact_dot(a, b):
    return lax.dot_general(
        a, b, (((1,), (0,)), ((), ())), precision=lax.Precision.HIGHEST, preferred_element_type=F32
    )


def exact_dot_nt(a, b):
    return lax.dot_general(
        a, b, (((1,), (1,)), ((), ())), precision=lax.Precision.HIGHEST, preferred_element_type=F32
    )


def lanes_cat(parts):
    return parts[0] if len(parts) == 1 else jnp.concatenate(parts, axis=1)


def iota(shape, dim):
    return lax.broadcasted_iota(jnp.int32, shape, dim)


def sigmoid(v):
    return 1.0 / (1.0 + jnp.exp(-v))


def whole(shape):
    return pl.BlockSpec(tuple(shape), lambda i, meta: (0,) * len(shape))


def one_micro(shape, micro):
    return pl.BlockSpec((1,) + tuple(shape), lambda i, meta: (micro,) + (0,) * len(shape))


ANYWHERE = pl.BlockSpec(memory_space=pl.ANY)


def call(body, meta, args, specs, outs, scratch=(), us=1, after=()):
    out_specs = [whole(o.shape) for o in outs]

    def late(meta_ref, *refs):
        body(meta_ref, *refs[len(after) :])

    args = tuple(after) + tuple(args)
    specs = [ANYWHERE] * len(after) + list(specs)
    return pl.pallas_call(
        late if after else body,
        out_shape=outs,
        cost_estimate=pl.CostEstimate(
            flops=us * FLOPS_PER_US, transcendentals=0, bytes_accessed=us * BYTES_PER_US
        ),
        grid_spec=pltpu.PrefetchScalarGridSpec(
            num_scalar_prefetch=1,
            grid=(1,),
            in_specs=specs,
            out_specs=out_specs,
            scratch_shapes=list(scratch),
        ),
        compiler_params=pltpu.CompilerParams(
            dimension_semantics=("arbitrary",), vmem_limit_bytes=VMEM_LIMIT
        ),
    )(meta, *args)


def shape(dims, dtype):
    return jax.ShapeDtypeStruct(tuple(dims), dtype)


def put_blocks(out, row, src):
    height, width = src.shape
    for j in range(width // LANES):
        out[row : row + height, :] = src[:, j * LANES : (j + 1) * LANES]
        row += height
    return row


def pack_attn_body(meta, w_qkv, a_qkv, w_out, a_out, b_qkv, b_out, out):
    row = 0
    for ref in (w_qkv, a_qkv, w_out, a_out, b_qkv, b_out):
        row = put_blocks(out, row, ref[...])


def pack_experts_body(rel_shape, meta, w_gu, a_gu, w_down, a_down, b_gu, b_down, *outs):
    for rel in range(rel_shape):
        member = meta[0] ^ rel
        row = 0
        for ref in (w_gu, a_gu, w_down, a_down, b_gu, b_down):
            row = put_blocks(outs[rel], row, ref[member])


def three_parts(v):
    high = v.astype(BF).astype(F32)
    mid = (v - high).astype(BF).astype(F32)
    return [high, mid, v - high - mid]


def put_packet(out, e, rows, at=0):
    for j in range(BLOCKS):
        out[e, at + j * CAP : at + (j + 1) * CAP, :] = rows[:, j * LANES : (j + 1) * LANES]


def packet_rows(packets):
    return lanes_cat(
        [packets[:, j * CAP : (j + 1) * CAP, :].reshape(SLOTS, LANES) for j in range(BLOCKS)]
    )


def slots_body(micros, meta, tok, cot, *refs):
    dy, sid_row, sid_col = refs
    strict = (iota((SEQ, SEQ), 0) < iota((SEQ, SEQ), 1)).astype(BF)
    experts = iota((FFN_EXPERTS, SEQ), 0)
    for micro in range(micros):
        turned = tok[micro].T
        route = [turned[16 + k : 17 + k, :].astype(jnp.int32) for k in range(2)]
        hot = [(experts == route[k]).astype(F32) for k in range(2)]
        before = dot((hot[0] + hot[1]).astype(BF), strict)
        sids = []
        for k in range(2):
            rank = jnp.sum(before * hot[k], axis=0, keepdims=True).astype(jnp.int32)
            sids.append(jnp.where(route[k] < FFN_EXPERTS, route[k] * CAP + rank, -1))
        rows = jnp.concatenate(sids + [jnp.zeros((6, SEQ), jnp.int32)], axis=0)
        sid_row[micro] = rows
        sid_col[micro] = rows.astype(F32).T.astype(jnp.int32)
        all_routes = iota((16, SEQ), 0)
        prev = turned[0:16, :]
        named = [
            jnp.sum(jnp.where(all_routes == route[k], prev, 0.0), axis=0, keepdims=True)
            for k in range(2)
        ]
        fields = [
            jnp.concatenate(
                three_parts(named[1 - k] - named[k])
                + [route[1 - k].astype(F32), jnp.zeros((SIDE - 4, SEQ), F32)],
                axis=0,
            ).astype(BF)
            for k in range(2)
        ]
        at = iota((FFN_EXPERTS * LANES, SEQ), 0)
        at = jnp.where(at % LANES < CAP, at // LANES * CAP + at % LANES, -2)
        hits = [(at == sids[k]).astype(F32).astype(BF) for k in range(2)]
        side = dot_nt(fields[0], hits[0]) + dot_nt(fields[1], hits[1])
        own_id = jnp.full((SIDE, LANES), 1.0, F32) * meta[micro].astype(F32)
        slot = iota((SLOTS, SEQ), 0)
        table = ((slot == sids[0]) | (slot == sids[1])).astype(F32).astype(BF)
        rows = dot(table, cot[micro, 0]).astype(BF)
        fourth = iota((SIDE, LANES), 0) == 4
        for e in range(FFN_EXPERTS):
            put_packet(dy, e, rows[e * CAP : (e + 1) * CAP], micro * WIDE)
            one = jnp.where(fourth, own_id, side[:, e * LANES : (e + 1) * LANES])
            dy[e, micro * WIDE + BLOCKS * CAP : (micro + 1) * WIDE, :] = one.astype(BF)


def load_wall(pieces, wall, sems, meta, first):
    copies = [
        pltpu.make_async_copy(piece, wall.at[meta[first + i]], sems.at[i])
        for i, piece in enumerate(pieces)
    ]
    for copy in copies:
        copy.start()
    return copies


class AttnWall:
    def __init__(self, wall, n_src):
        self.wall = wall
        self.n_src = n_src
        self.rows = D // n_src
        self.low = RANKS // n_src
        self.base = (QKV_BLOCKS + AQKV_BLOCKS + OUT_BLOCKS + 1) * self.rows

    def block(self, j, count=1):
        return lanes_cat(
            [
                self.wall[:, (j + i) * self.rows : (j + i + 1) * self.rows, :].reshape(D, LANES)
                for i in range(count)
            ]
        )

    def rank_block(self, j, count=1):
        return lanes_cat(
            [
                self.wall[
                    :, self.base + (j + i) * self.low : self.base + (j + i + 1) * self.low, :
                ].reshape(RANKS, LANES)
                for i in range(count)
            ]
        )

    def qkv(self, j, count=1):
        return self.block(j, count)

    def a_qkv(self, j=0, count=3):
        return self.block(QKV_BLOCKS + j, count)

    def w_out(self):
        return self.block(QKV_BLOCKS + AQKV_BLOCKS, OUT_BLOCKS)

    def a_out(self):
        return self.block(QKV_BLOCKS + AQKV_BLOCKS + OUT_BLOCKS)

    def b_qkv(self, j, count=1):
        return self.rank_block(j, count)

    def b_out(self):
        return self.rank_block(QKV_BLOCKS, OUT_BLOCKS)


def turn(v, cos, sin):
    ahead = pltpu.roll(v, LANES - HEAD // 2, axis=1)
    behind = pltpu.roll(v, HEAD // 2, axis=1)
    first = (iota(v.shape, 1) % HEAD) < HEAD // 2
    return v * cos + jnp.where(first, ahead, behind) * sin


def rank_mask(which):
    return ((iota((1, RANKS), 1) // RANK) == which).astype(F32)


def allowed_bias(meta, at):
    t = iota((SEQ, SEQ), 0)
    u = iota((SEQ, SEQ), 1)
    ok = t >= u
    for j in range(2):
        start, end = meta[at + 2 * j], meta[at + 2 * j + 1]
        ok = ok | ((t >= start) & (t < end) & (u >= start) & (u < end))
    return jnp.concatenate([ok, ok], axis=0)


def split_heads(v):
    low = (iota((1, LANES), 1) < HEAD).astype(v.dtype)
    return jnp.concatenate([v * low, v * (1 - low).astype(v.dtype)], axis=0)


def join_heads(v):
    low = iota((SEQ, LANES), 1) < HEAD
    return jnp.where(low, v[:SEQ], v[SEQ:])


def attn_forward_body(
    micro, n_src, meta, hid, cos_ref, sin_ref, gain_a, gain_m, sid_row, *refs
):
    pieces = refs[:n_src]
    qkv, attended, ranks, resid, lse, send, wall_ref, sems = refs[n_src:]
    copies = load_wall(pieces, wall_ref, sems, meta, 0)
    wall = AttnWall(wall_ref, n_src)
    at_id = n_src + 1 + micro
    at_span = n_src + 3 + 4 * micro
    hidden = hid[0, 0].astype(F32)
    scale = lax.rsqrt(jnp.mean(hidden * hidden, axis=-1, keepdims=True) + EPS)
    normed = (hidden * scale * gain_a[...]).astype(BF)
    mask = rank_mask(meta[at_id])
    ok = allowed_bias(meta, at_span)
    cos, sin = cos_ref[...], sin_ref[...]
    for copy in copies:
        copy.wait()
    proj = dot(normed, wall.a_qkv())
    ranks_in = [(proj[:, j * RANKS : (j + 1) * RANKS] * mask).astype(BF) for j in range(3)]
    for j in range(3):
        ranks[:, j * RANKS : (j + 1) * RANKS] = ranks_in[j]
    for j in range(3):
        for pair in range(3):
            at = j * 6 + pair * 2
            part = dot(normed, wall.qkv(at, 2)) + dot(ranks_in[j], wall.b_qkv(at, 2))
            for half in range(2):
                one = part[:, half * LANES : (half + 1) * LANES]
                if j < 2:
                    one = turn(one, cos, sin)
                qkv[:, (at + half) * LANES : (at + half + 1) * LANES] = one.astype(BF)
    lse_cols = []
    for pair in range(6):
        query = qkv[:, pair * LANES : (pair + 1) * LANES]
        key = qkv[:, (6 + pair) * LANES : (7 + pair) * LANES]
        value = qkv[:, (12 + pair) * LANES : (13 + pair) * LANES]
        scores = jnp.where(ok, dot_nt(split_heads(query), key) * (1.0 / math.sqrt(HEAD)), NEG)
        top = jnp.max(scores, axis=-1, keepdims=True)
        expo = jnp.exp(scores - top)
        total = jnp.sum(expo, axis=-1, keepdims=True)
        probs = (expo * (1.0 / total)).astype(BF)
        attended[:, pair * LANES : (pair + 1) * LANES] = join_heads(dot(probs, value)).astype(BF)
        logs = top + jnp.log(total)
        lse[:, pair : pair + 1] = logs
    mixed = attended[...]
    ranks_out = (dot(mixed, wall.a_out()) * mask).astype(BF)
    ranks[:, 3 * RANKS :] = ranks_out
    out = hidden + dot(mixed, wall.w_out()) + dot(ranks_out, wall.b_out())
    resid[...] = out
    scale_m = lax.rsqrt(jnp.mean(out * out, axis=-1, keepdims=True) + EPS)
    lowered = (out * scale_m * gain_m[...]).astype(BF)
    sids = sid_row[0]
    at = iota((SLOTS, SEQ), 0)
    table = ((at == sids[0:1, :]) | (at == sids[1:2, :])).astype(F32).astype(BF)
    send[...] = dot(table, lowered).astype(BF).reshape(FFN_EXPERTS, CAP, D)


class ExpertWall:
    def __init__(self, wall, n_src):
        self.wall = wall
        self.n_src = n_src
        self.rows = D // n_src
        self.ff = FF // n_src
        self.low = RANKS // n_src
        self.down_at = (GU_BLOCKS + AGU_BLOCKS) * self.rows
        self.rank_at = self.down_at + (DOWN_BLOCKS + 1) * self.ff

    def block(self, j):
        start = j * self.rows
        if not isinstance(j, int):
            start = pl.multiple_of(start, self.rows)
        return self.wall[:, pl.ds(start, self.rows), :].reshape(D, LANES)

    def gate_up(self, j, count):
        return lanes_cat([self.block(j + i) for i in range(count)])

    def a_gate_up(self):
        return lanes_cat([self.block(GU_BLOCKS + i) for i in range(AGU_BLOCKS)])

    def rank_block(self, j):
        start = self.rank_at + j * self.low
        if not isinstance(j, int):
            start = pl.multiple_of(start, self.low)
        return self.wall[:, pl.ds(start, self.low), :].reshape(RANKS, LANES)

    def b_gate_up(self, j, count):
        return lanes_cat([self.rank_block(j + i) for i in range(count)])

    def b_down(self):
        return lanes_cat([self.rank_block(GU_BLOCKS + i) for i in range(DOWN_BLOCKS)])

    def down(self, src, count):
        return lanes_cat(
            [
                self.wall[
                    pl.ds(src, count), self.down_at + i * self.ff : self.down_at + (i + 1) * self.ff, :
                ].reshape(count * self.ff, LANES)
                for i in range(DOWN_BLOCKS)
            ]
        )

    def a_down(self, src, count):
        start = self.down_at + DOWN_BLOCKS * self.ff
        return self.wall[pl.ds(src, count), start : start + self.ff, :].reshape(
            count * self.ff, LANES
        )


CHUNK = 512


def expert_body(n_src, carried, meta, tin, dyp, route_w, *refs):
    if carried:
        before, refs = refs[0], refs[1:]
    pieces = refs[:n_src]
    fo, dtin, *refs = refs[n_src:]
    if carried:
        kept, away, *refs = refs
        *refs, grads = refs
        wall_ref, sems, fo_acc, dt_acc, pd_acc, dug_acc, *more = refs
    else:
        grads, wall_ref, sems, fo_acc, dt_acc, pd_acc, dug_acc = refs
    copies = load_wall(pieces, wall_ref, sems, meta, 0)
    wall = ExpertWall(wall_ref, n_src)
    if carried:
        earlier = pltpu.make_async_copy(before, more[0], more[1])
        earlier.start()
    own = meta[n_src]
    tokens = tin[...].reshape(SLOTS, D)
    cot = packet_rows(dyp).astype(F32)
    cols = jnp.concatenate(
        [dyp[s, BLOCKS * CAP :, :].astype(F32).T[:CAP] for s in range(FFN_EXPERTS)], axis=0
    )
    logits = exact_dot(tokens.astype(F32), route_w[...])
    lane = iota((SLOTS, LANES), 1)
    gap = jnp.sum(
        jnp.where(lane == own, logits, 0.0)
        - jnp.where(lane == cols[:, 3:4].astype(jnp.int32), logits, 0.0),
        axis=1,
        keepdims=True,
    )
    gate = sigmoid(gap - (cols[:, 0:1] + cols[:, 1:2] + cols[:, 2:3]))
    mask = ((lane // RANK) == cols[:, 4:5].astype(jnp.int32)).astype(F32)
    d_out = (cot * gate).astype(BF)
    for copy in copies:
        copy.wait()

    a_gu = wall.a_gate_up()
    proj = dot(tokens, a_gu)
    ranks_in = [(proj[:, j * RANKS : (j + 1) * RANKS] * mask).astype(BF) for j in range(2)]
    d_ranks_down = (dot_nt(d_out, wall.b_down()) * mask).astype(BF)
    fo_acc[...] = jnp.zeros_like(fo_acc)
    dt_acc[...] = jnp.zeros_like(dt_acc)
    pd_acc[...] = jnp.zeros_like(pd_acc)
    dug_acc[...] = jnp.zeros_like(dug_acc)
    blocks = CHUNK // LANES
    srcs = max(1, CHUNK // wall.ff)
    gb_at = AGU_BLOCKS * wall.rows
    ad_at = gb_at + GU_BLOCKS * wall.low
    bd_at = ad_at + wall.ff

    def step(f, carry):
        j = f * blocks
        wg = wall.gate_up(j, blocks)
        wu = wall.gate_up(j + GU_BLOCKS // 2, blocks)
        bg = wall.b_gate_up(j, blocks)
        bu = wall.b_gate_up(j + GU_BLOCKS // 2, blocks)
        wd = wall.down(f * srcs, srcs)
        ad = wall.a_down(f * srcs, srcs)
        g = dot(tokens, wg) + dot(ranks_in[0], bg)
        u = dot(tokens, wu) + dot(ranks_in[1], bu)
        d_hidden = dot_nt(d_out, wd) + dot_nt(d_ranks_down, ad)
        sg = sigmoid(g)
        act = g * sg
        hidden = (act * u).astype(BF)
        d_gate = (d_hidden * u * (sg * (1.0 + g * (1.0 - sg)))).astype(BF)
        d_up = (d_hidden * act).astype(BF)
        fo_acc[...] += dot(hidden, wd)
        pd_acc[...] += dot(hidden, ad)
        dt_acc[...] += dot_nt(d_gate, wg) + dot_nt(d_up, wu)
        dug_acc[:, :RANKS] += dot_nt(d_gate, bg)
        dug_acc[:, RANKS:] += dot_nt(d_up, bu)
        for k, (rank, grad) in enumerate(((ranks_in[0], d_gate), (ranks_in[1], d_up))):
            part = dot_tn(rank, grad)
            for i in range(blocks):
                at = gb_at + (j + k * (GU_BLOCKS // 2) + i) * wall.low
                rows = pl.ds(at if isinstance(at, int) else pl.multiple_of(at, 8), wall.low)
                one = part[:, i * LANES : (i + 1) * LANES].reshape(n_src, wall.low, LANES)
                grads[:, rows, :] = one
        part = dot_tn(hidden, d_ranks_down).reshape(srcs, wall.ff, LANES)
        grads[pl.ds(f * srcs, srcs), ad_at : ad_at + wall.ff, :] = part
        return carry

    if wall.low % 8:
        for f in range(FF // CHUNK):
            step(f, 0)
    else:
        lax.fori_loop(0, FF // CHUNK, step, 0)
    ranks_down = (pd_acc[...] * mask).astype(BF)
    result = (fo_acc[...] + dot(ranks_down, wall.b_down())).astype(BF)
    along = jnp.sum(cot * result.astype(F32), axis=1, keepdims=True)
    parts = three_parts(along)
    along = jnp.where(lane == 0, parts[0], jnp.where(lane == 1, parts[1], 0.0))
    along = jnp.where(lane == 2, parts[2], along).astype(BF)
    eye = (iota((CAP, LANES), 0) == iota((CAP, LANES), 1)).astype(F32).astype(BF)
    fo[...] = result.reshape(FFN_EXPERTS, CAP, D)
    for r in range(FFN_EXPERTS):
        side = dot_tn(along[r * CAP : (r + 1) * CAP], eye)[:SIDE]
        dtin[r, BLOCKS * CAP :, :] = side.astype(BF)
    part = dot_tn(ranks_down, d_out)
    for i in range(DOWN_BLOCKS):
        grads[:, bd_at + i * wall.low : bd_at + (i + 1) * wall.low, :] = part[
            :, i * LANES : (i + 1) * LANES
        ].reshape(n_src, wall.low, LANES)
    d_ranks = [(dug_acc[:, k * RANKS : (k + 1) * RANKS] * mask).astype(BF) for k in range(2)]
    both = lanes_cat(d_ranks)
    d_tokens = (dt_acc[...] + dot_nt(both, a_gu)).astype(BF)
    for r in range(FFN_EXPERTS):
        put_packet(dtin, r, d_tokens[r * CAP : (r + 1) * CAP])
    part = dot_tn(tokens, both)
    for i in range(AGU_BLOCKS):
        grads[:, i * wall.rows : (i + 1) * wall.rows, :] = part[
            :, i * LANES : (i + 1) * LANES
        ].reshape(n_src, wall.rows, LANES)
    if carried:
        earlier.wait()
        split_sums(grads, more[0], meta[n_src + 1], kept, away)


def split_sums(grads, before, core, keep, away):
    for i in range(keep.shape[0]):
        mine, theirs = pl.ds(2 * i + core, 1), pl.ds(2 * i + 1 - core, 1)
        keep[i : i + 1] = grads[mine] + before[mine]
        away[i : i + 1] = (grads[theirs] + before[theirs]).astype(BF)


def halves_body(meta, kept, got, keep, away):
    half = keep.shape[0]
    mine, theirs = pl.ds(meta[0] * half, half), pl.ds((1 - meta[0]) * half, half)
    keep[...] = kept[mine] + got[mine].astype(F32)
    away[...] = (kept[theirs] + got[theirs].astype(F32)).astype(BF)


def attn_backward_body(micro, n_src, carried, meta, hid, cot, resid_ref, qkv, attended, ranks, lse,
                       dtin, tok, sid_col, gain_a, gain_m, route_w, consts, cos_ref, sin_ref,
                       *refs):
    if carried:
        before, refs = refs[0], refs[1:]
    pieces = refs[:n_src]
    base, gates, grad_in, *refs = refs[n_src:]
    if carried:
        kept, away, *refs = refs
        *refs, grads = refs
        wall_ref, sems, dqkv, *more = refs
    else:
        grads, wall_ref, sems, dqkv = refs
    copies = load_wall(pieces, wall_ref, sems, meta, 0)
    if carried:
        earlier = pltpu.make_async_copy(before, more[0], more[1])
        earlier.start()
    wall = AttnWall(wall_ref, n_src)
    at_id = n_src + 1 + micro
    at_span = n_src + 3 + 4 * micro
    mask = rank_mask(meta[at_id])
    resid = resid_ref[...]
    dy = cot[0, 0].astype(F32)
    scale_m = lax.rsqrt(jnp.mean(resid * resid, axis=-1, keepdims=True) + EPS)
    gain = gain_m[...]
    normed = resid * scale_m * gain
    lowered = normed.astype(BF).astype(F32)
    weights = route_w[...]
    scores = exact_dot(lowered, weights)
    token = tok[0]
    lane = iota((SEQ, LANES), 1)
    route = [token[:, 16 + k : 17 + k].astype(jnp.int32) for k in range(2)]
    logits = scores + token
    chosen = [
        jnp.sum(jnp.where(lane == route[k], logits, 0.0), axis=1, keepdims=True) for k in range(2)
    ]
    gate = [sigmoid(chosen[k] - chosen[1 - k]) for k in range(2)]
    keep = [sigmoid(scores[:, 12 + j : 13 + j]) for j in range(2)]
    slot = iota((SEQ, SLOTS), 1)
    hits = [(slot == sid_col[0][:, k : k + 1]).astype(F32).astype(BF) for k in range(2)]
    spread = iota((SEQ, FFN_EXPERTS * LANES), 1)
    spread = jnp.where(spread % LANES < CAP, spread // LANES * CAP + spread % LANES, -2)
    side = lanes_cat([dtin[e, BLOCKS * CAP :, :] for e in range(FFN_EXPERTS)])
    along = []
    for k in range(2):
        found = (spread == sid_col[0][:, k : k + 1]).astype(F32).astype(BF)
        parts = dot_nt(found, side)
        along.append(parts[:, 0:1] + parts[:, 1:2] + parts[:, 2:3])
    value = [consts[j : j + 1, :] for j in range(2)]
    is_copy = [(route[k] == FFN_EXPERTS + 1).astype(F32) for k in range(2)]
    is_const = [
        [(route[k] == FFN_EXPERTS + 2 + j).astype(F32) for j in range(2)] for k in range(2)
    ]
    share = sum(
        gate[k] * (is_copy[k] + is_const[k][0] * keep[0] + is_const[k][1] * keep[1])
        for k in range(2)
    )
    named = [gate[0] * is_const[0][j] + gate[1] * is_const[1][j] for j in range(2)]
    out = resid + share * normed
    out = out + (named[0] * (1.0 - keep[0])) * value[0] + (named[1] * (1.0 - keep[1])) * value[1]
    base[...] = out
    gates[...] = jnp.where(lane == 0, gate[0], jnp.where(lane == 1, gate[1], 0.0))
    dy_normed = jnp.sum(dy * normed, axis=1, keepdims=True)
    dy_value = [jnp.sum(dy * value[j], axis=1, keepdims=True) for j in range(2)]
    d_gate = []
    for k in range(2):
        one = along[k] + is_copy[k] * dy_normed
        for j in range(2):
            one = one + is_const[k][j] * (keep[j] * dy_normed + (1.0 - keep[j]) * dy_value[j])
        d_gate.append(one)
    centre = gate[0] * d_gate[0] + gate[1] * d_gate[1]
    d_logits = jnp.zeros((SEQ, LANES), F32)
    for k in range(2):
        d_logits = d_logits + jnp.where(lane == route[k], gate[k] * (d_gate[k] - centre), 0.0)
    for j in range(2):
        d_keep = named[j] * (dy_normed - dy_value[j])
        d_logits = d_logits + jnp.where(
            lane == 12 + j, d_keep * keep[j] * (1.0 - keep[j]), 0.0
        )
    d_normed = share * dy + exact_dot_nt(d_logits, weights)
    d_normed = d_normed + dot(hits[0] + hits[1], packet_rows(dtin))
    scaled = gain * d_normed
    d_resid = (
        dy
        + scale_m * scaled
        - resid * (scale_m * scale_m * scale_m) * jnp.mean(scaled * resid, axis=-1, keepdims=True)
    )
    d_branch = d_resid.astype(BF)
    for copy in copies:
        copy.wait()
    d_ranks_out = (dot_nt(d_branch, wall.b_out()) * mask).astype(BF)
    d_mixed = (dot_nt(d_branch, wall.w_out()) + dot_nt(d_ranks_out, wall.a_out())).astype(BF)
    a_rows, b_rows = wall.rows, wall.low
    gb_at = AQKV_BLOCKS * a_rows
    ao_at = gb_at + QKV_BLOCKS * b_rows
    bo_at = ao_at + a_rows
    part = dot_tn(ranks[:, 3 * RANKS :], d_branch)
    for i in range(OUT_BLOCKS):
        grads[:, bo_at + i * b_rows : bo_at + (i + 1) * b_rows, :] = part[
            :, i * LANES : (i + 1) * LANES
        ].reshape(n_src, b_rows, LANES)
    grads[:, ao_at : ao_at + a_rows, :] = dot_tn(attended[...], d_ranks_out).reshape(
        n_src, a_rows, LANES
    )
    ok = allowed_bias(meta, at_span)
    cos, sin = cos_ref[...], -sin_ref[...]
    inv = 1.0 / math.sqrt(HEAD)
    for pair in range(6):
        query = split_heads(qkv[:, pair * LANES : (pair + 1) * LANES])
        key = qkv[:, (6 + pair) * LANES : (7 + pair) * LANES]
        val = qkv[:, (12 + pair) * LANES : (13 + pair) * LANES]
        d_heads = split_heads(d_mixed[:, pair * LANES : (pair + 1) * LANES])
        sc = jnp.where(ok, dot_nt(query, key) * inv, NEG)
        probs = jnp.exp(sc - lse[:, pair : pair + 1])
        d_probs = dot_nt(d_heads, val)
        row_dot = jnp.sum(probs * d_probs, axis=-1, keepdims=True)
        d_scores = (probs * (d_probs - row_dot)).astype(BF)
        d_query = join_heads(dot(d_scores, key)) * inv
        d_key = dot_tn(d_scores, query) * inv
        d_value = dot_tn(probs.astype(BF), d_heads)
        dqkv[:, pair * LANES : (pair + 1) * LANES] = turn(d_query, cos, sin).astype(BF)
        dqkv[:, (6 + pair) * LANES : (7 + pair) * LANES] = turn(d_key, cos, sin).astype(BF)
        dqkv[:, (12 + pair) * LANES : (13 + pair) * LANES] = d_value.astype(BF)
    hidden = hid[0, 0].astype(F32)
    scale = lax.rsqrt(jnp.mean(hidden * hidden, axis=-1, keepdims=True) + EPS)
    first = gain_a[...]
    normed_low = (hidden * scale * first).astype(BF)
    d_in = jnp.zeros((SEQ, D), F32)
    d_ranks = []
    for j in range(3):
        part = dqkv[:, j * D : (j + 1) * D]
        d_ranks.append((dot_nt(part, wall.b_qkv(j * 6, 6)) * mask).astype(BF))
        d_in = d_in + dot_nt(part, wall.qkv(j * 6, 6))
        gb = dot_tn(ranks[:, j * RANKS : (j + 1) * RANKS], part)
        for i in range(6):
            at = gb_at + (j * 6 + i) * b_rows
            grads[:, at : at + b_rows, :] = gb[:, i * LANES : (i + 1) * LANES].reshape(
                n_src, b_rows, LANES
            )
    ranks_all = lanes_cat(d_ranks)
    d_in = d_in + dot_nt(ranks_all, wall.a_qkv())
    ga = dot_tn(normed_low, ranks_all)
    for i in range(3):
        grads[:, i * a_rows : (i + 1) * a_rows, :] = ga[:, i * LANES : (i + 1) * LANES].reshape(
            n_src, a_rows, LANES
        )
    scaled = first * d_in
    grad_in[...] = (
        d_resid
        + scale * scaled
        - hidden * (scale * scale * scale) * jnp.mean(scaled * hidden, axis=-1, keepdims=True)
    )
    if carried:
        earlier.wait()
        split_sums(grads, more[0], meta[n_src], kept, away)


def output_body(micros, meta, *refs):
    sid_col, outs = refs[3 * micros], refs[3 * micros + 1 :]
    slot = iota((SEQ, SLOTS), 1)
    for micro in range(micros):
        total, gates, fo = (refs[3 * micro + i][...] for i in range(3))
        for k in range(2):
            hits = (slot == sid_col[micro, :, k : k + 1]).astype(F32).astype(BF)
            total = total + gates[:, k : k + 1] * dot(hits, fo.reshape(SLOTS, D))
        outs[micro][...] = total.astype(BF)


def flip(values, axis, bit, size):
    return lax.ppermute(values, axis, [(i, i ^ bit) for i in range(size)])


def later(values, others):
    return lax.optimization_barrier((values, others))[0]


def bits(size):
    return [1 << i for i in range(size.bit_length() - 1)]


def next_half(kept, got, side):
    half = (kept.shape[0] // 2,) + kept.shape[1:]
    return call(
        halves_body,
        side.reshape(1).astype(jnp.int32),
        (kept, got),
        [whole(kept.shape), whole(got.shape)],
        [shape(half, F32), shape(half, BF)],
        us=2,
    )


def sums_scratch(dims):
    return [pltpu.VMEM(dims, F32), pltpu.SemaphoreType.DMA, pltpu.VMEM(dims, F32)]


def body(members, hidden_in, prev_logits, routes, adapter_ids, image_spans, cotangent, gain_attn,
         gain_moe, router_weight, const_gate, const_value, w_qkv, w_out, a_qkv, b_qkv, a_out, b_out,
         w_gate_up, w_down, a_gate_up, b_gate_up, a_down, b_down):
    rest = lax.axis_size("y")
    peers = lax.axis_size("z")
    n_src = rest * members * 2
    micros = hidden_in.shape[0]
    y, x, c, z = (lax.axis_index(name) for name in ("y", "x", "c", "z"))
    place = (y * members + x) * 2 + c

    attn_rows = (QKV_BLOCKS + AQKV_BLOCKS + OUT_BLOCKS + 1) * (D // n_src) + (
        QKV_BLOCKS + OUT_BLOCKS
    ) * (RANKS // n_src)
    expert_rows = (
        (GU_BLOCKS + AGU_BLOCKS) * (D // n_src)
        + (DOWN_BLOCKS + 1) * (FF // n_src)
        + (GU_BLOCKS + DOWN_BLOCKS) * (RANKS // n_src)
    )
    none = jnp.zeros((1,), jnp.int32)
    args = (w_qkv, a_qkv, w_out, a_out, b_qkv, b_out)
    (attn_own,) = call(
        pack_attn_body,
        none,
        args,
        [whole(a.shape) for a in args],
        [shape((attn_rows, LANES), BF)],
        us=2,
    )
    tok = jnp.concatenate(
        [
            prev_logits[:, 0],
            jnp.zeros((micros, SEQ, 4), F32),
            routes[:, 0].astype(F32),
            jnp.zeros((micros, SEQ, LANES - 18), F32),
        ],
        axis=2,
    )
    route_w = jnp.concatenate(
        [router_weight, const_gate, jnp.zeros((D, LANES - 14), F32)], axis=1
    )
    half = HEAD // 2
    freqs = jnp.exp(jnp.arange(half, dtype=F32) * (-2.0 * math.log(10000.0) / HEAD))
    angles = jnp.arange(SEQ, dtype=F32)[:, None] * freqs[None, :]
    cos = jnp.tile(jnp.cos(angles), (1, 4))
    sin = jnp.sin(angles)
    sin = jnp.tile(jnp.concatenate([-sin, sin], axis=1), (1, 2))
    gain_a = gain_attn.reshape(1, D)
    gain_m = gain_moe.reshape(1, D)

    packet = shape((FFN_EXPERTS, CAP, D), BF)
    wide_packet = shape((FFN_EXPERTS, WIDE, LANES), BF)
    dy_send, sid_row, sid_col = call(
        functools.partial(slots_body, micros),
        adapter_ids.reshape(-1),
        (tok, cotangent),
        [whole(tok.shape), whole(cotangent.shape)],
        [
            shape((FFN_EXPERTS, micros * WIDE, LANES), BF),
            shape((micros, 8, SEQ), jnp.int32),
            shape((micros, SEQ, 8), jnp.int32),
        ],
        us=4,
        after=(attn_own,),
    )

    args = (w_gate_up, a_gate_up, w_down, a_down, b_gate_up, b_down)
    expert_own = call(
        functools.partial(pack_experts_body, members),
        x.reshape(1).astype(jnp.int32),
        args,
        [whole(a.shape) for a in args],
        [shape((expert_rows, LANES), BF)] * members,
        us=4,
        after=(sid_row,),
    )

    attn_pieces = [(attn_own, 0)]
    for bit in bits(members):
        attn_pieces += [(flip(v, "x", bit, members), m ^ (bit * 2)) for v, m in attn_pieces]
    for bit in bits(rest):
        way = bit * members * 2
        beside = flip(attn_own, "y", bit, rest)
        attn_pieces += [(beside, way)] + [
            (flip(later(v, (sid_row, beside)), "y", bit, rest), m ^ way)
            for v, m in attn_pieces[1:]
        ]
    attn_near, attn_far = attn_pieces[1][0], attn_pieces[-1][0]
    attn_beside = attn_pieces[members][0]
    attn_pieces += [
        (flip(v if m == 0 or v is attn_far else later(v, attn_far), "c", 1, 2), m ^ 1)
        for v, m in attn_pieces
    ]
    attn_bufs = [v for v, m in attn_pieces]
    meta_attn = jnp.concatenate(
        [
            place ^ jnp.array([m for v, m in attn_pieces], jnp.int32),
            c.reshape(1),
            adapter_ids.reshape(-1),
            image_spans.reshape(-1),
        ]
    ).astype(jnp.int32)

    group = ("z", "x") if members > 1 else "z"

    def trade(values):
        return lax.all_to_all(values, group, 0, 0, tiled=True)

    expert_pieces = [(expert_own[0], 0)]
    for rel in range(1, members):
        pairs = [(i, i ^ rel) for i in range(members)]
        away = later(expert_own[rel], attn_near)
        expert_pieces.append((lax.ppermute(away, "x", pairs), rel * 2))
    first = bits(rest)[0]
    own = later(expert_own[0], attn_beside)
    beside = (flip(own, "y", first, rest), first * members * 2)
    near = [[v for v, m in expert_pieces[1:]] + [beside[0]]]

    dy_got = trade(dy_send)
    saved, tin = [], []
    for micro in range(micros):
        args = (hidden_in, cos, sin, gain_a, gain_m, sid_row, *attn_bufs)
        specs = [
            one_micro((1, SEQ, D), micro),
            whole(cos.shape),
            whole(sin.shape),
            whole(gain_a.shape),
            whole(gain_m.shape),
            one_micro((8, SEQ), micro),
        ] + [ANYWHERE] * n_src
        saved.append(
            call(
                functools.partial(attn_forward_body, micro, n_src),
                meta_attn,
                args,
                specs,
                [
                    shape((SEQ, 3 * D), BF),
                    shape((SEQ, D), BF),
                    shape((SEQ, 4 * RANKS), BF),
                    shape((SEQ, D), F32),
                    shape((2 * SEQ, 8), F32),
                    packet,
                ],
                [
                    pltpu.VMEM((n_src, attn_rows, LANES), BF),
                    pltpu.SemaphoreType.DMA((n_src,)),
                ],
                us=FORWARD_HINT,
                after=tuple(near[micro]) if micro < len(near) else (),
            )
        )
        if micro == 0:
            for bit in bits(rest):
                relay = expert_pieces[1:] if bit == first else expert_pieces
                more = [
                    (flip(v, "y", bit, rest), m ^ (bit * members * 2)) for v, m in relay
                ]
                expert_pieces += ([beside] if bit == first else []) + more
        send = saved[micro][5]
        tin.append(trade(send if micro == 0 else later(send, expert_pieces[-1][0])))
    expert_pieces += [
        (flip(later(v, saved[-1][4]), "c", 1, 2), m ^ 1) for v, m in expert_pieces
    ]
    expert_bufs = [v for v, m in expert_pieces]
    meta_expert = jnp.concatenate(
        [
            place ^ jnp.array([m for v, m in expert_pieces], jnp.int32),
            (z * members + x).reshape(1),
            c.reshape(1),
        ]
    ).astype(jnp.int32)

    expert_grad_rows = (
        AGU_BLOCKS * (D // n_src)
        + (GU_BLOCKS + DOWN_BLOCKS) * (RANKS // n_src)
        + FF // n_src
    )
    grads_e = None
    fo_send, dtin = [], []
    for micro in range(micros):
        carried = grads_e is not None
        args = (tin[micro], dy_got, route_w)
        specs = [whole(a.shape) for a in args]
        specs[1] = pl.BlockSpec(
            (FFN_EXPERTS, WIDE, LANES), lambda i, meta, micro=micro: (0, micro, 0)
        )
        if carried:
            args += tuple(grads_e)
            specs.append(ANYWHERE)
        specs += [ANYWHERE] * n_src
        sums = (n_src, expert_grad_rows, LANES)
        halves = (n_src // 2, expert_grad_rows, LANES)
        fo, d_tokens, *grads_e = call(
            functools.partial(expert_body, n_src, carried),
            meta_expert,
            args + tuple(expert_bufs),
            specs,
            [
                packet,
                wide_packet,
            ]
            + ([shape(halves, F32), shape(halves, BF)] if carried else [shape(sums, F32)]),
            [
                pltpu.VMEM((n_src, expert_rows, LANES), BF),
                pltpu.SemaphoreType.DMA((n_src,)),
                pltpu.VMEM((SLOTS, D), F32),
                pltpu.VMEM((SLOTS, D), F32),
                pltpu.VMEM((SLOTS, RANKS), F32),
                pltpu.VMEM((SLOTS, 2 * RANKS), F32),
            ]
            + (sums_scratch(sums) if carried else []),
            us=31,
        )
        fo_send.append(fo)
        dtin.append(trade(d_tokens))

    attn_grad_rows = (AQKV_BLOCKS + 1) * (D // n_src) + (QKV_BLOCKS + OUT_BLOCKS) * (
        RANKS // n_src
    )
    grads_a = None
    mixed, grad_rows = [], []
    for micro in range(micros):
        carried = grads_a is not None
        qkv, attended, ranks, resid, lse = saved[micro][:5]
        args = (hidden_in, cotangent, resid, qkv, attended, ranks, lse, dtin[micro], tok, sid_col,
                gain_a, gain_m, route_w, const_value, cos, sin)
        specs = [whole(a.shape) for a in args]
        specs[0] = one_micro((1, SEQ, D), micro)
        specs[1] = one_micro((1, SEQ, D), micro)
        specs[8] = one_micro((SEQ, LANES), micro)
        specs[9] = one_micro((SEQ, 8), micro)
        if carried:
            args += tuple(grads_a)
            specs.append(ANYWHERE)
        specs += [ANYWHERE] * n_src
        sums = (n_src, attn_grad_rows, LANES)
        halves = (n_src // 2, attn_grad_rows, LANES)
        base, gates, grad_in, *grads_a = call(
            functools.partial(attn_backward_body, micro, n_src, carried),
            meta_attn,
            args + tuple(attn_bufs),
            specs,
            [
                shape((SEQ, D), F32),
                shape((SEQ, LANES), F32),
                shape((SEQ, D), F32),
            ]
            + ([shape(halves, F32), shape(halves, BF)] if carried else [shape(sums, F32)]),
            [
                pltpu.VMEM((n_src, attn_rows, LANES), BF),
                pltpu.SemaphoreType.DMA((n_src,)),
                pltpu.VMEM((SEQ, 3 * D), BF),
            ]
            + (sums_scratch(sums) if carried else []),
            us=19,
            after=(away,) if carried else (),
        )
        grad_rows.append(grad_in)
        mixed.append((base, gates, trade(later(fo_send[micro], base))))
        if not carried:
            kept, away = later(grads_e, base)
            got = flip(away, "c", 1, 2)
            for bit in reversed(bits(rest)):
                kept, away = next_half(kept, got, (y // bit) % 2)
                got = flip(away, "y", bit, rest)
            total = kept + got.astype(F32)
            held = (mixed[0][2], total)
    args = tuple(v for parts in mixed for v in parts) + (sid_col,)
    block_rows = call(
        functools.partial(output_body, micros),
        none,
        args,
        [whole(a.shape) for a in args],
        [shape((SEQ, D), BF)] * micros,
        us=5,
    )
    owned = lax.dynamic_index_in_dim(total, x, 0, keepdims=True)
    for rel in range(1, members):
        away = lax.dynamic_index_in_dim(total, x ^ rel, 0, keepdims=True).astype(BF)
        got = lax.ppermute(away, "x", [(i, i ^ rel) for i in range(members)])
        owned = jnp.concatenate([owned, got.astype(F32)], axis=0)
    if members > 1:
        owned = owned[x ^ jnp.arange(members)]

    def blocks_of(values, row, count, height):
        part = values[:, row : row + count * height].reshape(-1, count, height, LANES)
        return jnp.moveaxis(part, 1, 2).reshape(-1, height, count * LANES)

    rows, low, ff = D // n_src, RANKS // n_src, FF // n_src
    at = 0
    grad_agu = blocks_of(owned, at, AGU_BLOCKS, rows)
    at += AGU_BLOCKS * rows
    grad_bgu = blocks_of(owned, at, GU_BLOCKS, low)
    at += GU_BLOCKS * low
    grad_ad = blocks_of(owned, at, 1, ff)
    at += ff
    grad_bd = blocks_of(owned, at, DOWN_BLOCKS, low)

    kept, away = grads_a
    got = flip(away, "c", 1, 2)
    for axis, place_on, size in (("y", y, rest), ("x", x, members)):
        for bit in reversed(bits(size)):
            kept, away = next_half(kept, got, (place_on // bit) % 2)
            got = flip(away, axis, bit, size)
        if axis == "y":
            kept = later(kept, held)
    total = kept + got.astype(F32)
    for bit in bits(peers):
        sent = total.astype(BF)
        total = sent.astype(F32) + flip(sent, "z", bit, peers).astype(F32)
    at = 0
    grad_aq = blocks_of(total, at, AQKV_BLOCKS, rows)[0]
    at += AQKV_BLOCKS * rows
    grad_bq = blocks_of(total, at, QKV_BLOCKS, low)[0]
    at += QKV_BLOCKS * low
    grad_ao = blocks_of(total, at, 1, rows)[0]
    at += rows
    grad_bo = blocks_of(total, at, OUT_BLOCKS, low)[0]

    return (jnp.stack(block_rows)[:, None], jnp.stack(grad_rows)[:, None], grad_aq, grad_bq,
            grad_ao, grad_bo, grad_agu, grad_bgu, grad_ad, grad_bd)


def solution(mesh):
    dp, expert = mesh.shape["dp"], mesh.shape["expert"]
    members = FFN_EXPERTS // expert
    fine = Mesh(
        mesh.devices.reshape(dp // (2 * members), members, 2, expert), ("y", "x", "c", "z")
    )
    owners = ("y", "x", "c")
    seqs = ("y", "x", "c", "z")
    tokens = P(None, seqs, None, None)
    rows = P(owners, None)
    expert_rows = P("z", owners, None)
    in_specs = (
        (tokens, tokens, tokens, P(None, seqs), tokens, tokens)
        + (P(),) * 5
        + (rows,) * 6
        + (expert_rows,) * 6
    )
    out_specs = (tokens, tokens) + (rows,) * 4 + (expert_rows,) * 4
    return jax.shard_map(
        functools.partial(body, members),
        mesh=fine,
        in_specs=in_specs,
        out_specs=out_specs,
        check_vma=False,
    )
```
